32 devices in a mesh: rows: 8 (over y, x, core), heads: 4 (over z).
Axes of the slice: x: 2, y: 2, z: 4, core: 2. Of those that a mesh axis runs over, the one named last changes fastest.
Arguments:
- tokens: bfloat16 [32768, 768], P(('rows', 'heads')), may hold values from -6 to 6
- block_kind: int32 [64], P('rows'), may hold values from 0 to 2, as said below
- query_weight: bfloat16 [768, 768], P('rows', 'heads'), may hold values from -0.4375 to 0.4375
- key_weight: bfloat16 [768, 768], P('rows', 'heads'), may hold values from -0.21875 to 0.21875
- value_weight: bfloat16 [768, 768], P('rows', 'heads'), may hold values from -0.21875 to 0.21875
- query_bias: bfloat16 [768], replicated, may hold values from -4 to 4
- value_bias: bfloat16 [768], replicated, may hold values from -2 to 2
- output_weight: bfloat16 [768, 768], P(('rows', 'heads')), may hold values from -0.875 to 0.875
- output_bias: bfloat16 [768], replicated, may hold values from -2 to 2
- first_gain: bfloat16 [768], replicated, may hold values from 0.5 to 1.5
- first_shift: bfloat16 [768], replicated, may hold values from -2 to 2
- inner_weight: bfloat16 [768, 3072], P(('rows', 'heads')), may hold values from -0.21875 to 0.21875
- inner_bias: bfloat16 [3072], replicated, may hold values from -2 to 2
- outer_weight: bfloat16 [3072, 768], P(('rows', 'heads')), may hold values from -0.109375 to 0.109375
- outer_bias: bfloat16 [768], replicated, may hold values from -2 to 2
- second_gain: bfloat16 [768], replicated, may hold values from 0.5 to 1.5
- second_shift: bfloat16 [768], replicated, may hold values from -2 to 2
- cotangent: bfloat16 [32768, 768], P(('rows', 'heads')), may hold values from -6 to 6
Outputs:
- layer_out: bfloat16 [32768, 768], P(('rows', 'heads'))
- tokens_grad: float32 [32768, 768], P(('rows', 'heads'))
- query_weight_grad: float32 [768, 768], P('rows', 'heads')
- key_weight_grad: float32 [768, 768], P('rows', 'heads')
- value_weight_grad: float32 [768, 768], P('rows', 'heads')
- query_bias_grad: float32 [768], replicated
- value_bias_grad: float32 [768], replicated
- output_weight_grad: float32 [768, 768], P(('rows', 'heads'))
- output_bias_grad: float32 [768], replicated
- first_gain_grad: float32 [768], replicated
- first_shift_grad: float32 [768], replicated
- inner_weight_grad: float32 [768, 3072], P(('rows', 'heads'))
- inner_bias_grad: float32 [3072], replicated
- outer_weight_grad: float32 [3072, 768], P(('rows', 'heads'))
- outer_bias_grad: float32 [768], replicated
- second_gain_grad: float32 [768], replicated
- second_shift_grad: float32 [768], replicated
The draws below stay inside these ranges and needn't reach their ends.
Inputs may be any that keep to these rules, and one draw needn't show every extreme that they name: `block_kind`: kind of each block of 512 tokens: 0 holds one sequence of 512 tokens, 1 holds four sequences of 128 tokens, 2 holds padding. Of the 8 blocks of one index of rows the padding ones come last, at most 4 of them.
All inputs are finite; a program needn't handle non-finite values.
Results may differ from the reference program's by a relative error of at most 0.015.
The reference program's roundings to bfloat16 on the way count: a program that leaves them out, or rounds other values in their place, can miss the bound.
Values may be sent and summed in bfloat16 or wider, within the bound.
No kernel may reach another device: no remote copies, remote signals or barrier semaphores. Data moves between devices by JAX's collectives and lax.ppermute only.
A program may use at most 192 MiB of HBM per device.

```python
import jax
import jax.numpy as jnp
from jax import lax

HEADS = 12
HEAD_DIM = 64
D = 768
FF = 3072
BLOCK = 512
BLK_GRP = 8
GROUP = 4096
TOKENS = 32768
N_ROWS = 8


def draw_block_kind(key, part):
    key_count, key_sort, key_full = jax.random.split(key, 3)
    counts = jax.random.randint(key_count, (N_ROWS,), BLK_GRP // 2, BLK_GRP + 1)
    full_group = jax.random.randint(key_full, (), 0, N_ROWS)
    counts = jnp.where(jnp.arange(N_ROWS) == full_group, BLK_GRP, counts)
    seq_sorts = jax.random.randint(key_sort, (N_ROWS, BLK_GRP), 0, 2)
    places = jnp.arange(BLK_GRP)[None, :]
    filled = jnp.where(places < counts[:, None], seq_sorts, 2)
    return filled.reshape(N_ROWS * BLK_GRP).astype(jnp.int32)


def levels(own_key, dims, pieces, smallest, high):
    gain = 1.0
    for axis_at, blocks in pieces:
        steps = jax.random.uniform(jax.random.fold_in(jax.random.fold_in(own_key, 6), axis_at), (blocks,), jnp.float32, smallest / len(pieces), high / len(pieces))
        gain = gain * jnp.repeat(jnp.exp(steps), dims[axis_at] // blocks).reshape((-1,) + (1,) * (len(dims) - 1 - axis_at))
    return gain


def normal_values(own_key, dims, deviation, limit, pieces=(), kind=jnp.bfloat16):
    array = jax.random.normal(own_key, dims, jnp.float32) * deviation
    if len(pieces) > 0:
        array = levels(own_key, dims, pieces, -0.22, 0.18) * array
    return jnp.clip(array, min=-limit, max=limit).astype(kind)


def setup_inputs(seed: int = 0) -> dict:
    seeds = jax.random.split(jax.random.key(seed), 19)
    return {
        "tokens": normal_values(seeds[0], (TOKENS, D), 1.0, 6.0, ((0, 32),)),
        "block_kind": draw_block_kind(jax.random.fold_in(seeds[18], 71), 0),
        "query_weight": normal_values(seeds[2], (D, D), (D // 4) ** -0.5, 0.4375, ((0, 8), (1, 4))),
        "key_weight": normal_values(seeds[3], (D, D), D ** -0.5, 0.21875, ((0, 8), (1, 4))),
        "value_weight": normal_values(seeds[4], (D, D), D ** -0.5, 0.21875, ((0, 8), (1, 4))),
        "query_bias": normal_values(seeds[5], (D,), 1.0, 4.0),
        "value_bias": normal_values(seeds[6], (D,), 0.5, 2.0),
        "output_weight": normal_values(seeds[7], (D, D), (D // 16) ** -0.5, 0.875, ((0, 32),)),
        "output_bias": normal_values(seeds[8], (D,), 0.5, 2.0),
        "first_gain": jnp.clip(1.0 + 0.1 * jax.random.normal(seeds[9], (D,), jnp.float32), 0.5, 1.5).astype(jnp.bfloat16),
        "first_shift": normal_values(seeds[10], (D,), 0.5, 2.0),
        "inner_weight": normal_values(seeds[11], (D, FF), D ** -0.5, 0.21875, ((0, 32),)),
        "inner_bias": normal_values(seeds[12], (FF,), 0.5, 2.0),
        "outer_weight": normal_values(seeds[13], (FF, D), FF ** -0.5, 0.109375, ((0, 32),)),
        "outer_bias": normal_values(seeds[14], (D,), 0.5, 2.0),
        "second_gain": jnp.clip(1.0 + 0.1 * jax.random.normal(seeds[15], (D,), jnp.float32), 0.5, 1.5).astype(jnp.bfloat16),
        "second_shift": normal_values(seeds[16], (D,), 0.5, 2.0),
        "cotangent": normal_values(seeds[17], (TOKENS, D), 1.0, 6.0, ((0, 32),)),
    }


EPSILON = 1e-06
SCALE = 0.125
MASKED = -1e+30
HIGHEST = lax.Precision.HIGHEST

@jax.custom_vjp
def low(v):
    return lax.optimization_barrier(v.astype(jnp.bfloat16)).astype(jnp.float32)

@jax.custom_vjp
def low_back(v):
    return v

def low_keep(v):
    return (low(v), None)

def low_pass(kept, grad):
    return (grad,)

def back_keep(v):
    return (v, None)

def back_low(kept, grad):
    return (low(grad),)
low.defvjp(low_keep, low_pass)
low_back.defvjp(back_keep, back_low)

def gelu_exact(inner):
    return 0.5 * inner * (1.0 + lax.erf(inner * 0.7071067811865476))

def norm_apply(hidden_in, norm_gain, norm_shift):
    average = lax.optimization_barrier(jnp.mean(hidden_in, axis=-1, keepdims=True))
    centred = hidden_in - average
    variance = lax.optimization_barrier(jnp.mean(centred * centred, axis=-1, keepdims=True))
    return centred * lax.rsqrt(variance + EPSILON) * norm_gain + norm_shift

def matmul(left, right):
    return jnp.dot(left, right, precision=HIGHEST, preferred_element_type=jnp.float32)

def attend_block(inputs):
    query_blk, key_blk, value_blk, block_type = inputs
    length = query_blk.shape[0]
    places = jnp.arange(length, dtype=jnp.int32)
    labels = jnp.where(block_type == 1, places // (length // 4), 0)
    allowed = labels[:, None] == labels[None, :]
    scores = jnp.einsum('qhd,khd->hqk', query_blk, key_blk, precision=HIGHEST) * SCALE
    scores = jnp.where(allowed[None], low_back(scores), MASKED)
    largest = lax.optimization_barrier(jnp.max(scores, axis=-1, keepdims=True))
    powers = jnp.exp(scores - largest)
    attention = powers / lax.optimization_barrier(jnp.sum(powers, axis=-1, keepdims=True))
    context = jnp.einsum('hqk,khd->qhd', low(attention), value_blk, precision=HIGHEST)
    return low(low_back(context))

def group_forward(group_tokens, group_kinds, params):
    query_weight, key_weight, value_weight, query_bias, value_bias, output_weight, output_bias, first_gain, first_shift, inner_weight, inner_bias, outer_weight, outer_bias, second_gain, second_shift = params
    queries = low(low_back(matmul(group_tokens, query_weight) + query_bias))
    keys_all = low(low_back(matmul(group_tokens, key_weight)))
    values_all = low(low_back(matmul(group_tokens, value_weight) + value_bias))
    row_count = group_tokens.shape[0]

    def blocks(matrix):
        return matrix.reshape(row_count // BLOCK, BLOCK, HEADS, HEAD_DIM)
    context = lax.map(jax.checkpoint(attend_block), (blocks(queries), blocks(keys_all), blocks(values_all), group_kinds))
    context = context.reshape(row_count, D)
    attended = low_back(matmul(context, output_weight) + output_bias)
    first_out = norm_apply(group_tokens + attended, first_gain, first_shift)
    inner_pre = low_back(matmul(low(first_out), inner_weight) + inner_bias)
    hidden_low = low(gelu_exact(inner_pre))
    branch = low_back(matmul(hidden_low, outer_weight) + outer_bias)
    final = norm_apply(first_out + branch, second_gain, second_shift)
    valid = jnp.repeat((group_kinds != 2).astype(jnp.float32), BLOCK)
    return final * valid[:, None]

def reference(tokens, block_kind, query_weight, key_weight, value_weight, query_bias, value_bias, output_weight, output_bias, first_gain, first_shift, inner_weight, inner_bias, outer_weight, outer_bias, second_gain, second_shift, cotangent):
    params = tuple((member.astype(jnp.float32) for member in (query_weight, key_weight, value_weight, query_bias, value_bias, output_weight, output_bias, first_gain, first_shift, inner_weight, inner_bias, outer_weight, outer_bias, second_gain, second_shift)))
    kinds = block_kind.reshape(N_ROWS, BLK_GRP)

    def whole(tokens_float, *weights):
        groups = tokens_float.reshape(N_ROWS, GROUP, D)

        def one_group(carry, inputs):
            return (carry, jax.checkpoint(group_forward)(inputs[0], inputs[1], weights))
        _, outputs = lax.scan(one_group, jnp.zeros((), jnp.float32), (groups, kinds))
        return outputs.reshape(TOKENS, D)
    final, pullback = jax.vjp(whole, tokens.astype(jnp.float32), *params)
    grads = pullback(cotangent.astype(jnp.float32))
    return (final.astype(jnp.bfloat16), grads[0], grads[1], grads[2], grads[3], grads[4], grads[5], grads[6], grads[7], grads[8], grads[9], grads[10], grads[11], grads[12], grads[13], grads[14], grads[15])
```

```python
import functools

import jax
import jax.numpy as jnp
from jax import lax
from jax.experimental import pallas as pl
from jax.experimental.pallas import tpu as pltpu
from jax.sharding import PartitionSpec as P

HEAD_DIM = 64
BLOCK = 512
PARTS = 4
EPSILON = 1e-06
SCALE = 0.125
F32 = jnp.float32
BF16 = jnp.bfloat16


def core_pick(core, first, second):
    return jnp.where(core == 1, second, first)


def exchange(value, stage):
    bits = {"core": (1, 1), "first": (2, 4), "second": (4, 2)}[stage]
    return lax.ppermute(value, "rows", [(i, i ^ bits[i & 1]) for i in range(8)])


def line_gather(piece):
    count = lax.axis_size("heads")
    here = lax.axis_index("heads")
    parts = []
    for shift in range(-(count - 1), count):
        if shift == 0:
            parts.append(piece)
        else:
            pairs = [(i + shift, i) for i in range(count) if 0 <= i + shift < count]
            parts.append(lax.ppermute(piece, "heads", pairs))
    return lax.dynamic_slice_in_dim(jnp.stack(parts), count - 1 - here, count)


def line_scatter(stacked):
    count = lax.axis_size("heads")
    here = lax.axis_index("heads")
    total = lax.dynamic_index_in_dim(stacked, here, keepdims=False).astype(F32)
    for shift in range(-(count - 1), count):
        if shift == 0:
            continue
        pairs = [(i, i + shift) for i in range(count) if 0 <= i + shift < count]
        target = jnp.clip(here + shift, 0, count - 1)
        sent = lax.dynamic_index_in_dim(stacked, target, keepdims=False)
        total = total + lax.ppermute(sent, "heads", pairs).astype(F32)
    return total


def rows_gather(piece):
    if lax.axis_size("rows") != 8:
        return lax.all_gather(piece, "rows", axis=0)
    here = lax.axis_index("rows")
    core = here & 1
    one = exchange(piece, "first")
    two = exchange(piece, "second")
    three = exchange(one, "second")
    mine = (piece, one, two, three)
    other = tuple(exchange(member, "core") for member in mine)
    full = jnp.zeros((8,) + piece.shape, piece.dtype)
    for base, who, members in ((here, core, mine), (here ^ 1, 1 - core, other)):
        masks = (0, core_pick(who, 2, 4), core_pick(who, 4, 2), 6)
        for mask, member in zip(masks, members):
            full = lax.dynamic_update_index_in_dim(full, member, base ^ mask, 0)
    return full


def rows_scatter(term):
    if lax.axis_size("rows") != 8:
        return lax.psum_scatter(term, "rows", scatter_dimension=0)
    here = lax.axis_index("rows")
    core = here & 1

    def slot(index):
        return lax.dynamic_index_in_dim(term, index, keepdims=False)

    own = (0, core_pick(core, 2, 4), core_pick(core, 4, 2), 6)
    away = (0, core_pick(core, 4, 2), core_pick(core, 2, 4), 6)
    sums = []
    for keep, give in zip(own, away):
        got = exchange(slot(here ^ 1 ^ give), "core")
        sums.append(slot(here ^ keep).astype(F32) + got.astype(F32))
    low = [member.astype(BF16) for member in sums]
    one = sums[1] + exchange(low[3], "second").astype(F32)
    zero = sums[0] + exchange(low[2], "second").astype(F32)
    zero = zero + exchange(one.astype(BF16), "first").astype(F32)
    return zero.astype(BF16)


def gather_dense(weight):
    lined = line_gather(weight)
    full = rows_gather(lined.reshape(-1, weight.shape[1]))
    return full.reshape(-1, weight.shape[1])


def scatter_dense(term):
    rows, heads = lax.axis_size("rows"), lax.axis_size("heads")
    part = rows_scatter(term.reshape(rows, term.shape[0] // rows, term.shape[1]))
    return line_scatter(part.reshape(heads, -1, term.shape[1]))


def gather_columns(weights):
    depth, width = weights[0].shape
    lined = line_gather(jnp.concatenate(weights, axis=1))
    heads = lined.shape[0]
    lined = lined.reshape(heads, depth, 3, width).transpose(1, 2, 0, 3)
    full = rows_gather(lined.reshape(depth, 3 * heads * width))
    return full.reshape(-1, 3 * heads * width)


def scatter_columns(term, width):
    rows, heads = lax.axis_size("rows"), lax.axis_size("heads")
    part = rows_scatter(term.reshape(rows, term.shape[0] // rows, term.shape[1]))
    part = part.reshape(-1, 3, heads, width).transpose(2, 0, 1, 3)
    total = line_scatter(part.reshape(heads, -1, 3 * width))
    return tuple(total[:, i * width : (i + 1) * width] for i in range(3))


def head_only(value, which):
    lanes = lax.broadcasted_iota(jnp.int32, value.shape, 1)
    keep = (lanes < HEAD_DIM) if which == 0 else (lanes >= HEAD_DIM)
    return jnp.where(keep, value, jnp.zeros_like(value))


def dot_lanes(left, right):
    return lax.dot_general(left, right, (((1,), (1,)), ((), ())), preferred_element_type=F32)


def dot_rows(left, right):
    return lax.dot_general(left, right, (((0,), (0,)), ((), ())), preferred_element_type=F32)


def dot_plain(left, right):
    return lax.dot_general(left, right, (((1,), (0,)), ((), ())), preferred_element_type=F32)


def forward_span(query_ref, key_ref, value_ref, context_ref, total_ref, start, length):
    span = pl.ds(start, length)
    query = query_ref[span, :] * jnp.asarray(SCALE, BF16)
    key, value = key_ref[span, :], value_ref[span, :]
    flipped = None
    for which in range(2):
        scores = dot_lanes(key, head_only(query, which))
        largest = jnp.max(scores, axis=0, keepdims=True)
        powers = jnp.exp(scores - largest)
        denominator = jnp.sum(powers, axis=0, keepdims=True)
        total_ref[0, 0, which : which + 1, span] = largest + jnp.log(denominator)
        part = dot_rows(head_only(value, which), powers.astype(BF16)) / denominator
        flipped = part if flipped is None else flipped + part
    context_ref[span, :] = flipped.T.astype(BF16)


def backward_span(
    query_ref, key_ref, value_ref, context_ref, grad_ref, total_ref, outs, start, length
):
    query_out, key_out, value_out = outs
    span = pl.ds(start, length)
    query = query_ref[span, :] * jnp.asarray(SCALE, BF16)
    key, value, grad = key_ref[span, :], value_ref[span, :], grad_ref[span, :]
    product = grad.astype(F32) * context_ref[span, :].astype(F32)
    flipped, key_sum, value_sum = None, None, None
    for which in range(2):
        query_one = head_only(query, which)
        grad_one = head_only(grad, which)
        ones = head_only(jnp.ones((8, 2 * HEAD_DIM), F32), which)
        row_dot = lax.dot_general(
            ones,
            product,
            (((1,), (1,)), ((), ())),
            precision=lax.Precision.HIGHEST,
            preferred_element_type=F32,
        )[:1]
        scores = dot_lanes(key, query_one)
        attention = jnp.exp(scores - total_ref[0, 0, which : which + 1, span])
        weight_grad = dot_lanes(value, grad_one)
        score_grad = (attention * (weight_grad - row_dot)).astype(BF16)
        value_part = dot_plain(attention.astype(BF16), grad_one)
        key_part = dot_plain(score_grad, query_one)
        query_part = dot_rows(head_only(key, which), score_grad)
        flipped = query_part if flipped is None else flipped + query_part
        key_sum = key_part if key_sum is None else key_sum + key_part
        value_sum = value_part if value_sum is None else value_sum + value_part
    query_out[span, :] = (flipped.T * SCALE).astype(BF16)
    key_out[span, :] = key_sum.astype(BF16)
    value_out[span, :] = value_sum.astype(BF16)


def by_kind(kind, run):
    @pl.when(kind != 1)
    def _():
        run(0, BLOCK)

    @pl.when(kind == 1)
    def _():
        for part in range(PARTS):
            run(part * (BLOCK // PARTS), BLOCK // PARTS)


def forward_kernel(kinds, query_ref, key_ref, value_ref, context_ref, total_ref):
    def run(start, length):
        forward_span(query_ref, key_ref, value_ref, context_ref, total_ref, start, length)

    by_kind(kinds[pl.program_id(0)], run)


def backward_kernel(kinds, *refs):
    def run(start, length):
        backward_span(*refs[:6], refs[6:], start, length)

    by_kind(kinds[pl.program_id(0)], run)


def attend_forward(kinds, packed, width):
    tokens = packed.shape[0]
    blocks, pairs = tokens // BLOCK, width // (2 * HEAD_DIM)

    def at(offset):
        return pl.BlockSpec((BLOCK, 2 * HEAD_DIM), lambda b, p, *_: (b, p + offset))

    totals = pl.BlockSpec((1, 1, 2, BLOCK), lambda b, p, *_: (b, p, 0, 0))
    return pl.pallas_call(
        forward_kernel,
        grid_spec=pltpu.PrefetchScalarGridSpec(
            num_scalar_prefetch=1,
            grid=(blocks, pairs),
            in_specs=[at(0), at(pairs), at(2 * pairs)],
            out_specs=[at(0), totals],
        ),
        out_shape=(
            jax.ShapeDtypeStruct((tokens, width), BF16),
            jax.ShapeDtypeStruct((blocks, pairs, 2, BLOCK), F32),
        ),
        cost_estimate=pl.CostEstimate(
            flops=4 * tokens * BLOCK * width,
            bytes_accessed=8 * tokens * width,
            transcendentals=tokens * BLOCK * width // HEAD_DIM,
        ),
        name="attend_forward",
    )(kinds, packed, packed, packed)


def attend_backward(kinds, packed, context, context_grad, totals):
    tokens, width = context.shape
    blocks, pairs = tokens // BLOCK, width // (2 * HEAD_DIM)

    def at(offset):
        return pl.BlockSpec((BLOCK, 2 * HEAD_DIM), lambda b, p, *_: (b, p + offset))

    total_spec = pl.BlockSpec((1, 1, 2, BLOCK), lambda b, p, *_: (b, p, 0, 0))
    return pl.pallas_call(
        backward_kernel,
        grid_spec=pltpu.PrefetchScalarGridSpec(
            num_scalar_prefetch=1,
            grid=(blocks, pairs),
            in_specs=[at(0), at(pairs), at(2 * pairs), at(0), at(0), total_spec],
            out_specs=[at(0), at(0), at(0)],
        ),
        out_shape=(jax.ShapeDtypeStruct((tokens, width), BF16),) * 3,
        cost_estimate=pl.CostEstimate(
            flops=10 * tokens * BLOCK * width,
            bytes_accessed=16 * tokens * width,
            transcendentals=tokens * BLOCK * width // HEAD_DIM,
        ),
        name="attend_backward",
    )(kinds, packed, packed, packed, context, context_grad, totals)


def gelu_exact(inner):
    return 0.5 * inner * (1.0 + lax.erf(inner * 0.7071067811865476))


def norm_apply(hidden_in, norm_gain, norm_shift):
    average = jnp.mean(hidden_in, axis=-1, keepdims=True)
    centred = hidden_in - average
    variance = jnp.mean(centred * centred, axis=-1, keepdims=True)
    return centred * lax.rsqrt(variance + EPSILON) * norm_gain + norm_shift


def shards(
    tokens,
    block_kind,
    query_weight,
    key_weight,
    value_weight,
    query_bias,
    value_bias,
    output_weight,
    output_bias,
    first_gain,
    first_shift,
    inner_weight,
    inner_bias,
    outer_weight,
    outer_bias,
    second_gain,
    second_shift,
    cotangent,
):
    width = tokens.shape[1]
    per_device = block_kind.shape[0] // lax.axis_size("heads")
    kinds = lax.dynamic_slice_in_dim(
        block_kind, lax.axis_index("heads") * per_device, per_device
    )
    valid = jnp.repeat((kinds != 2).astype(F32), BLOCK)[:, None]

    packed_weight = gather_columns((query_weight, key_weight, value_weight))
    output_full = gather_dense(output_weight)
    inner_full = gather_dense(inner_weight)
    outer_full = gather_dense(outer_weight)

    packed_bias = jnp.concatenate([query_bias, jnp.zeros_like(query_bias), value_bias])
    packed = (dot_plain(tokens, packed_weight) + packed_bias.astype(F32)).astype(BF16)
    context, totals = attend_forward(kinds, packed, width)

    attended = dot_plain(context, output_full) + output_bias
    first_sum = tokens.astype(F32) + attended
    first_out = norm_apply(first_sum, first_gain, first_shift)
    first_low = first_out.astype(BF16)
    inner_pre = dot_plain(first_low, inner_full) + inner_bias
    hidden_low = gelu_exact(inner_pre).astype(BF16)
    second_sum = first_out + (dot_plain(hidden_low, outer_full) + outer_bias)
    final = norm_apply(second_sum, second_gain, second_shift)
    layer_out = (final * valid).astype(BF16)

    out_grad = cotangent.astype(F32) * valid
    _, second_pull = jax.vjp(
        norm_apply, second_sum, second_gain.astype(F32), second_shift.astype(F32)
    )
    second_grad, second_gain_grad, second_shift_grad = second_pull(out_grad)
    branch_grad = second_grad.astype(BF16)
    outer_term = dot_rows(hidden_low, branch_grad).astype(BF16)
    outer_bias_grad = jnp.sum(branch_grad, axis=0, dtype=F32)
    outer_weight_grad = scatter_dense(outer_term)
    hidden_grad = dot_lanes(branch_grad, outer_full)
    _, gelu_pull = jax.vjp(gelu_exact, inner_pre)
    inner_grad = gelu_pull(hidden_grad)[0].astype(BF16)
    inner_term = dot_rows(first_low, inner_grad).astype(BF16)
    inner_bias_grad = jnp.sum(inner_grad, axis=0, dtype=F32)
    inner_weight_grad = scatter_dense(inner_term)
    first_out_grad = second_grad + dot_lanes(inner_grad, inner_full)
    _, first_pull = jax.vjp(
        norm_apply, first_sum, first_gain.astype(F32), first_shift.astype(F32)
    )
    first_grad, first_gain_grad, first_shift_grad = first_pull(first_out_grad)
    attended_grad = first_grad.astype(BF16)
    output_term = dot_rows(context, attended_grad).astype(BF16)
    output_bias_grad = jnp.sum(attended_grad, axis=0, dtype=F32)
    output_weight_grad = scatter_dense(output_term)
    context_grad = dot_lanes(attended_grad, output_full).astype(BF16)

    pieces = attend_backward(kinds, packed, context, context_grad, totals)
    packed_grad = jnp.concatenate(pieces, axis=1)
    packed_term = dot_rows(tokens, packed_grad).astype(BF16)
    query_weight_grad, key_weight_grad, value_weight_grad = scatter_columns(
        packed_term, query_weight.shape[1]
    )
    query_bias_grad = jnp.sum(pieces[0], axis=0, dtype=F32)
    value_bias_grad = jnp.sum(pieces[2], axis=0, dtype=F32)
    tokens_grad = first_grad + dot_lanes(packed_grad, packed_weight)

    small = lax.psum(
        (
            query_bias_grad,
            value_bias_grad,
            output_bias_grad,
            first_gain_grad,
            first_shift_grad,
            inner_bias_grad,
            outer_bias_grad,
            second_gain_grad,
            second_shift_grad,
        ),
        ("rows", "heads"),
    )
    return (
        layer_out,
        tokens_grad,
        query_weight_grad,
        key_weight_grad,
        value_weight_grad,
        small[0],
        small[1],
        output_weight_grad,
        small[2],
        small[3],
        small[4],
        inner_weight_grad,
        small[5],
        outer_weight_grad,
        small[6],
        small[7],
        small[8],
    )


def solution(mesh):
    both = P(("rows", "heads"), None)
    placed = (
        (both, P("rows"))
        + (P("rows", "heads"),) * 3
        + (P(), P(), both, P(), P(), P(), both, P(), both, P(), P(), P(), both)
    )
    given = (
        (both, both)
        + (P("rows", "heads"),) * 3
        + (P(), P(), both, P(), P(), P(), both, P(), both, P(), P(), P())
    )
    return jax.shard_map(
        shards, mesh=mesh, in_specs=placed, out_specs=given, check_vma=False
    )
```

```python
import functools

import jax
import jax.numpy as jnp
from jax import lax
from jax.experimental import pallas as pl
from jax.experimental.pallas import tpu as pltpu
from jax.sharding import PartitionSpec as P

HEAD_DIM = 64
BLOCK = 512
PARTS = 4
EPSILON = 1e-06
SCALE = 0.125
F32 = jnp.float32
BF16 = jnp.bfloat16


def by_core(first, second):
    return jnp.where(lax.axis_index("rows") & 1 == 1, second, first)


SWAPS = {"core": (1, 1), "first": (2, 4), "second": (4, 2)}


def exchange(value, stage):
    bits = SWAPS[stage]
    return lax.ppermute(value, "rows", [(i, i ^ bits[i & 1]) for i in range(8)])


def shift_line(value, step):
    return lax.ppermute(value, "heads", [(i, (i + step) % 4) for i in range(4)])


def slot_orders():
    here = lax.axis_index("rows")
    first, second = by_core(2, 4), by_core(4, 2)
    keep = jnp.stack([here, here ^ first, here ^ second, here ^ 6])
    away = jnp.stack([here, here ^ second, here ^ first, here ^ 6]) ^ 1
    return keep.astype(jnp.int32), away.astype(jnp.int32)


def after(value, *others):
    return lax.optimization_barrier((value,) + others)[0]


def behind(value, gates):
    if not gates:
        return value
    values = value if isinstance(value, tuple) else (value,)
    values = lax.optimization_barrier(values + tuple(gates))[: len(values)]
    return values if isinstance(value, tuple) else values[0]


def line_gather(piece):
    return (piece,) + tuple(shift_line(piece, step) for step in (1, 2, 3))


def line_order(pieces):
    here = lax.axis_index("heads")
    turned = [pieces[-i % 4] for i in range(4)]
    for bit in (1, 2):
        turned = [
            jnp.where(here & bit == bit, turned[i - bit], turned[i]) for i in range(4)
        ]
    return jnp.stack(turned)


def plane_gather(piece):
    return exchange(piece, "first"), exchange(piece, "second")


def plane_rest(ones):
    return exchange(after(*ones), "second")


def core_gather(mine):
    return tuple(exchange(member, "core") for member in mine)


def scatter_steps(send, keep, stack):
    gates = yield send
    got = behind(exchange(send, "core"), gates)
    low = (keep[2:].astype(F32) + got[2:].astype(F32)).astype(BF16)
    gates = yield low
    got_two = behind(exchange(low, "second"), gates)
    one = (keep[1].astype(F32) + got[1].astype(F32) + got_two[1].astype(F32)).astype(BF16)
    gates = yield one
    got_one = behind(exchange(one, "first"), gates).astype(F32)
    zero = keep[0].astype(F32) + got[0].astype(F32) + got_two[0].astype(F32)
    stacked = stack((zero + got_one).astype(BF16))
    here = lax.axis_index("heads")
    sent = [
        lax.dynamic_index_in_dim(stacked, (here + step) % 4, keepdims=False)
        for step in range(4)
    ]
    gates = yield sent[3]
    parts = tuple(shift_line(sent[step], step) for step in (1, 2, 3))
    parts = behind(parts, gates)
    yield sent[0].astype(F32) + sum(part.astype(F32) for part in parts)


def stack_rows(part):
    return part.reshape(4, -1, part.shape[1])


def stack_columns(part):
    width = part.shape[1] // 12
    return part.reshape(-1, 3, 4, width).transpose(2, 0, 1, 3).reshape(4, -1, 3 * width)


def total_steps(value):
    value = value + exchange(value, "core")
    yield value
    value = value + exchange(value, "second")
    yield value
    value = value + exchange(value, "first")
    yield value
    yield value + sum(shift_line(value, step) for step in (1, 2, 3))


HBM = pl.BlockSpec(memory_space=pl.ANY)
WIDE = pltpu.CompilerParams(vmem_limit_bytes=50 << 20)


def copy_all(moves, semaphores):
    copies = [
        pltpu.make_async_copy(source, target, semaphores.at[i])
        for i, (source, target) in enumerate(moves)
    ]
    for copy in copies:
        copy.start()
    for copy in copies:
        copy.wait()


def project_kernel(order, tokens, bias, *refs):
    pieces, (packed, full, semaphores) = refs[:8], refs[8:]

    @pl.when(pl.program_id(0) == 0)
    def _():
        copy_all([(pieces[i], full.at[order[i]]) for i in range(8)], semaphores)

    weight = full[...].reshape(-1, full.shape[2])
    packed[...] = (dot_plain(tokens[...], weight) + bias[...]).astype(BF16)


def project(order, tokens, bias, pieces):
    count, width = tokens.shape
    depth, columns = pieces[0].shape
    tile = count // 4
    return pl.pallas_call(
        project_kernel,
        grid_spec=pltpu.PrefetchScalarGridSpec(
            num_scalar_prefetch=1,
            grid=(4,),
            in_specs=[
                pl.BlockSpec((tile, width), lambda i, *_: (i, 0)),
                pl.BlockSpec((1, columns), lambda i, *_: (0, 0)),
            ]
            + [HBM] * 8,
            out_specs=[
                pl.BlockSpec((tile, columns), lambda i, *_: (i, 0)),
                pl.BlockSpec((8, depth, columns), lambda i, *_: (0, 0, 0)),
            ],
            scratch_shapes=[pltpu.SemaphoreType.DMA((8,))],
        ),
        out_shape=(
            jax.ShapeDtypeStruct((count, columns), BF16),
            jax.ShapeDtypeStruct((8, depth, columns), BF16),
        ),
        compiler_params=WIDE,
        cost_estimate=pl.CostEstimate(
            flops=2 * count * width * columns,
            bytes_accessed=2 * (count * (width + columns) + 2 * width * columns),
            transcendentals=0,
        ),
        name="project",
    )(order, tokens, bias, *pieces)


def join_kernel(order, *refs):
    pieces, (output_full, inner_full, semaphores) = refs[:8], refs[8:]
    depth, width = output_full.shape[1:]
    moves = []
    for slot in range(8):
        moves.append((pieces[slot].at[pl.ds(0, depth)], output_full.at[order[slot]]))
        for column in range(inner_full.shape[2] // width):
            source = pieces[slot].at[pl.ds(depth * (1 + column), depth)]
            target = inner_full.at[order[slot], :, pl.ds(column * width, width)]
            moves.append((source, target))
    copy_all(moves, semaphores)


def join(order, pieces, depth, columns):
    width = pieces[0].shape[1]
    shapes = [(8, depth, width), (8, depth, columns * width)]
    size = pieces[0].size * 8
    return pl.pallas_call(
        join_kernel,
        in_specs=[pl.BlockSpec(memory_space=pltpu.SMEM)] + [HBM] * 8,
        out_specs=[pl.BlockSpec(memory_space=pltpu.VMEM)] * 2,
        out_shape=tuple(jax.ShapeDtypeStruct(shape, BF16) for shape in shapes),
        scratch_shapes=[pltpu.SemaphoreType.DMA((8 * (columns + 1),))],
        compiler_params=WIDE,
        cost_estimate=pl.CostEstimate(flops=0, bytes_accessed=4 * size, transcendentals=0),
        name="join",
    )(order, *pieces)


def rows_terms_kernel(parts, order, *refs):
    lefts, rights = refs[:parts], refs[parts : 2 * parts]
    send_ref, keep_ref, turned, product = refs[2 * parts :]
    step = pl.program_id(0)
    depth = send_ref.shape[1]
    begin = 0
    for left, right in zip(lefts, rights):
        steps = right[1]

        @pl.when(step == begin)
        def _(left=left):
            turned[...] = left[...].T

        @pl.when((step >= begin) & (step < begin + steps))
        def _(right=right[0]):
            product[...] = dot_plain(turned[...], right[...])

        begin += steps
    for slot in range(4):
        for out, place in ((send_ref, 4 + slot), (keep_ref, slot)):
            start = pl.multiple_of(order[place] * depth, depth)
            out[slot] = product[pl.ds(start, depth), :].astype(BF16)


def rows_terms(pairs, order):
    tokens, width = pairs[0][0].shape
    counts = [right.shape[1] // width for _, right in pairs]
    total = sum(counts)

    def right_spec(begin, count):
        return pl.BlockSpec(
            (tokens, width), lambda i, *_: (0, jnp.clip(i - begin, 0, count - 1))
        )

    begins = [sum(counts[:i]) for i in range(len(counts))]
    whole = pl.BlockSpec((tokens, width), lambda i, *_: (0, 0))
    slots = pl.BlockSpec((4, width // 8, width), lambda i, *_: (0, 0, i))

    def kernel(order_ref, *refs):
        n = len(pairs)
        rights = tuple(zip(refs[n : 2 * n], counts))
        rows_terms_kernel(n, order_ref, *refs[:n], *rights, *refs[2 * n :])

    return pl.pallas_call(
        kernel,
        grid_spec=pltpu.PrefetchScalarGridSpec(
            num_scalar_prefetch=1,
            grid=(total,),
            in_specs=[whole for _ in pairs] + [right_spec(b, c) for b, c in zip(begins, counts)],
            out_specs=[slots, slots],
            scratch_shapes=[pltpu.VMEM((width, tokens), BF16), pltpu.VMEM((width, width), F32)],
        ),
        out_shape=(jax.ShapeDtypeStruct((4, width // 8, total * width), BF16),) * 2,
        compiler_params=pltpu.CompilerParams(vmem_limit_bytes=48 << 20),
        cost_estimate=pl.CostEstimate(
            flops=2 * tokens * width * width * total,
            bytes_accessed=2 * (tokens + width) * width * total,
            transcendentals=0,
        ),
        name="rows_terms",
    )(order, *[left for left, _ in pairs], *[right for _, right in pairs])


def columns_term_kernel(order, left, right, out):
    out[0] = dot_rows(left[...], right[...]).astype(BF16)


def columns_term(left, right, order):
    tokens, width = right.shape
    depth = left.shape[1] // 8
    return pl.pallas_call(
        columns_term_kernel,
        grid_spec=pltpu.PrefetchScalarGridSpec(
            num_scalar_prefetch=1,
            grid=(4,),
            in_specs=[
                pl.BlockSpec((tokens, depth), lambda i, order: (0, order[i])),
                pl.BlockSpec((tokens, width), lambda i, order: (0, 0)),
            ],
            out_specs=pl.BlockSpec((1, depth, width), lambda i, order: (i, 0, 0)),
        ),
        out_shape=jax.ShapeDtypeStruct((4, depth, width), BF16),
        compiler_params=pltpu.CompilerParams(vmem_limit_bytes=48 << 20),
        cost_estimate=pl.CostEstimate(
            flops=2 * tokens * width * depth * 4,
            bytes_accessed=2 * (tokens * depth * 4 + tokens * width + depth * width * 4),
            transcendentals=0,
        ),
        name="columns_term",
    )(order, left, right)


class SlotMoves:
    def __init__(self):
        self.keep, self.away = slot_orders()
        self.order = jnp.concatenate([self.keep, self.away])

    def gather(self, weights, output_weight, inner_weight, outer_weight):
        depth, width = output_weight.shape
        self.columns = inner_weight.shape[1] // width
        pieces = line_gather(jnp.concatenate(weights, axis=1))
        split = [
            inner_weight[:, i * width : (i + 1) * width] for i in range(self.columns)
        ]
        self.dense_line = line_gather(jnp.concatenate([output_weight, *split]))
        lined = line_order(pieces)
        rows = lined.shape[1]
        lined = lined.reshape(4, rows, 3, -1).transpose(1, 2, 0, 3).reshape(rows, -1)
        ones = plane_gather(lined)
        two = plane_rest(ones)
        self.dense_line = behind(self.dense_line, ones)
        mine = (lined,) + ones + (two,)
        self.packed_pieces = mine + core_gather(mine)
        outer_weight = after(outer_weight, pieces[3])
        self.outer_full = lax.all_gather(outer_weight, ("rows", "heads"), axis=0, tiled=True)

    def project(self, tokens, bias):
        lined = line_order(self.dense_line)
        width = lined.shape[2]
        lined = lined.reshape(4, self.columns + 1, -1, width).transpose(1, 0, 2, 3)
        lined = lined.reshape(-1, width)
        tokens = after(tokens, lined)
        packed, full = project(self.order, tokens, bias.reshape(1, -1), self.packed_pieces)
        ones = behind(plane_gather(lined), (packed,))
        self.dense_mine = (lined,) + ones
        self.dense_depth = lined.shape[0] // (self.columns + 1)
        return after(packed, *ones), full.reshape(-1, full.shape[2])

    def dense_start(self, packed, earlier):
        mine = self.dense_mine
        got = core_gather(mine) + (plane_rest(mine[1:]),)
        got = got if earlier is None else behind(got, (earlier[0],))
        self.dense_got = got
        return after(packed, got[3])

    def dense(self, context):
        got = self.dense_got
        (last,) = behind(core_gather(got[3:]), (context,))
        pieces = self.dense_mine + got[3:] + got[:3] + (last,)
        fulls = join(self.order, pieces, self.dense_depth, self.columns)
        return tuple(full.reshape(-1, full.shape[2]) for full in fulls) + (self.outer_full,)

    def outer_terms(self, hidden_low, branch_grad):
        send = columns_term(hidden_low, branch_grad, self.away)
        keep = columns_term(after(hidden_low, send), branch_grad, self.keep)
        return keep, self.begin(scatter_steps(send, keep, stack_rows))

    def inner_terms(self, inner_pair, output_pair):
        terms = rows_terms((inner_pair, output_pair), self.order)
        return terms[1], self.begin(scatter_steps(*terms, stack_rows))

    def inner_cut(self, both):
        cut = self.columns * both.shape[1] // (self.columns + 1)
        return both[:, :cut], both[:, cut:]

    def packed_terms(self, tokens, packed_grad):
        terms = rows_terms(((tokens, packed_grad),), self.order)
        return self.begin(scatter_steps(*terms, stack_columns))

    def begin(self, steps):
        next(steps)
        return steps

    def packed_cut(self, total):
        width = total.shape[1] // 3
        return tuple(total[:, i * width : (i + 1) * width] for i in range(3))

    def behind(self, value, steps, *gates):
        return after(value, steps.send(gates))

    def hold(self, value, gate):
        return after(value, gate)

    def finish(self, steps, *gates):
        return steps.send(gates)

    def last(self, value, steps, small, earlier):
        low = steps.send(())
        totals = total_steps(after(small, low))
        value = value(low)
        done = earlier.send((value,))
        gates = (value,)
        while True:
            beside = next(totals)
            try:
                sent = steps.send((beside,) + gates)
            except StopIteration:
                return value, sent, beside, done
            gates = ()


class PlainMoves:
    def gather(self, weights, *dense):
        full = [
            lax.all_gather(lax.all_gather(w, "rows", axis=0, tiled=True), "heads", axis=1, tiled=True)
            for w in weights
        ]
        self.packed_weight = jnp.concatenate(full, axis=1)
        self.fulls = tuple(
            lax.all_gather(w, ("rows", "heads"), axis=0, tiled=True) for w in dense
        )

    def project(self, tokens, bias):
        packed = (dot_plain(tokens, self.packed_weight) + bias).astype(BF16)
        return packed, self.packed_weight

    def dense_start(self, packed, earlier):
        return packed

    def dense(self, context):
        return self.fulls

    def scatter(self, term):
        return lax.psum_scatter(term, ("rows", "heads"), scatter_dimension=0, tiled=True)

    def outer_terms(self, hidden_low, branch_grad):
        return None, self.scatter(dot_rows(hidden_low, branch_grad))

    def inner_terms(self, inner_pair, output_pair):
        both = self.scatter(dot_rows(*inner_pair)), self.scatter(dot_rows(*output_pair))
        return None, both

    def inner_cut(self, both):
        return both

    def packed_terms(self, tokens, packed_grad):
        term = dot_rows(tokens, packed_grad)
        width = tokens.shape[1]
        parts = [term[:, i * width : (i + 1) * width] for i in range(3)]
        parts = [lax.psum_scatter(p, "heads", scatter_dimension=1, tiled=True) for p in parts]
        return tuple(
            lax.psum_scatter(p, "rows", scatter_dimension=0, tiled=True) for p in parts
        )

    def packed_cut(self, total):
        return total

    def behind(self, value, steps, *gates):
        return value

    def hold(self, value, gate):
        return value

    def finish(self, steps, *gates):
        return steps

    def last(self, value, steps, small, earlier):
        return value(small), steps, lax.psum(small, ("rows", "heads")), earlier


def head_only(value, which):
    lanes = lax.broadcasted_iota(jnp.int32, value.shape, 1)
    keep = (lanes < HEAD_DIM) if which == 0 else (lanes >= HEAD_DIM)
    return jnp.where(keep, value, jnp.zeros_like(value))


def dot_lanes(left, right):
    return lax.dot_general(left, right, (((1,), (1,)), ((), ())), preferred_element_type=F32)


def dot_rows(left, right):
    return lax.dot_general(left, right, (((0,), (0,)), ((), ())), preferred_element_type=F32)


def dot_plain(left, right):
    return lax.dot_general(left, right, (((1,), (0,)), ((), ())), preferred_element_type=F32)


def forward_span(query_ref, key_ref, value_ref, context_ref, total_ref, start, length):
    span = pl.ds(start, length)
    query = query_ref[span, :] * jnp.asarray(SCALE, BF16)
    key, value = key_ref[span, :], value_ref[span, :]
    flipped = None
    for which in range(2):
        scores = dot_lanes(key, head_only(query, which))
        largest = jnp.max(scores, axis=0, keepdims=True)
        powers = jnp.exp(scores - largest)
        denominator = jnp.sum(powers, axis=0, keepdims=True)
        total_ref[0, 0, which : which + 1, span] = largest + jnp.log(denominator)
        part = dot_rows(head_only(value, which), powers.astype(BF16)) / denominator
        flipped = part if flipped is None else flipped + part
    context_ref[span, :] = flipped.T.astype(BF16)


def backward_span(
    query_ref, key_ref, value_ref, context_ref, grad_ref, total_ref, outs, start, length
):
    query_out, key_out, value_out = outs
    span = pl.ds(start, length)
    query = query_ref[span, :] * jnp.asarray(SCALE, BF16)
    key, value, grad = key_ref[span, :], value_ref[span, :], grad_ref[span, :]
    product = grad.astype(F32) * context_ref[span, :].astype(F32)
    flipped, key_sum, value_sum = None, None, None
    for which in range(2):
        query_one = head_only(query, which)
        grad_one = head_only(grad, which)
        ones = head_only(jnp.ones((8, 2 * HEAD_DIM), F32), which)
        row_dot = lax.dot_general(
            ones,
            product,
            (((1,), (1,)), ((), ())),
            precision=lax.Precision.HIGHEST,
            preferred_element_type=F32,
        )[:1]
        scores = dot_lanes(key, query_one)
        attention = jnp.exp(scores - total_ref[0, 0, which : which + 1, span])
        weight_grad = dot_lanes(value, grad_one)
        score_grad = (attention * (weight_grad - row_dot)).astype(BF16)
        value_part = dot_plain(attention.astype(BF16), grad_one)
        key_part = dot_plain(score_grad, query_one)
        query_part = dot_rows(head_only(key, which), score_grad)
        flipped = query_part if flipped is None else flipped + query_part
        key_sum = key_part if key_sum is None else key_sum + key_part
        value_sum = value_part if value_sum is None else value_sum + value_part
    query_out[span, :] = (flipped.T * SCALE).astype(BF16)
    key_out[span, :] = key_sum.astype(BF16)
    value_out[span, :] = value_sum.astype(BF16)


def by_kind(kind, run):
    @pl.when(kind != 1)
    def _():
        run(0, BLOCK)

    @pl.when(kind == 1)
    def _():
        length = BLOCK // PARTS

        @pl.loop(0, PARTS)
        def _(part):
            run(pl.multiple_of(part * length, length), length)


def forward_kernel(block, kinds, query_ref, key_ref, value_ref, *refs):
    def run(start, length):
        forward_span(query_ref, key_ref, value_ref, *refs[-2:], start, length)

    by_kind(kinds[block], run)


def backward_kernel(block, kinds, *refs):
    def run(start, length):
        backward_span(*refs[:6], refs[-3:], start, length)

    by_kind(kinds[block], run)


def attend(kernel, block, kinds, operands, earlier, outs, cost, name):
    pairs = outs[0].shape[1] // (2 * HEAD_DIM)

    def spec(offset):
        if offset is None:
            return pl.BlockSpec((1, 1, 2, BLOCK), lambda p, *_: (block, p, 0, 0))
        return pl.BlockSpec((BLOCK, 2 * HEAD_DIM), lambda p, *_: (block, p + offset))

    given = () if earlier is None else earlier
    first = 1 + len(operands)
    return pl.pallas_call(
        functools.partial(kernel, block),
        grid_spec=pltpu.PrefetchScalarGridSpec(
            num_scalar_prefetch=1,
            grid=(pairs,),
            in_specs=[spec(offset) for _, offset in operands] + [HBM for _ in given],
            out_specs=[spec(None if len(out.shape) == 4 else 0) for out in outs],
        ),
        out_shape=outs,
        input_output_aliases={first + i: i for i in range(len(given))},
        cost_estimate=cost,
        name=name,
    )(kinds, *[operand for operand, _ in operands], *given)


def attend_forward(block, kinds, packed, earlier):
    tokens, width = packed.shape[0], packed.shape[1] // 3
    pairs = width // (2 * HEAD_DIM)
    outs = (
        jax.ShapeDtypeStruct((tokens, width), BF16),
        jax.ShapeDtypeStruct((tokens // BLOCK, pairs, 2, BLOCK), F32),
    )
    cost = pl.CostEstimate(
        flops=16 * BLOCK * BLOCK * width,
        bytes_accessed=8 * BLOCK * width,
        transcendentals=BLOCK * BLOCK * width // HEAD_DIM,
    )
    operands = [(packed, 0), (packed, pairs), (packed, 2 * pairs)]
    return attend(forward_kernel, block, kinds, operands, earlier, outs, cost, "attend_forward")


def attend_backward(block, kinds, packed, context, context_grad, totals, earlier):
    tokens, width = context.shape
    pairs = width // (2 * HEAD_DIM)
    outs = (jax.ShapeDtypeStruct((tokens, width), BF16),) * 3
    cost = pl.CostEstimate(
        flops=40 * BLOCK * BLOCK * width,
        bytes_accessed=16 * BLOCK * width,
        transcendentals=BLOCK * BLOCK * width // HEAD_DIM,
    )
    operands = [(packed, 0), (packed, pairs), (packed, 2 * pairs), (context, 0)]
    operands += [(context_grad, 0), (totals, None)]
    return attend(backward_kernel, block, kinds, operands, earlier, outs, cost, "attend_backward")


def gelu_exact(inner):
    return 0.5 * inner * (1.0 + lax.erf(inner * 0.7071067811865476))


def norm_apply(hidden_in, norm_gain, norm_shift):
    average = jnp.mean(hidden_in, axis=-1, keepdims=True)
    centred = hidden_in - average
    variance = jnp.mean(centred * centred, axis=-1, keepdims=True)
    return centred * lax.rsqrt(variance + EPSILON) * norm_gain + norm_shift


def shards(
    tokens,
    block_kind,
    query_weight,
    key_weight,
    value_weight,
    query_bias,
    value_bias,
    output_weight,
    output_bias,
    first_gain,
    first_shift,
    inner_weight,
    inner_bias,
    outer_weight,
    outer_bias,
    second_gain,
    second_shift,
    cotangent,
):
    width = tokens.shape[1]
    per_device = block_kind.shape[0] // lax.axis_size("heads")
    kinds = lax.dynamic_slice_in_dim(
        block_kind, lax.axis_index("heads") * per_device, per_device
    )
    valid = jnp.repeat((kinds != 2).astype(F32), BLOCK)[:, None]

    eight_by_four = lax.axis_size("rows") == 8 and lax.axis_size("heads") == 4
    moves = SlotMoves() if eight_by_four else PlainMoves()
    moves.gather(
        (query_weight, key_weight, value_weight), output_weight, inner_weight, outer_weight
    )

    packed_bias = jnp.concatenate([query_bias, jnp.zeros_like(query_bias), value_bias])
    packed, packed_weight = moves.project(tokens, packed_bias.astype(F32))
    earlier = None
    for block in range(per_device):
        if block == per_device - 1:
            packed = moves.dense_start(packed, earlier)
        earlier = attend_forward(block, kinds, packed, earlier)
    context, totals = earlier
    output_full, inner_full, outer_full = moves.dense(context)

    attended = dot_plain(context, output_full) + output_bias
    first_sum = tokens.astype(F32) + attended
    first_out = norm_apply(first_sum, first_gain, first_shift)
    first_low = first_out.astype(BF16)
    inner_pre = dot_plain(first_low, inner_full) + inner_bias
    hidden_low = gelu_exact(inner_pre).astype(BF16)
    second_sum = first_out + (dot_plain(hidden_low, outer_full) + outer_bias)
    final = norm_apply(second_sum, second_gain, second_shift)
    layer_out = (final * valid).astype(BF16)

    out_grad = cotangent.astype(F32) * valid
    _, second_pull = jax.vjp(
        norm_apply, second_sum, second_gain.astype(F32), second_shift.astype(F32)
    )
    second_grad, second_gain_grad, second_shift_grad = second_pull(out_grad)
    branch_grad = second_grad.astype(BF16)
    kernel_done, outer_steps = moves.outer_terms(hidden_low, branch_grad)
    outer_bias_grad = jnp.sum(branch_grad, axis=0, dtype=F32)
    branch_grad = moves.behind(branch_grad, outer_steps, kernel_done)
    hidden_grad = dot_lanes(branch_grad, outer_full)
    _, gelu_pull = jax.vjp(gelu_exact, inner_pre)
    inner_grad = gelu_pull(hidden_grad)[0].astype(BF16)
    inner_bias_grad = jnp.sum(inner_grad, axis=0, dtype=F32)
    inner_grad = moves.behind(inner_grad, outer_steps, inner_grad)
    first_out_grad = second_grad + dot_lanes(inner_grad, inner_full)
    _, first_pull = jax.vjp(
        norm_apply, first_sum, first_gain.astype(F32), first_shift.astype(F32)
    )
    first_grad, first_gain_grad, first_shift_grad = first_pull(first_out_grad)
    attended_grad = first_grad.astype(BF16)
    output_bias_grad = jnp.sum(attended_grad, axis=0, dtype=F32)
    terms_grad = moves.behind(attended_grad, outer_steps, attended_grad)
    kernel_done, inner_steps = moves.inner_terms((first_low, inner_grad), (context, terms_grad))
    outer_weight_grad = moves.finish(outer_steps, kernel_done)
    attended_grad = moves.hold(attended_grad, outer_weight_grad)
    context_grad = dot_lanes(attended_grad, output_full).astype(BF16)
    context_grad = moves.behind(context_grad, inner_steps, context_grad)
    pieces = None
    for block in range(per_device):
        if block > 0:
            context_grad = moves.behind(context_grad, inner_steps, pieces[0])
        pieces = attend_backward(block, kinds, packed, context, context_grad, totals, pieces)
    packed_grad = jnp.concatenate(pieces, axis=1)
    packed_grad = moves.behind(packed_grad, inner_steps, pieces[0])
    packed_steps = moves.packed_terms(tokens, packed_grad)
    sums = (
        jnp.sum(pieces[0], axis=0, dtype=F32),
        jnp.sum(pieces[2], axis=0, dtype=F32),
        output_bias_grad,
        first_gain_grad,
        first_shift_grad,
        outer_bias_grad,
        second_gain_grad,
        second_shift_grad,
    )
    inner_rows = inner_bias_grad.reshape(-1, width)

    def tokens_part(gate):
        return first_grad + dot_lanes(after(packed_grad, gate), packed_weight)

    tokens_grad, packed_total, small, inner_both = moves.last(
        tokens_part, packed_steps, jnp.concatenate([jnp.stack(sums), inner_rows]), inner_steps
    )
    inner_weight_grad, output_weight_grad = moves.inner_cut(inner_both)
    query_weight_grad, key_weight_grad, value_weight_grad = moves.packed_cut(packed_total)
    return (
        layer_out,
        tokens_grad,
        query_weight_grad,
        key_weight_grad,
        value_weight_grad,
        small[0],
        small[1],
        output_weight_grad,
        small[2],
        small[3],
        small[4],
        inner_weight_grad,
        small[len(sums) :].reshape(-1),
        outer_weight_grad,
        small[5],
        small[6],
        small[7],
    )


def solution(mesh):
    both = P(("rows", "heads"), None)
    placed = (
        (both, P("rows"))
        + (P("rows", "heads"),) * 3
        + (P(), P(), both, P(), P(), P(), both, P(), both, P(), P(), P(), both)
    )
    given = (
        (both, both)
        + (P("rows", "heads"),) * 3
        + (P(), P(), both, P(), P(), P(), both, P(), both, P(), P(), P())
    )
    return jax.shard_map(
        shards, mesh=mesh, in_specs=placed, out_specs=given, check_vma=False
    )
```

```python
import functools

import jax
import jax.numpy as jnp
from jax import lax
from jax.experimental import pallas as pl
from jax.experimental.pallas import tpu as pltpu
from jax.sharding import PartitionSpec as P

HEAD_DIM = 64
BLOCK = 512
PARTS = 4
EPSILON = 1e-06
SCALE = 0.125
F32 = jnp.float32
BF16 = jnp.bfloat16


def by_core(first, second):
    return jnp.where(lax.axis_index("rows") & 1 == 1, second, first)


SWAPS = {"core": (1, 1), "first": (2, 4), "second": (4, 2)}


def exchange(value, stage):
    bits = SWAPS[stage]
    return lax.ppermute(value, "rows", [(i, i ^ bits[i & 1]) for i in range(8)])


def shift_line(value, step):
    return lax.ppermute(value, "heads", [(i, (i + step) % 4) for i in range(4)])


def slot_orders():
    here = lax.axis_index("rows")
    first, second = by_core(2, 4), by_core(4, 2)
    keep = jnp.stack([here, here ^ first, here ^ second, here ^ 6])
    away = jnp.stack([here, here ^ second, here ^ first, here ^ 6]) ^ 1
    return keep.astype(jnp.int32), away.astype(jnp.int32)


def after(value, *others):
    return lax.optimization_barrier((value,) + others)[0]


def behind(value, gates):
    if not gates:
        return value
    values = value if isinstance(value, tuple) else (value,)
    values = lax.optimization_barrier(values + tuple(gates))[: len(values)]
    return values if isinstance(value, tuple) else values[0]


def line_gather(piece):
    return (piece,) + tuple(shift_line(piece, step) for step in (1, 2, 3))


def line_order(pieces):
    here = lax.axis_index("heads")
    turned = [pieces[-i % 4] for i in range(4)]
    for bit in (1, 2):
        turned = [
            jnp.where(here & bit == bit, turned[i - bit], turned[i]) for i in range(4)
        ]
    return jnp.stack(turned)


def plane_gather(piece):
    return exchange(piece, "first"), exchange(piece, "second")


def plane_rest(ones):
    return exchange(after(*ones), "second")


def core_gather(mine):
    return tuple(exchange(member, "core") for member in mine)


def scatter_steps(send, keep, stack):
    gates = yield send
    got = behind(exchange(send, "core"), gates)
    low = (keep[2:].astype(F32) + got[2:].astype(F32)).astype(BF16)
    gates = yield low
    got_two = behind(exchange(low, "second"), gates)
    one = (keep[1].astype(F32) + got[1].astype(F32) + got_two[1].astype(F32)).astype(BF16)
    gates = yield one
    got_one = behind(exchange(one, "first"), gates).astype(F32)
    zero = keep[0].astype(F32) + got[0].astype(F32) + got_two[0].astype(F32)
    stacked = stack((zero + got_one).astype(BF16))
    here = lax.axis_index("heads")
    sent = [
        lax.dynamic_index_in_dim(stacked, (here + step) % 4, keepdims=False)
        for step in range(4)
    ]
    gates = yield sent[3]
    parts = tuple(shift_line(sent[step], step) for step in (1, 2, 3))
    parts = behind(parts, gates)
    yield sent[0].astype(F32) + sum(part.astype(F32) for part in parts)


def stack_rows(part):
    return part.reshape(4, -1, part.shape[1])


def stack_columns(part):
    width = part.shape[1] // 12
    return part.reshape(-1, 3, 4, width).transpose(2, 0, 1, 3).reshape(4, -1, 3 * width)


def total_steps(value):
    value = value + exchange(value, "core")
    yield value
    value = value + exchange(value, "second")
    yield value
    value = value + exchange(value, "first")
    yield value
    yield value + sum(shift_line(value, step) for step in (1, 2, 3))


HBM = pl.BlockSpec(memory_space=pl.ANY)
WIDE = pltpu.CompilerParams(vmem_limit_bytes=50 << 20)


def copy_all(moves, semaphores):
    copies = [
        pltpu.make_async_copy(source, target, semaphores.at[i])
        for i, (source, target) in enumerate(moves)
    ]
    for copy in copies:
        copy.start()
    for copy in copies:
        copy.wait()


def project_kernel(order, tokens, bias, *refs):
    pieces, (packed, full, semaphores) = refs[:8], refs[8:]

    @pl.when(pl.program_id(0) == 0)
    def _():
        copy_all([(pieces[i], full.at[order[i]]) for i in range(8)], semaphores)

    weight = full[...].reshape(-1, full.shape[2])
    packed[...] = (dot_plain(tokens[...], weight) + bias[...]).astype(BF16)


def project(order, tokens, bias, pieces):
    count, width = tokens.shape
    depth, columns = pieces[0].shape
    tile = count // 4
    return pl.pallas_call(
        project_kernel,
        grid_spec=pltpu.PrefetchScalarGridSpec(
            num_scalar_prefetch=1,
            grid=(4,),
            in_specs=[
                pl.BlockSpec((tile, width), lambda i, *_: (i, 0)),
                pl.BlockSpec((1, columns), lambda i, *_: (0, 0)),
            ]
            + [HBM] * 8,
            out_specs=[
                pl.BlockSpec((tile, columns), lambda i, *_: (i, 0)),
                pl.BlockSpec((8, depth, columns), lambda i, *_: (0, 0, 0)),
            ],
            scratch_shapes=[pltpu.SemaphoreType.DMA((8,))],
        ),
        out_shape=(
            jax.ShapeDtypeStruct((count, columns), BF16),
            jax.ShapeDtypeStruct((8, depth, columns), BF16),
        ),
        compiler_params=WIDE,
        cost_estimate=pl.CostEstimate(
            flops=2 * count * width * columns,
            bytes_accessed=2 * (count * (width + columns) + 2 * width * columns),
            transcendentals=0,
        ),
        name="project",
    )(order, tokens, bias, *pieces)


def rows_terms_kernel(parts, order, *refs):
    lefts, rights = refs[:parts], refs[parts : 2 * parts]
    send_ref, keep_ref, turned, product = refs[2 * parts :]
    step = pl.program_id(0)
    depth = send_ref.shape[1]
    begin = 0
    for left, right in zip(lefts, rights):
        steps = right[1]

        @pl.when(step == begin)
        def _(left=left):
            turned[...] = left[...].T

        @pl.when((step >= begin) & (step < begin + steps))
        def _(right=right[0]):
            product[...] = dot_plain(turned[...], right[...])

        begin += steps
    for slot in range(4):
        for out, place in ((send_ref, 4 + slot), (keep_ref, slot)):
            start = pl.multiple_of(order[place] * depth, depth)
            out[slot] = product[pl.ds(start, depth), :].astype(BF16)


def rows_terms(pairs, order):
    tokens, width = pairs[0][0].shape
    counts = [right.shape[1] // width for _, right in pairs]
    total = sum(counts)

    def right_spec(begin, count):
        return pl.BlockSpec(
            (tokens, width), lambda i, *_: (0, jnp.clip(i - begin, 0, count - 1))
        )

    begins = [sum(counts[:i]) for i in range(len(counts))]
    whole = pl.BlockSpec((tokens, width), lambda i, *_: (0, 0))
    slots = pl.BlockSpec((4, width // 8, width), lambda i, *_: (0, 0, i))

    def kernel(order_ref, *refs):
        n = len(pairs)
        rights = tuple(zip(refs[n : 2 * n], counts))
        rows_terms_kernel(n, order_ref, *refs[:n], *rights, *refs[2 * n :])

    return pl.pallas_call(
        kernel,
        grid_spec=pltpu.PrefetchScalarGridSpec(
            num_scalar_prefetch=1,
            grid=(total,),
            in_specs=[whole for _ in pairs] + [right_spec(b, c) for b, c in zip(begins, counts)],
            out_specs=[slots, slots],
            scratch_shapes=[pltpu.VMEM((width, tokens), BF16), pltpu.VMEM((width, width), F32)],
        ),
        out_shape=(jax.ShapeDtypeStruct((4, width // 8, total * width), BF16),) * 2,
        compiler_params=pltpu.CompilerParams(vmem_limit_bytes=48 << 20),
        cost_estimate=pl.CostEstimate(
            flops=2 * tokens * width * width * total,
            bytes_accessed=2 * (tokens + width) * width * total,
            transcendentals=0,
        ),
        name="rows_terms",
    )(order, *[left for left, _ in pairs], *[right for _, right in pairs])


def columns_term_kernel(order, left, right, out):
    out[0] = dot_rows(left[...], right[...]).astype(BF16)


def columns_term(left, right, order):
    tokens, width = right.shape
    depth = left.shape[1] // 8
    return pl.pallas_call(
        columns_term_kernel,
        grid_spec=pltpu.PrefetchScalarGridSpec(
            num_scalar_prefetch=1,
            grid=(4,),
            in_specs=[
                pl.BlockSpec((tokens, depth), lambda i, order: (0, order[i])),
                pl.BlockSpec((tokens, width), lambda i, order: (0, 0)),
            ],
            out_specs=pl.BlockSpec((1, depth, width), lambda i, order: (i, 0, 0)),
        ),
        out_shape=jax.ShapeDtypeStruct((4, depth, width), BF16),
        compiler_params=pltpu.CompilerParams(vmem_limit_bytes=48 << 20),
        cost_estimate=pl.CostEstimate(
            flops=2 * tokens * width * depth * 4,
            bytes_accessed=2 * (tokens * depth * 4 + tokens * width + depth * width * 4),
            transcendentals=0,
        ),
        name="columns_term",
    )(order, left, right)


class SlotMoves:
    def __init__(self):
        self.keep, self.away = slot_orders()
        self.order = jnp.concatenate([self.keep, self.away])

    def gather(self, weights, output_weight, inner_weight, outer_weight):
        depth, width = output_weight.shape
        self.columns = inner_weight.shape[1] // width
        pieces = line_gather(jnp.concatenate(weights, axis=1))
        split = [
            inner_weight[:, i * width : (i + 1) * width] for i in range(self.columns)
        ]
        self.dense_line = line_gather(jnp.concatenate([output_weight, *split]))
        lined = line_order(pieces)
        rows = lined.shape[1]
        lined = lined.reshape(4, rows, 3, -1).transpose(1, 2, 0, 3).reshape(rows, -1)
        ones = plane_gather(lined)
        two = plane_rest(ones)
        self.dense_line = behind(self.dense_line, ones)
        mine = (lined,) + ones + (two,)
        self.packed_pieces = mine + core_gather(mine)
        outer_weight = after(outer_weight, pieces[3])
        self.outer_full = lax.all_gather(outer_weight, ("rows", "heads"), axis=0, tiled=True)

    def project(self, tokens, bias):
        lined = line_order(self.dense_line)
        width = lined.shape[2]
        lined = lined.reshape(4, self.columns + 1, -1, width).transpose(1, 0, 2, 3)
        lined = lined.reshape(-1, width)
        tokens = after(tokens, lined)
        packed, full = project(self.order, tokens, bias.reshape(1, -1), self.packed_pieces)
        ones = behind(plane_gather(lined), (packed,))
        self.dense_mine = (lined,) + ones
        self.dense_depth = lined.shape[0] // (self.columns + 1)
        return after(packed, *ones), full.reshape(-1, full.shape[2])

    def dense_start(self, packed, earlier):
        mine = self.dense_mine
        got = core_gather(mine) + (plane_rest(mine[1:]),)
        got = got if earlier is None else behind(got, (earlier[0],))
        self.dense_got = got
        return after(packed, got[3])

    def dense(self, context):
        got = self.dense_got
        (last,) = behind(core_gather(got[3:]), (context,))
        pieces = self.dense_mine + got[3:] + got[:3] + (last,)
        outer = self.outer_full.reshape(self.columns, -1, self.outer_full.shape[1])
        return load_slots, 8 * (self.columns + 1) + 1, self.order, pieces + (outer,)

    def outer_terms(self, hidden_low, branch_grad):
        send = columns_term(hidden_low, branch_grad, self.away)
        keep = columns_term(after(hidden_low, send), branch_grad, self.keep)
        return keep, self.begin(scatter_steps(send, keep, stack_rows))

    def inner_terms(self, inner_pair, output_pair):
        return rows_terms((inner_pair, output_pair), self.order)

    def inner_steps(self, terms, gate):
        send, keep = terms
        return self.begin(scatter_steps(after(send, gate), keep, stack_rows))

    def inner_cut(self, both):
        cut = self.columns * both.shape[1] // (self.columns + 1)
        return both[:, :cut], both[:, cut:]

    def packed_terms(self, tokens, packed_grad):
        return rows_terms(((tokens, packed_grad),), self.order)

    def packed_steps(self, terms):
        return self.begin(scatter_steps(*terms, stack_columns))

    def begin(self, steps):
        next(steps)
        return steps

    def packed_cut(self, total):
        width = total.shape[1] // 3
        return tuple(total[:, i * width : (i + 1) * width] for i in range(3))

    def behind(self, value, steps, *gates):
        return after(value, steps.send(gates))

    def hold(self, value, gate):
        return after(value, gate)

    def finish(self, steps, *gates):
        return steps.send(gates)

    def last(self, value, steps, small, earlier):
        low = steps.send(())
        totals = total_steps(after(small, low))
        value = value(low)
        done = earlier.send((value,))
        gates = (value,)
        while True:
            beside = next(totals)
            try:
                sent = steps.send((beside,) + gates)
            except StopIteration:
                return value, sent, beside, done
            gates = ()


class PlainMoves:
    def gather(self, weights, *dense):
        full = [
            lax.all_gather(lax.all_gather(w, "rows", axis=0, tiled=True), "heads", axis=1, tiled=True)
            for w in weights
        ]
        self.packed_weight = jnp.concatenate(full, axis=1)
        self.fulls = tuple(
            lax.all_gather(w, ("rows", "heads"), axis=0, tiled=True) for w in dense
        )

    def project(self, tokens, bias):
        packed = (dot_plain(tokens, self.packed_weight) + bias).astype(BF16)
        return packed, self.packed_weight

    def dense_start(self, packed, earlier):
        return packed

    def dense(self, context):
        output, inner, outer = self.fulls
        width = output.shape[1]
        chunks = inner.shape[1] // width
        sources = (
            output.reshape(8, -1, width),
            inner.reshape(8, -1, inner.shape[1]),
            outer.reshape(chunks, -1, width),
        )
        return load_whole, 2 + chunks, jnp.zeros((8,), jnp.int32), sources

    def scatter(self, term):
        return lax.psum_scatter(term, ("rows", "heads"), scatter_dimension=0, tiled=True)

    def outer_terms(self, hidden_low, branch_grad):
        return None, self.scatter(dot_rows(hidden_low, branch_grad))

    def inner_terms(self, inner_pair, output_pair):
        return self.scatter(dot_rows(*inner_pair)), self.scatter(dot_rows(*output_pair))

    def inner_steps(self, terms, gate):
        return terms

    def inner_cut(self, both):
        return both

    def packed_terms(self, tokens, packed_grad):
        term = dot_rows(tokens, packed_grad)
        width = tokens.shape[1]
        parts = [term[:, i * width : (i + 1) * width] for i in range(3)]
        parts = [lax.psum_scatter(p, "heads", scatter_dimension=1, tiled=True) for p in parts]
        return tuple(
            lax.psum_scatter(p, "rows", scatter_dimension=0, tiled=True) for p in parts
        )

    def packed_steps(self, terms):
        return terms

    def packed_cut(self, total):
        return total

    def behind(self, value, steps, *gates):
        return value

    def hold(self, value, gate):
        return value

    def finish(self, steps, *gates):
        return steps

    def last(self, value, steps, small, earlier):
        return value(small), steps, lax.psum(small, ("rows", "heads")), earlier


def head_only(value, which):
    lanes = lax.broadcasted_iota(jnp.int32, value.shape, 1)
    keep = (lanes < HEAD_DIM) if which == 0 else (lanes >= HEAD_DIM)
    return jnp.where(keep, value, jnp.zeros_like(value))


def dot_lanes(left, right):
    return lax.dot_general(left, right, (((1,), (1,)), ((), ())), preferred_element_type=F32)


def dot_rows(left, right):
    return lax.dot_general(left, right, (((0,), (0,)), ((), ())), preferred_element_type=F32)


def dot_plain(left, right):
    return lax.dot_general(left, right, (((1,), (0,)), ((), ())), preferred_element_type=F32)


def forward_span(query_ref, key_ref, value_ref, context_ref, total_ref, start, length):
    span = pl.ds(start, length)
    query = query_ref[span, :] * jnp.asarray(SCALE, BF16)
    key, value = key_ref[span, :], value_ref[span, :]
    flipped = None
    for which in range(2):
        scores = dot_lanes(key, head_only(query, which))
        largest = jnp.max(scores, axis=0, keepdims=True)
        powers = jnp.exp(scores - largest)
        denominator = jnp.sum(powers, axis=0, keepdims=True)
        total_ref[0, 0, which : which + 1, span] = largest + jnp.log(denominator)
        part = dot_rows(head_only(value, which), powers.astype(BF16)) / denominator
        flipped = part if flipped is None else flipped + part
    context_ref[span, :] = flipped.T.astype(BF16)


def backward_span(
    query_ref, key_ref, value_ref, context_ref, grad_ref, total_ref, outs, start, length
):
    query_out, key_out, value_out = outs
    span = pl.ds(start, length)
    query = query_ref[span, :] * jnp.asarray(SCALE, BF16)
    key, value, grad = key_ref[span, :], value_ref[span, :], grad_ref[span, :]
    product = grad.astype(F32) * context_ref[span, :].astype(F32)
    flipped, key_sum, value_sum = None, None, None
    for which in range(2):
        query_one = head_only(query, which)
        grad_one = head_only(grad, which)
        ones = head_only(jnp.ones((8, 2 * HEAD_DIM), F32), which)
        row_dot = lax.dot_general(
            ones,
            product,
            (((1,), (1,)), ((), ())),
            precision=lax.Precision.HIGHEST,
            preferred_element_type=F32,
        )[:1]
        scores = dot_lanes(key, query_one)
        attention = jnp.exp(scores - total_ref[0, 0, which : which + 1, span])
        weight_grad = dot_lanes(value, grad_one)
        score_grad = (attention * (weight_grad - row_dot)).astype(BF16)
        value_part = dot_plain(attention.astype(BF16), grad_one)
        key_part = dot_plain(score_grad, query_one)
        query_part = dot_rows(head_only(key, which), score_grad)
        flipped = query_part if flipped is None else flipped + query_part
        key_sum = key_part if key_sum is None else key_sum + key_part
        value_sum = value_part if value_sum is None else value_sum + value_part
    query_out[span, :] = (flipped.T * SCALE).astype(BF16)
    key_out[span, :] = key_sum.astype(BF16)
    value_out[span, :] = value_sum.astype(BF16)


def by_kind(kind, run):
    @pl.when(kind != 1)
    def _():
        run(0, BLOCK)

    @pl.when(kind == 1)
    def _():
        length = BLOCK // PARTS

        @pl.loop(0, PARTS)
        def _(part):
            run(pl.multiple_of(part * length, length), length)


def forward_kernel(block, kinds, query_ref, key_ref, value_ref, *refs):
    def run(start, length):
        forward_span(query_ref, key_ref, value_ref, *refs[-2:], start, length)

    by_kind(kinds[block], run)


def backward_kernel(block, kinds, *refs):
    def run(start, length):
        backward_span(*refs[:6], refs[-3:], start, length)

    by_kind(kinds[block], run)


def attend(kernel, block, kinds, operands, earlier, outs, cost, name):
    pairs = outs[0].shape[1] // (2 * HEAD_DIM)

    def spec(offset):
        if offset is None:
            return pl.BlockSpec((1, 1, 2, BLOCK), lambda p, *_: (block, p, 0, 0))
        return pl.BlockSpec((BLOCK, 2 * HEAD_DIM), lambda p, *_: (block, p + offset))

    given = () if earlier is None else earlier
    first = 1 + len(operands)
    return pl.pallas_call(
        functools.partial(kernel, block),
        grid_spec=pltpu.PrefetchScalarGridSpec(
            num_scalar_prefetch=1,
            grid=(pairs,),
            in_specs=[spec(offset) for _, offset in operands] + [HBM for _ in given],
            out_specs=[spec(None if len(out.shape) == 4 else 0) for out in outs],
        ),
        out_shape=outs,
        input_output_aliases={first + i: i for i in range(len(given))},
        cost_estimate=cost,
        name=name,
    )(kinds, *[operand for operand, _ in operands], *given)


def attend_forward(block, kinds, packed, earlier):
    tokens, width = packed.shape[0], packed.shape[1] // 3
    pairs = width // (2 * HEAD_DIM)
    outs = (
        jax.ShapeDtypeStruct((tokens, width), BF16),
        jax.ShapeDtypeStruct((tokens // BLOCK, pairs, 2, BLOCK), F32),
    )
    cost = pl.CostEstimate(
        flops=16 * BLOCK * BLOCK * width,
        bytes_accessed=8 * BLOCK * width,
        transcendentals=BLOCK * BLOCK * width // HEAD_DIM,
    )
    operands = [(packed, 0), (packed, pairs), (packed, 2 * pairs)]
    return attend(forward_kernel, block, kinds, operands, earlier, outs, cost, "attend_forward")


def attend_backward(block, kinds, packed, context, context_grad, totals, earlier):
    tokens, width = context.shape
    pairs = width // (2 * HEAD_DIM)
    outs = (jax.ShapeDtypeStruct((tokens, width), BF16),) * 3
    cost = pl.CostEstimate(
        flops=40 * BLOCK * BLOCK * width,
        bytes_accessed=16 * BLOCK * width,
        transcendentals=BLOCK * BLOCK * width // HEAD_DIM,
    )
    operands = [(packed, 0), (packed, pairs), (packed, 2 * pairs), (context, 0)]
    operands += [(context_grad, 0), (totals, None)]
    return attend(backward_kernel, block, kinds, operands, earlier, outs, cost, "attend_backward")


def norm_parts(value):
    average = jnp.mean(value, axis=-1, keepdims=True)
    centred = value - average
    scale = lax.rsqrt(jnp.mean(centred * centred, axis=-1, keepdims=True) + EPSILON)
    return centred * scale, scale


def norm_back(grad, gain, normed, scale):
    inner = grad * gain
    average = jnp.mean(inner, axis=-1, keepdims=True)
    along = jnp.mean(inner * normed, axis=-1, keepdims=True)
    return scale * (inner - average - normed * along)


def row_sum(value):
    return jnp.sum(value, axis=0, keepdims=True)


def dense_kernel(load, kinds, order, context, tokens, cotangent, vectors, *refs):
    count = len(refs) - 14
    sources = refs[:count]
    layer_out, hidden, branch, first_low, inner_grad, attended, first_grad, context_grad, sums = (
        refs[count : count + 9]
    )
    output_full, inner_full, outer_full, slopes, semaphores = refs[count + 9 :]
    step = pl.program_id(0)
    chunks, width = inner_full.shape[0], context.shape[1]

    @pl.when(step == 0)
    def _():
        copy_all(load(order, sources, output_full, inner_full, outer_full), semaphores)
        sums[...] = jnp.zeros_like(sums)

    def vector(row):
        return vectors[pl.ds(row, 1), :]

    def add(row, value):
        sums[pl.ds(row, 1), :] += row_sum(value)

    output_weight = output_full[...].reshape(width, width)
    attended_out = dot_plain(context[...], output_weight) + vector(0)
    first_normed, first_scale = norm_parts(tokens[...].astype(F32) + attended_out)
    first_out = first_normed * vector(1) + vector(2)
    low = first_out.astype(BF16)
    first_low[...] = low
    second = first_out + vector(3)
    for chunk in range(chunks):
        columns = pl.ds(chunk * width, width)
        inner = dot_plain(low, inner_full[chunk].reshape(width, width)) + vector(6 + chunk)
        half = 0.5 * (1.0 + lax.erf(inner * 0.7071067811865476))
        slopes[:, columns] = half + inner * jnp.exp(-0.5 * inner * inner) * 0.3989422804014327
        hidden_low = (inner * half).astype(BF16)
        hidden[:, columns] = hidden_low
        second = second + dot_plain(hidden_low, outer_full[chunk])
    normed, scale = norm_parts(second)
    block = step * context.shape[0] // BLOCK
    valid = jnp.where(kinds[block] != 2, 1.0, 0.0).astype(F32)
    layer_out[...] = ((normed * vector(4) + vector(5)) * valid).astype(BF16)
    out_grad = cotangent[...].astype(F32) * valid
    add(4, out_grad * normed)
    add(5, out_grad)
    second_grad = norm_back(out_grad, vector(4), normed, scale)
    branch_low = second_grad.astype(BF16)
    branch[...] = branch_low
    add(3, branch_low.astype(F32))
    first_out_grad = second_grad
    for chunk in range(chunks):
        columns = pl.ds(chunk * width, width)
        hidden_grad = dot_lanes(branch_low, outer_full[chunk])
        inner_low = (hidden_grad * slopes[:, columns]).astype(BF16)
        inner_grad[:, columns] = inner_low
        add(6 + chunk, inner_low.astype(F32))
        first_out_grad = first_out_grad + dot_lanes(
            inner_low, inner_full[chunk].reshape(width, width)
        )
    add(1, first_out_grad * first_normed)
    add(2, first_out_grad)
    grad = norm_back(first_out_grad, vector(1), first_normed, first_scale)
    first_grad[...] = grad
    attended_low = grad.astype(BF16)
    attended[...] = attended_low
    add(0, attended_low.astype(F32))
    context_grad[...] = dot_lanes(attended_low, output_weight).astype(BF16)


def dense(load, copies, kinds, order, context, tokens, cotangent, vectors, sources):
    count, width = tokens.shape
    chunks = vectors.shape[0] - 6
    tile = 256
    narrow = pl.BlockSpec((tile, width), lambda i, *_: (i, 0))
    wide = pl.BlockSpec((tile, chunks * width), lambda i, *_: (i, 0))
    fixed = pl.BlockSpec(vectors.shape, lambda i, *_: (0, 0))
    low = jax.ShapeDtypeStruct((count, width), BF16)
    low_wide = jax.ShapeDtypeStruct((count, chunks * width), BF16)
    return pl.pallas_call(
        functools.partial(dense_kernel, load),
        grid_spec=pltpu.PrefetchScalarGridSpec(
            num_scalar_prefetch=2,
            grid=(count // tile,),
            in_specs=[narrow, narrow, narrow, fixed] + [HBM] * len(sources),
            out_specs=[narrow, wide, narrow, narrow, wide, narrow, narrow, narrow, fixed],
            scratch_shapes=[
                pltpu.VMEM((8, width // 8, width), BF16),
                pltpu.VMEM((chunks, 8, width // 8, width), BF16),
                pltpu.VMEM((chunks, width, width), BF16),
                pltpu.VMEM((tile, chunks * width), F32),
                pltpu.SemaphoreType.DMA((copies,)),
            ],
        ),
        out_shape=(
            low,
            low_wide,
            low,
            low,
            low_wide,
            low,
            jax.ShapeDtypeStruct((count, width), F32),
            low,
            jax.ShapeDtypeStruct(vectors.shape, F32),
        ),
        compiler_params=WIDE,
        cost_estimate=pl.CostEstimate(
            flops=4 * count * width * width * (1 + 2 * chunks),
            bytes_accessed=2 * count * width * (10 + 2 * chunks),
            transcendentals=2 * count * width * chunks,
        ),
        name="dense",
    )(kinds, order, context, tokens, cotangent, vectors, *sources)


def load_slots(order, sources, output_full, inner_full, outer_full):
    pieces, outer = sources[:8], sources[8]
    depth = output_full.shape[1]
    moves = []
    for slot in range(8):
        moves.append((pieces[slot].at[pl.ds(0, depth)], output_full.at[order[slot]]))
        for chunk in range(inner_full.shape[0]):
            source = pieces[slot].at[pl.ds(depth * (1 + chunk), depth)]
            moves.append((source, inner_full.at[chunk, order[slot]]))
    return moves + [(outer, outer_full)]


def load_whole(order, sources, output_full, inner_full, outer_full):
    output, inner, outer = sources
    width = output.shape[2]
    moves = [(output, output_full), (outer, outer_full)]
    for chunk in range(inner_full.shape[0]):
        moves.append((inner.at[:, :, pl.ds(chunk * width, width)], inner_full.at[chunk]))
    return moves


def shards(
    tokens,
    block_kind,
    query_weight,
    key_weight,
    value_weight,
    query_bias,
    value_bias,
    output_weight,
    output_bias,
    first_gain,
    first_shift,
    inner_weight,
    inner_bias,
    outer_weight,
    outer_bias,
    second_gain,
    second_shift,
    cotangent,
):
    width = tokens.shape[1]
    per_device = block_kind.shape[0] // lax.axis_size("heads")
    kinds = lax.dynamic_slice_in_dim(
        block_kind, lax.axis_index("heads") * per_device, per_device
    )
    singles = (output_bias, first_gain, first_shift, outer_bias, second_gain, second_shift)
    vectors = jnp.concatenate([jnp.stack(singles), inner_bias.reshape(-1, width)]).astype(F32)
    eight_by_four = lax.axis_size("rows") == 8 and lax.axis_size("heads") == 4
    moves = SlotMoves() if eight_by_four else PlainMoves()
    moves.gather(
        (query_weight, key_weight, value_weight), output_weight, inner_weight, outer_weight
    )

    packed_bias = jnp.concatenate([query_bias, jnp.zeros_like(query_bias), value_bias])
    packed, packed_weight = moves.project(tokens, packed_bias.astype(F32))
    earlier = None
    for block in range(per_device):
        if block == per_device - 1:
            packed = moves.dense_start(packed, earlier)
        earlier = attend_forward(block, kinds, packed, earlier)
    context, totals = earlier
    load, copies, order, sources = moves.dense(context)
    (
        layer_out,
        hidden_low,
        branch_grad,
        first_low,
        inner_grad,
        attended_grad,
        first_grad,
        context_grad,
        sums,
    ) = dense(load, copies, kinds, order, context, tokens, cotangent, vectors, sources)

    kernel_done, outer_steps = moves.outer_terms(hidden_low, branch_grad)
    inner_grad = moves.behind(inner_grad, outer_steps, kernel_done)
    inner_terms = moves.inner_terms((first_low, inner_grad), (context, attended_grad))
    context_grad = moves.behind(context_grad, outer_steps, inner_terms[1])
    inner_steps = moves.inner_steps(inner_terms, context_grad)
    pieces = None
    for block in range(per_device):
        if block == per_device - 1:
            context_grad = moves.behind(context_grad, outer_steps, pieces[0])
            context_grad = moves.behind(context_grad, inner_steps, pieces[0])
        pieces = attend_backward(block, kinds, packed, context, context_grad, totals, pieces)
    outer_weight_grad = moves.finish(outer_steps, pieces[0])
    packed_grad = jnp.concatenate(pieces, axis=1)
    packed_grad = moves.behind(packed_grad, inner_steps, pieces[0])
    packed_grad = moves.hold(packed_grad, outer_weight_grad)
    packed_terms = moves.packed_terms(tokens, packed_grad)
    packed_steps = moves.packed_steps(packed_terms)
    inner_ready = moves.behind(packed_terms[1], inner_steps, packed_terms[1])
    bias_sums = jnp.stack([jnp.sum(pieces[i], axis=0, dtype=F32) for i in (0, 2)])

    def tokens_part(gate):
        return first_grad + dot_lanes(after(packed_grad, gate, inner_ready), packed_weight)

    tokens_grad, packed_total, small, inner_both = moves.last(
        tokens_part, packed_steps, jnp.concatenate([sums, bias_sums]), inner_steps
    )
    inner_weight_grad, output_weight_grad = moves.inner_cut(inner_both)
    query_weight_grad, key_weight_grad, value_weight_grad = moves.packed_cut(packed_total)
    rows = sums.shape[0]
    return (
        layer_out,
        tokens_grad,
        query_weight_grad,
        key_weight_grad,
        value_weight_grad,
        small[rows],
        small[rows + 1],
        output_weight_grad,
        small[0],
        small[1],
        small[2],
        inner_weight_grad,
        small[6:rows].reshape(-1),
        outer_weight_grad,
        small[3],
        small[4],
        small[5],
    )


def solution(mesh):
    both = P(("rows", "heads"), None)
    placed = (
        (both, P("rows"))
        + (P("rows", "heads"),) * 3
        + (P(), P(), both, P(), P(), P(), both, P(), both, P(), P(), P(), both)
    )
    given = (
        (both, both)
        + (P("rows", "heads"),) * 3
        + (P(), P(), both, P(), P(), P(), both, P(), both, P(), P(), P())
    )
    return jax.shard_map(
        shards, mesh=mesh, in_specs=placed, out_specs=given, check_vma=False
    )
```

```python
import functools

import jax
import jax.numpy as jnp
from jax import lax
from jax.experimental import pallas as pl
from jax.experimental.pallas import tpu as pltpu
from jax.sharding import PartitionSpec as P

HEAD_DIM = 64
BLOCK = 512
PARTS = 4
EPSILON = 1e-06
SCALE = 0.125
F32 = jnp.float32
BF16 = jnp.bfloat16


def by_core(first, second):
    return jnp.where(lax.axis_index("rows") & 1 == 1, second, first)


SWAPS = {"core": (1, 1), "first": (2, 4), "second": (4, 2)}


def exchange(value, stage):
    bits = SWAPS[stage]
    return lax.ppermute(value, "rows", [(i, i ^ bits[i & 1]) for i in range(8)])


def shift_line(value, step):
    return lax.ppermute(value, "heads", [(i, (i + step) % 4) for i in range(4)])


def slot_orders():
    here = lax.axis_index("rows")
    first, second = by_core(2, 4), by_core(4, 2)
    keep = jnp.stack([here, here ^ first, here ^ second, here ^ 6])
    away = jnp.stack([here, here ^ second, here ^ first, here ^ 6]) ^ 1
    return keep.astype(jnp.int32), away.astype(jnp.int32)


def after(value, *others):
    return lax.optimization_barrier((value,) + others)[0]


def behind(value, gates):
    if not gates:
        return value
    values = value if isinstance(value, tuple) else (value,)
    values = lax.optimization_barrier(values + tuple(gates))[: len(values)]
    return values if isinstance(value, tuple) else values[0]


def line_gather(piece):
    return (piece,) + tuple(shift_line(piece, step) for step in (1, 2, 3))


def line_order(pieces):
    here = lax.axis_index("heads")
    turned = [pieces[-i % 4] for i in range(4)]
    for bit in (1, 2):
        turned = [
            jnp.where(here & bit == bit, turned[i - bit], turned[i]) for i in range(4)
        ]
    return jnp.stack(turned)


def plane_gather(piece):
    return exchange(piece, "first"), exchange(piece, "second")


def plane_rest(ones):
    return exchange(after(*ones), "second")


def core_gather(mine):
    return tuple(exchange(member, "core") for member in mine)


def scatter_steps(send, keep, stack, finish):
    gates = yield send
    got = behind(exchange(send, "core"), gates)
    low = (keep[2:].astype(F32) + got[2:].astype(F32)).astype(BF16)
    gates = yield low
    got_two = behind(exchange(low, "second"), gates)
    one = (keep[1].astype(F32) + got[1].astype(F32) + got_two[1].astype(F32)).astype(BF16)
    gates = yield one
    got_one = behind(exchange(one, "first"), gates).astype(F32)
    zero = keep[0].astype(F32) + got[0].astype(F32) + got_two[0].astype(F32)
    stacked = stack((zero + got_one).astype(BF16))
    here = lax.axis_index("heads")
    sent = [
        lax.dynamic_index_in_dim(stacked, (here + step) % 4, keepdims=False)
        for step in range(4)
    ]
    gates = yield sent[2]
    (two,) = behind((shift_line(sent[2], 2),), gates)
    gates = yield two
    one, three = behind((shift_line(sent[1], 1), shift_line(sent[3], 3)), gates)
    yield finish(sent[0], one, two, three)


def add_pieces(*pieces):
    return sum(piece.astype(F32) for piece in pieces)


def stack_rows(part):
    return part.reshape(4, -1, part.shape[1])


def stack_columns(part):
    width = part.shape[1] // 12
    columns = part[:-8].reshape(-1, 3, 4, width).transpose(2, 0, 1, 3)
    columns = columns.reshape(4, -1, 3 * width)
    rows = [part[-8:, i * 3 * width : (i + 1) * 3 * width] for i in range(4)]
    rows = jnp.broadcast_to(jnp.concatenate(rows), (4, 32, 3 * width))
    return jnp.concatenate([columns, rows], axis=1)


HBM = pl.BlockSpec(memory_space=pl.ANY)
WIDE = pltpu.CompilerParams(vmem_limit_bytes=58 << 20)


def copy_all(moves, semaphores):
    copies = [
        pltpu.make_async_copy(source, target, semaphores.at[i])
        for i, (source, target) in enumerate(moves)
    ]
    for copy in copies:
        copy.start()
    for copy in copies:
        copy.wait()


VMEM = pl.BlockSpec(memory_space=pltpu.VMEM)


def small_call(kernel, outs, name, *operands):
    return pl.pallas_call(
        kernel,
        in_specs=[VMEM for _ in operands],
        out_specs=[VMEM for _ in outs],
        out_shape=[jax.ShapeDtypeStruct(shape, dtype) for shape, dtype in outs],
        name=name,
    )(*operands)


def pack_kernel(*refs):
    refs[3][...] = jnp.concatenate([ref[...] for ref in refs[:3]], axis=1)


def pack(weights):
    depth, width = weights[0].shape
    return small_call(pack_kernel, [((depth, 3 * width), BF16)], "pack", *weights)[0]


def order_kernel(*refs):
    pieces, out = refs[:4], refs[4]
    here = lax.axis_index("heads")
    width = out.shape[1] // 12
    columns = []
    for head in range(4):
        value = pieces[0][...]
        for step in (1, 2, 3):
            value = jnp.where((here - head) % 4 == step, pieces[step][...], value)
        columns.append(value)
    for part in range(3):
        cut = slice(part * width, (part + 1) * width)
        out[:, part * 4 * width : (part + 1) * 4 * width] = jnp.concatenate(
            [value[:, cut] for value in columns], axis=1
        )


def order_columns(pieces):
    depth, width = pieces[0].shape
    return small_call(order_kernel, [((depth, 4 * width), BF16)], "order", *pieces)[0]


def split_kernel(*refs):
    total = sum(ref[...].astype(F32) for ref in refs[:4])
    depth, width = refs[4].shape
    for part in range(3):
        refs[4 + part][...] = total[:depth, part * width : (part + 1) * width]
    refs[7][...] = total[depth:]


def split_pieces(*pieces):
    rows, width = pieces[0].shape
    outs = [((rows - 32, width // 3), F32)] * 3 + [((32, width), F32)]
    return small_call(split_kernel, outs, "split", *pieces)


def project_kernel(order, tokens, bias, *refs):
    pieces, (packed, full, semaphores) = refs[:8], refs[8:]

    @pl.when(pl.program_id(0) == 0)
    def _():
        copy_all([(pieces[i], full.at[order[i]]) for i in range(8)], semaphores)

    weight = full[...].reshape(-1, full.shape[2])
    packed[...] = (dot_plain(tokens[...], weight) + bias[...]).astype(BF16)


def project(order, tokens, bias, pieces):
    count, width = tokens.shape
    depth, columns = pieces[0].shape
    tile = count // 2
    return pl.pallas_call(
        project_kernel,
        grid_spec=pltpu.PrefetchScalarGridSpec(
            num_scalar_prefetch=1,
            grid=(2,),
            in_specs=[
                pl.BlockSpec((tile, width), lambda i, *_: (i, 0)),
                pl.BlockSpec((1, columns), lambda i, *_: (0, 0)),
            ]
            + [HBM] * 8,
            out_specs=[
                pl.BlockSpec((tile, columns), lambda i, *_: (i, 0)),
                pl.BlockSpec((8, depth, columns), lambda i, *_: (0, 0, 0)),
            ],
            scratch_shapes=[pltpu.SemaphoreType.DMA((8,))],
        ),
        out_shape=(
            jax.ShapeDtypeStruct((count, columns), BF16),
            jax.ShapeDtypeStruct((8, depth, columns), BF16),
        ),
        compiler_params=WIDE,
        cost_estimate=pl.CostEstimate(
            flops=2 * count * width * columns,
            bytes_accessed=2 * (count * (width + columns) + 2 * width * columns),
            transcendentals=0,
        ),
        name="project",
    )(order, tokens, bias, *pieces)


def rows_terms_kernel(counts, extra, order, *refs):
    parts = len(counts)
    lefts, rights = refs[:parts], refs[parts : 2 * parts]
    send_ref, keep_ref, turned, product = refs[-4:]
    step = pl.program_id(0)
    width = product.shape[0]
    depth = width // 8
    begin = 0
    for left, right, steps in zip(lefts, rights, counts):

        @pl.when(step == begin)
        def _(left=left):
            turned[...] = left[...].T

        @pl.when((step >= begin) & (step < begin + steps))
        def _(right=right):
            product[...] = dot_plain(turned[...], right[...].reshape(right.shape[-2:]))

        begin += steps
    if extra:
        value = rights[0][...].reshape(rights[0].shape[-2:]).astype(F32)
        rows = lax.broadcasted_iota(jnp.int32, (8, width), 0)
        added = jnp.where(rows == 4, row_sum(value), refs[2 * parts][...]).astype(BF16)
    for slot in range(4):
        for out, place in ((send_ref, 4 + slot), (keep_ref, slot)):
            start = pl.multiple_of(order[place] * depth, depth)
            out[slot, :depth, :] = product[pl.ds(start, depth), :].astype(BF16)
            if extra:
                out[slot, depth:, :] = added


def rows_terms(pairs, order, extra=None):
    tokens, width = pairs[0][0].shape
    counts = [right.size // (tokens * width) for _, right in pairs]
    total = sum(counts)
    begins = [sum(counts[:i]) for i in range(len(counts))]
    depth = width // 8 + (0 if extra is None else 8)

    def right_spec(right, begin, count):
        def at(i):
            return jnp.clip(i - begin, 0, count - 1)

        if len(right.shape) == 3:
            return pl.BlockSpec((1, tokens, width), lambda i, *_: (at(i), 0, 0))
        return pl.BlockSpec((tokens, width), lambda i, *_: (0, at(i)))

    whole = pl.BlockSpec((tokens, width), lambda i, *_: (0, 0))
    slots = pl.BlockSpec((4, depth, width), lambda i, *_: (0, 0, i))
    specs = [right_spec(right, b, c) for (_, right), b, c in zip(pairs, begins, counts)]
    operands = [left for left, _ in pairs] + [right for _, right in pairs]
    if extra is not None:
        specs.append(pl.BlockSpec((8, width), lambda i, *_: (0, i)))
        operands.append(extra)
    return pl.pallas_call(
        functools.partial(rows_terms_kernel, counts, extra is not None),
        grid_spec=pltpu.PrefetchScalarGridSpec(
            num_scalar_prefetch=1,
            grid=(total,),
            in_specs=[whole for _ in pairs] + specs,
            out_specs=[slots, slots],
            scratch_shapes=[pltpu.VMEM((width, tokens), BF16), pltpu.VMEM((width, width), F32)],
        ),
        out_shape=(jax.ShapeDtypeStruct((4, depth, total * width), BF16),) * 2,
        compiler_params=pltpu.CompilerParams(vmem_limit_bytes=40 << 20),
        cost_estimate=pl.CostEstimate(
            flops=2 * tokens * width * width * total,
            bytes_accessed=2 * (tokens + width) * width * total,
            transcendentals=0,
        ),
        name="rows_terms",
    )(order, *operands)


def columns_term_kernel(order, left, right, out):
    out[0] = dot_rows(left[...], right[...]).astype(BF16)


def columns_term(left, right, order):
    tokens, width = right.shape
    depth = left.shape[1] // 8
    return pl.pallas_call(
        columns_term_kernel,
        grid_spec=pltpu.PrefetchScalarGridSpec(
            num_scalar_prefetch=1,
            grid=(4,),
            in_specs=[
                pl.BlockSpec((tokens, depth), lambda i, order: (0, order[i])),
                pl.BlockSpec((tokens, width), lambda i, order: (0, 0)),
            ],
            out_specs=pl.BlockSpec((1, depth, width), lambda i, order: (i, 0, 0)),
        ),
        out_shape=jax.ShapeDtypeStruct((4, depth, width), BF16),
        compiler_params=pltpu.CompilerParams(vmem_limit_bytes=32 << 20),
        cost_estimate=pl.CostEstimate(
            flops=2 * tokens * width * depth * 4,
            bytes_accessed=2 * (tokens * depth * 4 + tokens * width + depth * width * 4),
            transcendentals=0,
        ),
        name="columns_term",
    )(order, left, right)


class SlotMoves:
    def __init__(self):
        self.keep, self.away = slot_orders()
        self.order = jnp.concatenate([self.keep, self.away])

    def gather(self, weights, output_weight, inner_weight, outer_weight):
        depth, width = output_weight.shape
        self.columns = inner_weight.shape[1] // width
        pieces = line_gather(pack(weights))
        split = [
            inner_weight[:, i * width : (i + 1) * width] for i in range(self.columns)
        ]
        self.dense_line = line_gather(jnp.concatenate([output_weight, *split]))
        lined = order_columns(pieces)
        ones = plane_gather(lined)
        two = plane_rest(ones)
        self.dense_line = behind(self.dense_line, ones)
        mine = (lined,) + ones + (two,)
        self.packed_pieces = mine + core_gather(mine)
        outer_weight = after(outer_weight, pieces[3])
        self.outer_full = lax.all_gather(outer_weight, ("rows", "heads"), axis=0, tiled=True)

    def project(self, tokens, bias):
        lined = line_order(self.dense_line)
        width = lined.shape[2]
        lined = lined.reshape(4, self.columns + 1, -1, width).transpose(1, 0, 2, 3)
        lined = lined.reshape(-1, width)
        tokens = after(tokens, lined)
        packed, full = project(self.order, tokens, bias.reshape(1, -1), self.packed_pieces)
        ones = behind(plane_gather(lined), (packed,))
        self.dense_mine = (lined,) + ones
        self.dense_depth = lined.shape[0] // (self.columns + 1)
        return after(packed, *ones), full.reshape(-1, full.shape[2])

    def dense_start(self, packed, earlier):
        mine = self.dense_mine
        got = core_gather(mine) + (plane_rest(mine[1:]),)
        got = got if earlier is None else behind(got, (earlier[0],))
        self.dense_got = got
        return after(packed, got[3])

    def dense(self, context):
        got = self.dense_got
        (last,) = behind(core_gather(got[3:]), (context,))
        pieces = self.dense_mine + got[3:] + got[:3] + (last,)
        outer = self.outer_full.reshape(self.columns, -1, self.outer_full.shape[1])
        return load_slots, 8 * (self.columns + 1) + 1, self.order, pieces + (outer,)

    def outer_terms(self, hidden_low, branch_grad):
        send = columns_term(hidden_low, branch_grad, self.away)
        keep = columns_term(after(hidden_low, send), branch_grad, self.keep)
        return keep, self.begin(scatter_steps(send, keep, stack_rows, add_pieces))

    def inner_terms(self, inner_pair, output_pair):
        return rows_terms((inner_pair, output_pair), self.order)

    def inner_steps(self, terms, gate):
        send, keep = terms
        return self.begin(scatter_steps(after(send, gate), keep, stack_rows, add_pieces))

    def inner_cut(self, both):
        cut = self.columns * both.shape[1] // (self.columns + 1)
        return both[:, :cut], both[:, cut:]

    def packed_terms(self, tokens, packed_grad, sums):
        width = tokens.shape[1]
        extra = jnp.concatenate([sums, jnp.zeros((24 - sums.shape[0], width), F32)])
        extra = extra.reshape(8, 3, width).reshape(8, 3 * width)
        return rows_terms(((tokens, packed_grad),), self.order, extra)

    def begin(self, steps):
        next(steps)
        return steps

    def hold(self, value, gate):
        return after(value, gate)

    def behind(self, value, steps, *gates):
        return after(value, steps.send(gates))

    def finish(self, steps, *gates):
        return steps.send(gates)

    def last(self, value, terms, earlier):
        steps = self.begin(scatter_steps(*terms, stack_columns, split_pieces))
        two = earlier.send((terms[1],))
        value = value((steps.send(()), two))
        done = earlier.send((value,))
        steps.send((value, done))
        for _ in range(2):
            steps.send(())
        *weights, total = steps.send(())
        rows = jnp.concatenate([total[i : i + 8] for i in (0, 8, 16, 24)], axis=1)
        rows = rows.reshape(24, -1)
        return value, weights, rows, rows[12], rows[14], done


class PlainMoves:
    def gather(self, weights, *dense):
        full = [
            lax.all_gather(lax.all_gather(w, "rows", axis=0, tiled=True), "heads", axis=1, tiled=True)
            for w in weights
        ]
        self.packed_weight = jnp.concatenate(full, axis=1)
        self.fulls = tuple(
            lax.all_gather(w, ("rows", "heads"), axis=0, tiled=True) for w in dense
        )

    def project(self, tokens, bias):
        packed = (dot_plain(tokens, self.packed_weight) + bias).astype(BF16)
        return packed, self.packed_weight

    def dense_start(self, packed, earlier):
        return packed

    def dense(self, context):
        output, inner, outer = self.fulls
        width = output.shape[1]
        chunks = inner.shape[1] // width
        sources = (
            output.reshape(8, -1, width),
            inner.reshape(8, -1, inner.shape[1]),
            outer.reshape(chunks, -1, width),
        )
        return load_whole, 2 + chunks, jnp.zeros((8,), jnp.int32), sources

    def scatter(self, term):
        return lax.psum_scatter(term, ("rows", "heads"), scatter_dimension=0, tiled=True)

    def outer_terms(self, hidden_low, branch_grad):
        return None, self.scatter(dot_rows(hidden_low, branch_grad))

    def inner_terms(self, inner_pair, output_pair):
        return self.scatter(dot_rows(*inner_pair)), self.scatter(dot_rows(*output_pair))

    def inner_steps(self, terms, gate):
        return terms

    def inner_cut(self, both):
        return both

    def packed_terms(self, tokens, packed_grad, sums):
        parts = [dot_rows(tokens, packed_grad[i]) for i in range(3)]
        parts = [lax.psum_scatter(p, "heads", scatter_dimension=1, tiled=True) for p in parts]
        weights = [lax.psum_scatter(p, "rows", scatter_dimension=0, tiled=True) for p in parts]
        biases = [jnp.sum(packed_grad[i], axis=0, dtype=F32) for i in (0, 2)]
        return weights, lax.psum((sums, *biases), ("rows", "heads"))

    def hold(self, value, gate):
        return value

    def behind(self, value, steps, *gates):
        return value

    def finish(self, steps, *gates):
        return steps

    def last(self, value, terms, earlier):
        weights, sums = terms
        return value(sums[:1]), weights, *sums, earlier


def head_only(value, which):
    lanes = lax.broadcasted_iota(jnp.int32, value.shape, 1)
    keep = (lanes < HEAD_DIM) if which == 0 else (lanes >= HEAD_DIM)
    return jnp.where(keep, value, jnp.zeros_like(value))


def dot_lanes(left, right):
    return lax.dot_general(left, right, (((1,), (1,)), ((), ())), preferred_element_type=F32)


def dot_rows(left, right):
    return lax.dot_general(left, right, (((0,), (0,)), ((), ())), preferred_element_type=F32)


def dot_plain(left, right):
    return lax.dot_general(left, right, (((1,), (0,)), ((), ())), preferred_element_type=F32)


def spans(parts):
    length = BLOCK // parts
    return [slice(i * length, (i + 1) * length) for i in range(parts)]


def by_part(product, left, right, parts, axis):
    return jnp.concatenate([product(left[at], right[at]) for at in spans(parts)], axis=axis)


def forward_pair(parts, query_ref, key_ref, value_ref, context_ref, total_ref, pair):
    lanes = pl.ds(pl.multiple_of(pair * 2 * HEAD_DIM, 2 * HEAD_DIM), 2 * HEAD_DIM)
    query = query_ref[:, lanes] * jnp.asarray(SCALE, BF16)
    key, value = key_ref[:, lanes], value_ref[:, lanes]
    flipped = None
    for which in range(2):
        scores = by_part(dot_lanes, key, head_only(query, which), parts, 1)
        largest = jnp.max(scores, axis=0, keepdims=True)
        powers = jnp.exp(scores - largest)
        denominator = jnp.sum(powers, axis=0, keepdims=True)
        total_ref[0, pair, which : which + 1, :] = largest + jnp.log(denominator)
        low, values = powers.astype(BF16), head_only(value, which)
        context = [dot_rows(values[at], low[:, at]) for at in spans(parts)]
        context = jnp.concatenate(context, axis=1) / denominator
        flipped = context if flipped is None else flipped + context
    context_ref[:, lanes] = flipped.T.astype(BF16)


def backward_pair(
    parts, query_ref, key_ref, value_ref, context_ref, grad_ref, total_ref, outs, pair
):
    lanes = pl.ds(pl.multiple_of(pair * 2 * HEAD_DIM, 2 * HEAD_DIM), 2 * HEAD_DIM)
    query = query_ref[:, lanes] * jnp.asarray(SCALE, BF16)
    key, value, grad = key_ref[:, lanes], value_ref[:, lanes], grad_ref[:, lanes]
    product = grad.astype(F32) * context_ref[:, lanes].astype(F32)
    flipped, key_sum, value_sum = None, None, None
    for which in range(2):
        query_one = head_only(query, which)
        grad_one = head_only(grad, which)
        ones = head_only(jnp.ones((8, 2 * HEAD_DIM), F32), which)
        row_dot = lax.dot_general(
            ones,
            product,
            (((1,), (1,)), ((), ())),
            precision=lax.Precision.HIGHEST,
            preferred_element_type=F32,
        )[:1]
        scores = by_part(dot_lanes, key, query_one, parts, 1)
        attention = jnp.exp(scores - total_ref[0, pair, which : which + 1, :])
        weight_grad = by_part(dot_lanes, value, grad_one, parts, 1)
        score_grad = (attention * (weight_grad - row_dot)).astype(BF16)
        low, keys = attention.astype(BF16), head_only(key, which)
        at_parts = spans(parts)
        value_part = [dot_plain(low[:, at], grad_one[at]) for at in at_parts]
        key_part = [dot_plain(score_grad[:, at], query_one[at]) for at in at_parts]
        query_part = [dot_rows(keys[at], score_grad[:, at]) for at in at_parts]
        value_part = jnp.concatenate(value_part, axis=0)
        key_part = jnp.concatenate(key_part, axis=0)
        query_part = jnp.concatenate(query_part, axis=1)
        flipped = query_part if flipped is None else flipped + query_part
        key_sum = key_part if key_sum is None else key_sum + key_part
        value_sum = value_part if value_sum is None else value_sum + value_part
    outs[0, :, lanes] = (flipped.T * SCALE).astype(BF16)
    outs[1, :, lanes] = key_sum.astype(BF16)
    outs[2, :, lanes] = value_sum.astype(BF16)


def by_kind(kind, pairs, run):
    for mine, parts in ((kind != 1, 1), (kind == 1, PARTS)):

        @pl.when(mine)
        def _(parts=parts):
            @pl.loop(0, pairs)
            def _(pair):
                run(parts, pair)


def forward_kernel(block, kinds, *refs):
    refs = refs[:3] + refs[-2:]
    by_kind(
        kinds[block(pl.program_id(0))],
        refs[4].shape[1],
        lambda parts, pair: forward_pair(parts, *refs, pair),
    )


def backward_kernel(block, kinds, *refs):
    refs = refs[:6] + refs[-1:]
    by_kind(
        kinds[block(pl.program_id(0))],
        refs[5].shape[1],
        lambda parts, pair: backward_pair(parts, *refs, pair),
    )


def attend(kernel, units, kinds, operands, earlier, outs, name):
    begin, end = units
    width = outs[0].shape[-1] // 2
    pairs = width // (2 * HEAD_DIM)

    def block(step):
        return (step + begin) // 2

    def half(step):
        return (step + begin) % 2

    narrow = (BLOCK, width)

    def spec(offset):
        return pl.BlockSpec(narrow, lambda i, *_: (block(i), half(i) + 2 * offset))

    totals = pl.BlockSpec((1, pairs, 2, BLOCK), lambda i, *_: (block(i), half(i), 0, 0))
    kinds_of = {
        2: spec(0),
        3: pl.BlockSpec((3,) + narrow, lambda i, *_: (0, block(i), half(i))),
        4: totals,
    }
    given = () if earlier is None else earlier
    first = 1 + len(operands)
    count = end - begin
    products = 4 if name == "attend_forward" else 10
    return pl.pallas_call(
        functools.partial(kernel, block),
        grid_spec=pltpu.PrefetchScalarGridSpec(
            num_scalar_prefetch=1,
            grid=(count,),
            in_specs=[totals if offset is None else spec(offset) for _, offset in operands]
            + [HBM for _ in given],
            out_specs=[kinds_of[len(out.shape)] for out in outs],
        ),
        out_shape=outs,
        input_output_aliases={first + i: i for i in range(len(given))},
        compiler_params=WIDE,
        cost_estimate=pl.CostEstimate(
            flops=products * count * BLOCK * BLOCK * width,
            bytes_accessed=products * count * BLOCK * width,
            transcendentals=count * BLOCK * BLOCK * width // HEAD_DIM,
        ),
        name=name,
    )(kinds, *[operand for operand, _ in operands], *given)


def attend_forward(units, kinds, packed, earlier):
    tokens, width = packed.shape[0], packed.shape[1] // 3
    pairs = width // (2 * HEAD_DIM)
    outs = (
        jax.ShapeDtypeStruct((tokens, width), BF16),
        jax.ShapeDtypeStruct((tokens // BLOCK, pairs, 2, BLOCK), F32),
    )
    operands = [(packed, 0), (packed, 1), (packed, 2)]
    return attend(forward_kernel, units, kinds, operands, earlier, outs, "attend_forward")


def attend_backward(units, kinds, packed, context, context_grad, totals, earlier):
    outs = (jax.ShapeDtypeStruct((3,) + context.shape, BF16),)
    operands = [(packed, 0), (packed, 1), (packed, 2), (context, 0)]
    operands += [(context_grad, 0), (totals, None)]
    return attend(backward_kernel, units, kinds, operands, earlier, outs, "attend_backward")


def tokens_kernel(first_grad, packed_grad, weight, out):
    width = out.shape[1]
    total = first_grad[...]
    for part in range(3):
        columns = weight[:, part * width : (part + 1) * width]
        total = total + dot_lanes(packed_grad[part], columns)
    out[...] = total


def tokens_gradient(first_grad, packed_grad, weight):
    count, width = first_grad.shape
    tile = count // 2
    rows = pl.BlockSpec((tile, width), lambda i: (i, 0))
    return pl.pallas_call(
        tokens_kernel,
        grid=(2,),
        in_specs=[
            rows,
            pl.BlockSpec((3, tile, width), lambda i: (0, i, 0)),
            pl.BlockSpec(weight.shape, lambda i: (0, 0)),
        ],
        out_specs=rows,
        out_shape=jax.ShapeDtypeStruct((count, width), F32),
        compiler_params=WIDE,
        cost_estimate=pl.CostEstimate(
            flops=6 * count * width * width,
            bytes_accessed=14 * count * width + 6 * width * width,
            transcendentals=0,
        ),
        name="tokens_gradient",
    )(first_grad, packed_grad, weight)


def norm_parts(value):
    average = jnp.mean(value, axis=-1, keepdims=True)
    centred = value - average
    scale = lax.rsqrt(jnp.mean(centred * centred, axis=-1, keepdims=True) + EPSILON)
    return centred * scale, scale


def norm_back(grad, gain, normed, scale):
    inner = grad * gain
    average = jnp.mean(inner, axis=-1, keepdims=True)
    along = jnp.mean(inner * normed, axis=-1, keepdims=True)
    return scale * (inner - average - normed * along)


def row_sum(value):
    return jnp.sum(value, axis=0, keepdims=True)


def dense_kernel(load, kinds, order, context, tokens, cotangent, vectors, *refs):
    count = len(refs) - 14
    sources = refs[:count]
    layer_out, hidden, branch, first_low, inner_grad, attended, first_grad, context_grad, sums = (
        refs[count : count + 9]
    )
    output_full, inner_full, outer_full, slopes, semaphores = refs[count + 9 :]
    step = pl.program_id(0)
    chunks, width = inner_full.shape[0], context.shape[1]

    @pl.when(step == 0)
    def _():
        copy_all(load(order, sources, output_full, inner_full, outer_full), semaphores)
        sums[...] = jnp.zeros_like(sums)

    def vector(row):
        return vectors[pl.ds(row, 1), :]

    def add(row, value):
        sums[pl.ds(row, 1), :] += row_sum(value)

    output_weight = output_full[...].reshape(width, width)
    attended_out = dot_plain(context[...], output_weight) + vector(0)
    first_normed, first_scale = norm_parts(tokens[...].astype(F32) + attended_out)
    first_out = first_normed * vector(1) + vector(2)
    low = first_out.astype(BF16)
    first_low[...] = low
    second = first_out + vector(3)
    for chunk in range(chunks):
        columns = pl.ds(chunk * width, width)
        inner = dot_plain(low, inner_full[chunk].reshape(width, width)) + vector(6 + chunk)
        half = 0.5 * (1.0 + lax.erf(inner * 0.7071067811865476))
        slopes[:, columns] = half + inner * jnp.exp(-0.5 * inner * inner) * 0.3989422804014327
        hidden_low = (inner * half).astype(BF16)
        hidden[:, columns] = hidden_low
        second = second + dot_plain(hidden_low, outer_full[chunk])
    normed, scale = norm_parts(second)
    block = step * context.shape[0] // BLOCK
    valid = jnp.where(kinds[block] != 2, 1.0, 0.0).astype(F32)
    layer_out[...] = ((normed * vector(4) + vector(5)) * valid).astype(BF16)
    out_grad = cotangent[...].astype(F32) * valid
    add(4, out_grad * normed)
    add(5, out_grad)
    second_grad = norm_back(out_grad, vector(4), normed, scale)
    branch_low = second_grad.astype(BF16)
    branch[...] = branch_low
    add(3, branch_low.astype(F32))
    first_out_grad = second_grad
    for chunk in range(chunks):
        columns = pl.ds(chunk * width, width)
        hidden_grad = dot_lanes(branch_low, outer_full[chunk])
        inner_low = (hidden_grad * slopes[:, columns]).astype(BF16)
        inner_grad[:, columns] = inner_low
        add(6 + chunk, inner_low.astype(F32))
        first_out_grad = first_out_grad + dot_lanes(
            inner_low, inner_full[chunk].reshape(width, width)
        )
    add(1, first_out_grad * first_normed)
    add(2, first_out_grad)
    grad = norm_back(first_out_grad, vector(1), first_normed, first_scale)
    first_grad[...] = grad
    attended_low = grad.astype(BF16)
    attended[...] = attended_low
    add(0, attended_low.astype(F32))
    context_grad[...] = dot_lanes(attended_low, output_weight).astype(BF16)


def dense(load, copies, kinds, order, context, tokens, cotangent, vectors, sources):
    count, width = tokens.shape
    chunks = vectors.shape[0] - 6
    tile = BLOCK
    narrow = pl.BlockSpec((tile, width), lambda i, *_: (i, 0))
    wide = pl.BlockSpec((tile, chunks * width), lambda i, *_: (i, 0))
    fixed = pl.BlockSpec(vectors.shape, lambda i, *_: (0, 0))
    low = jax.ShapeDtypeStruct((count, width), BF16)
    low_wide = jax.ShapeDtypeStruct((count, chunks * width), BF16)
    return pl.pallas_call(
        functools.partial(dense_kernel, load),
        grid_spec=pltpu.PrefetchScalarGridSpec(
            num_scalar_prefetch=2,
            grid=(count // tile,),
            in_specs=[narrow, narrow, narrow, fixed] + [HBM] * len(sources),
            out_specs=[narrow, wide, narrow, narrow, wide, narrow, narrow, narrow, fixed],
            scratch_shapes=[
                pltpu.VMEM((8, width // 8, width), BF16),
                pltpu.VMEM((chunks, 8, width // 8, width), BF16),
                pltpu.VMEM((chunks, width, width), BF16),
                pltpu.VMEM((tile, chunks * width), F32),
                pltpu.SemaphoreType.DMA((copies,)),
            ],
        ),
        out_shape=(
            low,
            low_wide,
            low,
            low,
            low_wide,
            low,
            jax.ShapeDtypeStruct((count, width), F32),
            low,
            jax.ShapeDtypeStruct(vectors.shape, F32),
        ),
        compiler_params=WIDE,
        cost_estimate=pl.CostEstimate(
            flops=4 * count * width * width * (1 + 2 * chunks),
            bytes_accessed=2 * count * width * (10 + 2 * chunks),
            transcendentals=2 * count * width * chunks,
        ),
        name="dense",
    )(kinds, order, context, tokens, cotangent, vectors, *sources)


def load_slots(order, sources, output_full, inner_full, outer_full):
    pieces, outer = sources[:8], sources[8]
    depth = output_full.shape[1]
    moves = []
    for slot in range(8):
        moves.append((pieces[slot].at[pl.ds(0, depth)], output_full.at[order[slot]]))
        for chunk in range(inner_full.shape[0]):
            source = pieces[slot].at[pl.ds(depth * (1 + chunk), depth)]
            moves.append((source, inner_full.at[chunk, order[slot]]))
    return moves + [(outer, outer_full)]


def load_whole(order, sources, output_full, inner_full, outer_full):
    output, inner, outer = sources
    width = output.shape[2]
    moves = [(output, output_full), (outer, outer_full)]
    for chunk in range(inner_full.shape[0]):
        moves.append((inner.at[:, :, pl.ds(chunk * width, width)], inner_full.at[chunk]))
    return moves


def shards(
    tokens,
    block_kind,
    query_weight,
    key_weight,
    value_weight,
    query_bias,
    value_bias,
    output_weight,
    output_bias,
    first_gain,
    first_shift,
    inner_weight,
    inner_bias,
    outer_weight,
    outer_bias,
    second_gain,
    second_shift,
    cotangent,
):
    width = tokens.shape[1]
    per_device = block_kind.shape[0] // lax.axis_size("heads")
    kinds = lax.dynamic_slice_in_dim(
        block_kind, lax.axis_index("heads") * per_device, per_device
    )
    singles = (output_bias, first_gain, first_shift, outer_bias, second_gain, second_shift)
    vectors = jnp.concatenate([jnp.stack(singles), inner_bias.reshape(-1, width)]).astype(F32)
    eight_by_four = lax.axis_size("rows") == 8 and lax.axis_size("heads") == 4
    moves = SlotMoves() if eight_by_four else PlainMoves()
    moves.gather(
        (query_weight, key_weight, value_weight), output_weight, inner_weight, outer_weight
    )

    packed_bias = jnp.concatenate([query_bias, jnp.zeros_like(query_bias), value_bias])
    packed, packed_weight = moves.project(tokens, packed_bias.astype(F32))
    units = 2 * per_device
    earlier = attend_forward((0, units // 2), kinds, packed, None)
    packed_late = moves.dense_start(packed, earlier)
    context, totals = attend_forward((units // 2, units), kinds, packed_late, earlier)
    load, copies, order, sources = moves.dense(context)
    (
        layer_out,
        hidden_low,
        branch_grad,
        first_low,
        inner_grad,
        attended_grad,
        first_grad,
        context_grad,
        sums,
    ) = dense(load, copies, kinds, order, context, tokens, cotangent, vectors, sources)

    kernel_done, outer_steps = moves.outer_terms(hidden_low, branch_grad)
    inner_grad = moves.behind(inner_grad, outer_steps, kernel_done)
    inner_terms = moves.inner_terms((first_low, inner_grad), (context, attended_grad))
    context_grad = moves.behind(context_grad, outer_steps, inner_terms[1])
    inner_steps = moves.inner_steps(inner_terms, context_grad)
    cuts = (0, units // 4, units - units // 4, units)
    grads = None
    for begin, end in zip(cuts, cuts[1:]):
        if begin == cuts[1]:
            context_grad = moves.behind(context_grad, outer_steps, grads[0])
            context_grad = moves.behind(context_grad, inner_steps, grads[0], context_grad)
        if begin == cuts[2]:
            moves.finish(outer_steps, grads[0])
            outer_weight_grad = moves.finish(outer_steps, grads[0])
            context_grad = moves.hold(context_grad, outer_weight_grad)
            context_grad = moves.behind(context_grad, inner_steps, grads[0], context_grad)
        grads = attend_backward(
            (begin, end), kinds, packed, context, context_grad, totals, grads
        )
    (packed_grad,) = grads
    packed_grad = moves.behind(packed_grad, inner_steps, packed_grad)
    packed_terms = moves.packed_terms(tokens, packed_grad, sums)

    def tokens_part(gate):
        return tokens_gradient(first_grad, after(packed_grad, *gate), packed_weight)

    tokens_grad, weight_grads, small, query_sums, value_sums, inner_both = moves.last(
        tokens_part, packed_terms, inner_steps
    )
    inner_weight_grad, output_weight_grad = moves.inner_cut(inner_both)
    return (
        layer_out,
        tokens_grad,
        *weight_grads,
        query_sums,
        value_sums,
        output_weight_grad,
        small[0],
        small[1],
        small[2],
        inner_weight_grad,
        small[6 : sums.shape[0]].reshape(-1),
        outer_weight_grad,
        small[3],
        small[4],
        small[5],
    )


def solution(mesh):
    both = P(("rows", "heads"), None)
    placed = (
        (both, P("rows"))
        + (P("rows", "heads"),) * 3
        + (P(), P(), both, P(), P(), P(), both, P(), both, P(), P(), P(), both)
    )
    given = (
        (both, both)
        + (P("rows", "heads"),) * 3
        + (P(), P(), both, P(), P(), P(), both, P(), both, P(), P(), P())
    )
    return jax.shard_map(
        shards, mesh=mesh, in_specs=placed, out_specs=given, check_vma=False
    )
```

```python
import functools

import jax
import jax.numpy as jnp
from jax import lax
from jax.experimental import pallas as pl
from jax.experimental.pallas import tpu as pltpu
from jax.sharding import PartitionSpec as P

HEAD_DIM = 64
BLOCK = 512
PARTS = 4
EPSILON = 1e-06
SCALE = 0.125
F32 = jnp.float32
BF16 = jnp.bfloat16


def by_core(first, second):
    return jnp.where(lax.axis_index("rows") & 1 == 1, second, first)


SWAPS = {"core": (1, 1), "first": (2, 4), "second": (4, 2)}


def exchange(value, stage):
    bits = SWAPS[stage]
    return lax.ppermute(value, "rows", [(i, i ^ bits[i & 1]) for i in range(8)])


def shift_line(value, step):
    return lax.ppermute(value, "heads", [(i, (i + step) % 4) for i in range(4)])


def slot_orders():
    here = lax.axis_index("rows")
    first, second = by_core(2, 4), by_core(4, 2)
    keep = jnp.stack([here, here ^ first, here ^ second, here ^ 6])
    away = jnp.stack([here, here ^ second, here ^ first, here ^ 6]) ^ 1
    return keep.astype(jnp.int32), away.astype(jnp.int32)


def after(value, *others):
    return lax.optimization_barrier((value,) + others)[0]


def behind(value, gates):
    if not gates:
        return value
    values = value if isinstance(value, tuple) else (value,)
    values = lax.optimization_barrier(values + tuple(gates))[: len(values)]
    return values if isinstance(value, tuple) else values[0]


def line_gather(piece):
    return (piece,) + tuple(shift_line(piece, step) for step in (1, 2, 3))


def line_order(pieces):
    here = lax.axis_index("heads")
    turned = [pieces[-i % 4] for i in range(4)]
    for bit in (1, 2):
        turned = [
            jnp.where(here & bit == bit, turned[i - bit], turned[i]) for i in range(4)
        ]
    return jnp.stack(turned)


def plane_gather(piece):
    return exchange(piece, "first"), exchange(piece, "second")


def plane_rest(ones):
    return exchange(after(*ones), "second")


def core_gather(mine):
    return tuple(exchange(member, "core") for member in mine)


def scatter_steps(send, keep, stack, finish):
    gates = yield send
    got = behind(exchange(send, "core"), gates)
    low = (keep[2:].astype(F32) + got[2:].astype(F32)).astype(BF16)
    gates = yield low
    got_two = behind(exchange(low, "second"), gates)
    one = (keep[1].astype(F32) + got[1].astype(F32) + got_two[1].astype(F32)).astype(BF16)
    gates = yield one
    got_one = behind(exchange(one, "first"), gates)
    sent = stack(keep, got, got_two, got_one)
    gates = yield sent[2]
    (two,) = behind((shift_line(sent[2], 2),), gates)
    gates = yield two
    one, three = behind((shift_line(sent[1], 1), shift_line(sent[3], 3)), gates)
    yield finish(sent[0], one, two, three)


def add_pieces(*pieces):
    return sum(piece.astype(F32) for piece in pieces)


def stack_rows(*parts):
    parts = [part[0] for part in parts[:3]] + [parts[3]]
    total = sum(part.astype(F32) for part in parts).astype(BF16)
    total = total.reshape(4, -1, total.shape[1])
    here = lax.axis_index("heads")
    return [
        lax.dynamic_index_in_dim(total, (here + step) % 4, keepdims=False) for step in range(4)
    ]


def columns_kernel(*refs):
    total = refs[3][...].astype(F32)
    for ref in refs[:3]:
        total = total + ref[0].astype(F32)
    here = lax.axis_index("heads")
    width = total.shape[1] // 12
    depth = total.shape[0] - 8
    rows = [total[depth:, i * 3 * width : (i + 1) * 3 * width] for i in range(4)]
    rows = jnp.concatenate(rows, axis=0).astype(BF16)
    heads = []
    for head in range(4):
        cuts = [slice((4 * i + head) * width, (4 * i + head + 1) * width) for i in range(3)]
        heads.append(jnp.concatenate([total[:depth, cut] for cut in cuts], axis=1).astype(BF16))
    for step in range(4):
        value = heads[0]
        for head in (1, 2, 3):
            value = jnp.where((here + step) % 4 == head, heads[head], value)
        refs[4 + step][:depth, :] = value
        refs[4 + step][depth:, :] = rows


def stack_columns(*parts):
    rows, columns = parts[3].shape
    own = pl.BlockSpec((1, rows, columns), lambda i: (0, 0, 0))
    out = (rows + 24, columns // 4)
    return pl.pallas_call(
        columns_kernel,
        grid=(1,),
        in_specs=[own, own, own, pl.BlockSpec((rows, columns), lambda i: (0, 0))],
        out_specs=[pl.BlockSpec(out, lambda i: (0, 0))] * 4,
        out_shape=[jax.ShapeDtypeStruct(out, BF16)] * 4,
        name="columns",
    )(*parts)


HBM = pl.BlockSpec(memory_space=pl.ANY)
WIDE = pltpu.CompilerParams(vmem_limit_bytes=58 << 20)


def copy_all(moves, semaphores):
    copies = [
        pltpu.make_async_copy(source, target, semaphores.at[i])
        for i, (source, target) in enumerate(moves)
    ]
    for copy in copies:
        copy.start()
    for copy in copies:
        copy.wait()


VMEM = pl.BlockSpec(memory_space=pltpu.VMEM)


def small_call(kernel, outs, name, *operands):
    return pl.pallas_call(
        kernel,
        in_specs=[VMEM for _ in operands],
        out_specs=[VMEM for _ in outs],
        out_shape=[jax.ShapeDtypeStruct(shape, dtype) for shape, dtype in outs],
        name=name,
    )(*operands)


def pack_kernel(*refs):
    refs[3][...] = jnp.concatenate([ref[...] for ref in refs[:3]], axis=1)


def pack(weights):
    depth, width = weights[0].shape
    return small_call(pack_kernel, [((depth, 3 * width), BF16)], "pack", *weights)[0]


def order_kernel(*refs):
    pieces, out = refs[:4], refs[4]
    here = lax.axis_index("heads")
    width = out.shape[1] // 12
    columns = []
    for head in range(4):
        value = pieces[0][...]
        for step in (1, 2, 3):
            value = jnp.where((here - head) % 4 == step, pieces[step][...], value)
        columns.append(value)
    for part in range(3):
        cut = slice(part * width, (part + 1) * width)
        out[:, part * 4 * width : (part + 1) * 4 * width] = jnp.concatenate(
            [value[:, cut] for value in columns], axis=1
        )


def order_columns(pieces):
    depth, width = pieces[0].shape
    return small_call(order_kernel, [((depth, 4 * width), BF16)], "order", *pieces)[0]


def split_kernel(*refs):
    total = sum(ref[...].astype(F32) for ref in refs[:4])
    depth, width = refs[4].shape
    for part in range(3):
        refs[4 + part][...] = total[:depth, part * width : (part + 1) * width]
    refs[7][...] = total[depth:]


def split_pieces(*pieces):
    rows, width = pieces[0].shape
    outs = [((rows - 32, width // 3), F32)] * 3 + [((32, width), F32)]
    return small_call(split_kernel, outs, "split", *pieces)


def project_kernel(order, tokens, bias, *refs):
    pieces, (packed, full, weight, semaphores) = refs[:8], refs[8:]
    step, last = pl.program_id(0), pl.num_programs(0) - 1
    out = pltpu.make_async_copy(weight, full, semaphores.at[8])

    @pl.when(step == 0)
    def _():
        copy_all([(pieces[i], weight.at[order[i]]) for i in range(8)], semaphores)
        out.start()

    whole = weight[...].reshape(-1, weight.shape[2])
    packed[...] = (dot_plain(tokens[...], whole) + bias[...]).astype(BF16)

    @pl.when(step == last)
    def _():
        out.wait()


def project(order, tokens, bias, pieces):
    count, width = tokens.shape
    depth, columns = pieces[0].shape
    tile = count // 4
    return pl.pallas_call(
        project_kernel,
        grid_spec=pltpu.PrefetchScalarGridSpec(
            num_scalar_prefetch=1,
            grid=(4,),
            in_specs=[
                pl.BlockSpec((tile, width), lambda i, *_: (i, 0)),
                pl.BlockSpec((1, columns), lambda i, *_: (0, 0)),
            ]
            + [HBM] * 8,
            out_specs=[
                pl.BlockSpec((tile, columns), lambda i, *_: (i, 0)),
                HBM,
            ],
            scratch_shapes=[
                pltpu.VMEM((8, depth, columns), BF16),
                pltpu.SemaphoreType.DMA((9,)),
            ],
        ),
        out_shape=(
            jax.ShapeDtypeStruct((count, columns), BF16),
            jax.ShapeDtypeStruct((8, depth, columns), BF16),
        ),
        compiler_params=WIDE,
        cost_estimate=pl.CostEstimate(
            flops=2 * count * width * columns,
            bytes_accessed=2 * (count * (width + columns) + 2 * width * columns),
            transcendentals=0,
        ),
        name="project",
    )(order, tokens, bias, *pieces)


def rows_terms_kernel(counts, extra, order, *refs):
    parts = len(counts)
    lefts, rights = refs[:parts], refs[parts : 2 * parts]
    send_ref, keep_ref, turned, product = refs[-4:]
    step = pl.program_id(0)
    width = product.shape[0]
    depth = width // 8
    begin = 0
    for left, right, steps in zip(lefts, rights, counts):

        @pl.when(step == begin)
        def _(left=left):
            turned[...] = left[...].T

        @pl.when((step >= begin) & (step < begin + steps))
        def _(right=right):
            product[...] = dot_plain(turned[...], right[...].reshape(right.shape[-2:]))

        begin += steps
    if extra:
        value = rights[0][...].reshape(rights[0].shape[-2:]).astype(F32)
        rows = lax.broadcasted_iota(jnp.int32, (8, width), 0)
        added = jnp.where(rows == 4, row_sum(value), refs[2 * parts][...]).astype(BF16)
    for slot in range(4):
        for out, place in ((send_ref, 4 + slot), (keep_ref, slot)):
            start = pl.multiple_of(order[place] * depth, depth)
            out[slot, :depth, :] = product[pl.ds(start, depth), :].astype(BF16)
            if extra:
                out[slot, depth:, :] = added


def rows_terms(pairs, order, extra=None):
    tokens, width = pairs[0][0].shape
    counts = [right.size // (tokens * width) for _, right in pairs]
    total = sum(counts)
    begins = [sum(counts[:i]) for i in range(len(counts))]
    depth = width // 8 + (0 if extra is None else 8)

    def right_spec(right, begin, count):
        def at(i):
            return jnp.clip(i - begin, 0, count - 1)

        if len(right.shape) == 3:
            return pl.BlockSpec((1, tokens, width), lambda i, *_: (at(i), 0, 0))
        return pl.BlockSpec((tokens, width), lambda i, *_: (0, at(i)))

    whole = pl.BlockSpec((tokens, width), lambda i, *_: (0, 0))
    slots = pl.BlockSpec((4, depth, width), lambda i, *_: (0, 0, i))
    specs = [right_spec(right, b, c) for (_, right), b, c in zip(pairs, begins, counts)]
    operands = [left for left, _ in pairs] + [right for _, right in pairs]
    if extra is not None:
        specs.append(pl.BlockSpec((8, width), lambda i, *_: (0, i)))
        operands.append(extra)
    return pl.pallas_call(
        functools.partial(rows_terms_kernel, counts, extra is not None),
        grid_spec=pltpu.PrefetchScalarGridSpec(
            num_scalar_prefetch=1,
            grid=(total,),
            in_specs=[whole for _ in pairs] + specs,
            out_specs=[slots, slots],
            scratch_shapes=[pltpu.VMEM((width, tokens), BF16), pltpu.VMEM((width, width), F32)],
        ),
        out_shape=(jax.ShapeDtypeStruct((4, depth, total * width), BF16),) * 2,
        compiler_params=pltpu.CompilerParams(vmem_limit_bytes=40 << 20),
        cost_estimate=pl.CostEstimate(
            flops=2 * tokens * width * width * total,
            bytes_accessed=2 * (tokens + width) * width * total,
            transcendentals=0,
        ),
        name="rows_terms",
    )(order, *operands)


def columns_term_kernel(order, left, right, out):
    out[0] = dot_rows(left[...], right[...]).astype(BF16)


def columns_term(left, right, order):
    tokens, width = right.shape
    depth = left.shape[1] // 8
    return pl.pallas_call(
        columns_term_kernel,
        grid_spec=pltpu.PrefetchScalarGridSpec(
            num_scalar_prefetch=1,
            grid=(4,),
            in_specs=[
                pl.BlockSpec((tokens, depth), lambda i, order: (0, order[i])),
                pl.BlockSpec((tokens, width), lambda i, order: (0, 0)),
            ],
            out_specs=pl.BlockSpec((1, depth, width), lambda i, order: (i, 0, 0)),
        ),
        out_shape=jax.ShapeDtypeStruct((4, depth, width), BF16),
        compiler_params=pltpu.CompilerParams(vmem_limit_bytes=32 << 20),
        cost_estimate=pl.CostEstimate(
            flops=2 * tokens * width * depth * 4,
            bytes_accessed=2 * (tokens * depth * 4 + tokens * width + depth * width * 4),
            transcendentals=0,
        ),
        name="columns_term",
    )(order, left, right)


class SlotMoves:
    def __init__(self):
        self.keep, self.away = slot_orders()
        self.order = jnp.concatenate([self.keep, self.away])

    def gather(self, weights, output_weight, inner_weight, outer_weight, smalls):
        depth, width = output_weight.shape
        self.columns = inner_weight.shape[1] // width
        pieces = line_gather(pack(weights))
        split = [
            inner_weight[:, i * width : (i + 1) * width] for i in range(self.columns)
        ]
        self.dense_line = line_gather(jnp.concatenate([output_weight, *split]))
        lined = order_columns(pieces)
        ones = plane_gather(lined)
        two = plane_rest(ones)
        self.dense_line = behind(self.dense_line, ones)
        mine = (lined,) + ones + (two,)
        self.packed_pieces = mine + core_gather(mine)
        outer_weight = after(outer_weight, pieces[3])
        self.outer_full = lax.all_gather(outer_weight, ("rows", "heads"), axis=0, tiled=True)
        return smalls

    def project(self, tokens, bias):
        lined = line_order(self.dense_line)
        width = lined.shape[2]
        lined = lined.reshape(4, self.columns + 1, -1, width).transpose(1, 0, 2, 3)
        lined = lined.reshape(-1, width)
        tokens = after(tokens, lined)
        packed, full = project(self.order, tokens, bias, self.packed_pieces)
        ones = behind(plane_gather(lined), (packed,))
        self.dense_mine = (lined,) + ones
        self.dense_depth = lined.shape[0] // (self.columns + 1)
        return after(packed, *ones), full.reshape(-1, full.shape[2])

    def dense_start(self, packed, earlier):
        mine = self.dense_mine
        got = core_gather(mine) + (plane_rest(mine[1:]),)
        got = got if earlier is None else behind(got, (earlier[0],))
        self.dense_got = got
        return after(packed, got[3])

    def dense(self, context):
        got = self.dense_got
        (last,) = behind(core_gather(got[3:]), (context,))
        pieces = self.dense_mine + got[3:] + got[:3] + (last,)
        outer = self.outer_full.reshape(self.columns, -1, self.outer_full.shape[1])
        return load_slots, 8 * (self.columns + 1) + 1, self.order, pieces + (outer,)

    def outer_terms(self, hidden_low, branch_grad):
        send = columns_term(hidden_low, branch_grad, self.away)
        keep = columns_term(after(hidden_low, send), branch_grad, self.keep)
        return keep, self.begin(scatter_steps(send, keep, stack_rows, add_pieces))

    def inner_terms(self, inner_pair, output_pair):
        return rows_terms((inner_pair, output_pair), self.order)

    def inner_steps(self, terms, gate):
        send, keep = terms
        return self.begin(scatter_steps(after(send, gate), keep, stack_rows, add_pieces))

    def inner_cut(self, both):
        cut = self.columns * both.shape[1] // (self.columns + 1)
        return both[:, :cut], both[:, cut:]

    def packed_terms(self, tokens, packed_grad, sums):
        width = tokens.shape[1]
        extra = jnp.concatenate([sums, jnp.zeros((24 - sums.shape[0], width), F32)])
        extra = extra.reshape(8, 3, width).reshape(8, 3 * width)
        return rows_terms(((tokens, packed_grad),), self.order, extra)

    def begin(self, steps):
        next(steps)
        return steps

    def hold(self, value, gate):
        return after(value, gate)

    def behind(self, value, steps, *gates):
        return after(value, steps.send(gates))

    def finish(self, steps, *gates):
        return steps.send(gates)

    def last(self, value, terms, earlier):
        steps = self.begin(scatter_steps(*terms, stack_columns, split_pieces))
        value = value((steps.send(()),))
        two = earlier.send((value,))
        steps.send((value, two))
        done = earlier.send(())
        steps.send((done,))
        steps.send(())
        *weights, total = steps.send(())
        rows = jnp.concatenate([total[i : i + 8] for i in (0, 8, 16, 24)], axis=1)
        rows = rows.reshape(24, -1)
        return value, weights, rows, rows[12], rows[14], done


class PlainMoves:
    def gather(self, weights, *dense):
        *dense, smalls = dense
        full = [
            lax.all_gather(lax.all_gather(w, "rows", axis=0, tiled=True), "heads", axis=1, tiled=True)
            for w in weights
        ]
        self.packed_weight = jnp.concatenate(full, axis=1)
        self.fulls = tuple(
            lax.all_gather(w, ("rows", "heads"), axis=0, tiled=True) for w in dense
        )
        return smalls

    def project(self, tokens, bias):
        packed = (dot_plain(tokens, self.packed_weight) + bias).astype(BF16)
        return packed, self.packed_weight

    def dense_start(self, packed, earlier):
        return packed

    def dense(self, context):
        output, inner, outer = self.fulls
        width = output.shape[1]
        chunks = inner.shape[1] // width
        sources = (
            output.reshape(8, -1, width),
            inner.reshape(8, -1, inner.shape[1]),
            outer.reshape(chunks, -1, width),
        )
        return load_whole, 2 + chunks, jnp.zeros((8,), jnp.int32), sources

    def scatter(self, term):
        return lax.psum_scatter(term, ("rows", "heads"), scatter_dimension=0, tiled=True)

    def outer_terms(self, hidden_low, branch_grad):
        return None, self.scatter(dot_rows(hidden_low, branch_grad))

    def inner_terms(self, inner_pair, output_pair):
        return self.scatter(dot_rows(*inner_pair)), self.scatter(dot_rows(*output_pair))

    def inner_steps(self, terms, gate):
        return terms

    def inner_cut(self, both):
        return both

    def packed_terms(self, tokens, packed_grad, sums):
        parts = [dot_rows(tokens, packed_grad[i]) for i in range(3)]
        parts = [lax.psum_scatter(p, "heads", scatter_dimension=1, tiled=True) for p in parts]
        weights = [lax.psum_scatter(p, "rows", scatter_dimension=0, tiled=True) for p in parts]
        biases = [jnp.sum(packed_grad[i], axis=0, dtype=F32) for i in (0, 2)]
        return weights, lax.psum((sums, *biases), ("rows", "heads"))

    def hold(self, value, gate):
        return value

    def behind(self, value, steps, *gates):
        return value

    def finish(self, steps, *gates):
        return steps

    def last(self, value, terms, earlier):
        weights, sums = terms
        return value(sums[:1]), weights, *sums, earlier


def head_only(value, which):
    lanes = lax.broadcasted_iota(jnp.int32, value.shape, 1)
    keep = (lanes < HEAD_DIM) if which == 0 else (lanes >= HEAD_DIM)
    return jnp.where(keep, value, jnp.zeros_like(value))


def dot_lanes(left, right):
    return lax.dot_general(left, right, (((1,), (1,)), ((), ())), preferred_element_type=F32)


def dot_rows(left, right):
    return lax.dot_general(left, right, (((0,), (0,)), ((), ())), preferred_element_type=F32)


def dot_plain(left, right):
    return lax.dot_general(left, right, (((1,), (0,)), ((), ())), preferred_element_type=F32)


def spans(parts):
    length = BLOCK // parts
    return [slice(i * length, (i + 1) * length) for i in range(parts)]


def by_part(product, left, right, parts, axis):
    return jnp.concatenate([product(left[at], right[at]) for at in spans(parts)], axis=axis)


def forward_pair(parts, query_ref, key_ref, value_ref, context_ref, total_ref, pair):
    lanes = pl.ds(pl.multiple_of(pair * 2 * HEAD_DIM, 2 * HEAD_DIM), 2 * HEAD_DIM)
    query = query_ref[:, lanes] * jnp.asarray(SCALE, BF16)
    key, value = key_ref[:, lanes], value_ref[:, lanes]
    flipped = None
    for which in range(2):
        scores = by_part(dot_lanes, key, head_only(query, which), parts, 1)
        largest = jnp.max(scores, axis=0, keepdims=True)
        powers = jnp.exp(scores - largest)
        denominator = jnp.sum(powers, axis=0, keepdims=True)
        total_ref[0, pair, which : which + 1, :] = largest + jnp.log(denominator)
        low, values = powers.astype(BF16), head_only(value, which)
        context = [dot_rows(values[at], low[:, at]) for at in spans(parts)]
        context = jnp.concatenate(context, axis=1) / denominator
        flipped = context if flipped is None else flipped + context
    context_ref[:, lanes] = flipped.T.astype(BF16)


def backward_pair(
    parts, query_ref, key_ref, value_ref, context_ref, grad_ref, total_ref, outs, pair
):
    lanes = pl.ds(pl.multiple_of(pair * 2 * HEAD_DIM, 2 * HEAD_DIM), 2 * HEAD_DIM)
    query = query_ref[:, lanes] * jnp.asarray(SCALE, BF16)
    key, value, grad = key_ref[:, lanes], value_ref[:, lanes], grad_ref[:, lanes]
    product = grad.astype(F32) * context_ref[:, lanes].astype(F32)
    flipped, key_sum, value_sum = None, None, None
    for which in range(2):
        query_one = head_only(query, which)
        grad_one = head_only(grad, which)
        ones = head_only(jnp.ones((8, 2 * HEAD_DIM), F32), which)
        row_dot = lax.dot_general(
            ones,
            product,
            (((1,), (1,)), ((), ())),
            precision=lax.Precision.HIGHEST,
            preferred_element_type=F32,
        )[:1]
        scores = by_part(dot_lanes, key, query_one, parts, 1)
        attention = jnp.exp(scores - total_ref[0, pair, which : which + 1, :])
        weight_grad = by_part(dot_lanes, value, grad_one, parts, 1)
        score_grad = (attention * (weight_grad - row_dot)).astype(BF16)
        low, keys = attention.astype(BF16), head_only(key, which)
        at_parts = spans(parts)
        value_part = [dot_plain(low[:, at], grad_one[at]) for at in at_parts]
        key_part = [dot_plain(score_grad[:, at], query_one[at]) for at in at_parts]
        query_part = [dot_rows(keys[at], score_grad[:, at]) for at in at_parts]
        value_part = jnp.concatenate(value_part, axis=0)
        key_part = jnp.concatenate(key_part, axis=0)
        query_part = jnp.concatenate(query_part, axis=1)
        flipped = query_part if flipped is None else flipped + query_part
        key_sum = key_part if key_sum is None else key_sum + key_part
        value_sum = value_part if value_sum is None else value_sum + value_part
    outs[0, :, lanes] = (flipped.T * SCALE).astype(BF16)
    outs[1, :, lanes] = key_sum.astype(BF16)
    outs[2, :, lanes] = value_sum.astype(BF16)


def by_kind(kind, pairs, run):
    for mine, parts in ((kind != 1, 1), (kind == 1, PARTS)):

        @pl.when(mine)
        def _(parts=parts):
            @pl.loop(0, pairs)
            def _(pair):
                run(parts, pair)


def forward_kernel(block, kinds, *refs):
    refs = refs[:3] + refs[-2:]
    by_kind(
        kinds[block(pl.program_id(0))],
        refs[4].shape[1],
        lambda parts, pair: forward_pair(parts, *refs, pair),
    )


def backward_kernel(block, kinds, *refs):
    refs = refs[:6] + refs[-1:]
    by_kind(
        kinds[block(pl.program_id(0))],
        refs[5].shape[1],
        lambda parts, pair: backward_pair(parts, *refs, pair),
    )


def attend(kernel, units, kinds, operands, earlier, outs, name):
    begin, end = units
    width = outs[0].shape[-1] // 2
    pairs = width // (2 * HEAD_DIM)

    def block(step):
        return (step + begin) // 2

    def half(step):
        return (step + begin) % 2

    narrow = (BLOCK, width)

    def spec(offset):
        return pl.BlockSpec(narrow, lambda i, *_: (block(i), half(i) + 2 * offset))

    totals = pl.BlockSpec((1, pairs, 2, BLOCK), lambda i, *_: (block(i), half(i), 0, 0))
    kinds_of = {
        2: spec(0),
        3: pl.BlockSpec((3,) + narrow, lambda i, *_: (0, block(i), half(i))),
        4: totals,
    }
    given = () if earlier is None else earlier
    first = 1 + len(operands)
    count = end - begin
    products = 4 if name == "attend_forward" else 10
    return pl.pallas_call(
        functools.partial(kernel, block),
        grid_spec=pltpu.PrefetchScalarGridSpec(
            num_scalar_prefetch=1,
            grid=(count,),
            in_specs=[totals if offset is None else spec(offset) for _, offset in operands]
            + [HBM for _ in given],
            out_specs=[kinds_of[len(out.shape)] for out in outs],
        ),
        out_shape=outs,
        input_output_aliases={first + i: i for i in range(len(given))},
        compiler_params=WIDE,
        cost_estimate=pl.CostEstimate(
            flops=products * count * BLOCK * BLOCK * width,
            bytes_accessed=products * count * BLOCK * width,
            transcendentals=count * BLOCK * BLOCK * width // HEAD_DIM,
        ),
        name=name,
    )(kinds, *[operand for operand, _ in operands], *given)


def attend_forward(units, kinds, packed, earlier):
    tokens, width = packed.shape[0], packed.shape[1] // 3
    pairs = width // (2 * HEAD_DIM)
    outs = (
        jax.ShapeDtypeStruct((tokens, width), BF16),
        jax.ShapeDtypeStruct((tokens // BLOCK, pairs, 2, BLOCK), F32),
    )
    operands = [(packed, 0), (packed, 1), (packed, 2)]
    return attend(forward_kernel, units, kinds, operands, earlier, outs, "attend_forward")


def attend_backward(units, kinds, packed, context, context_grad, totals, earlier):
    outs = (jax.ShapeDtypeStruct((3,) + context.shape, BF16),)
    operands = [(packed, 0), (packed, 1), (packed, 2), (context, 0)]
    operands += [(context_grad, 0), (totals, None)]
    return attend(backward_kernel, units, kinds, operands, earlier, outs, "attend_backward")


def tokens_kernel(first_grad, packed_grad, weight, out):
    width = out.shape[1]
    total = first_grad[...]
    for part in range(3):
        columns = weight[:, part * width : (part + 1) * width]
        total = total + dot_lanes(packed_grad[part], columns)
    out[...] = total


def tokens_gradient(first_grad, packed_grad, weight):
    count, width = first_grad.shape
    tile = count // 2
    rows = pl.BlockSpec((tile, width), lambda i: (i, 0))
    return pl.pallas_call(
        tokens_kernel,
        grid=(2,),
        in_specs=[
            rows,
            pl.BlockSpec((3, tile, width), lambda i: (0, i, 0)),
            pl.BlockSpec(weight.shape, lambda i: (0, 0)),
        ],
        out_specs=rows,
        out_shape=jax.ShapeDtypeStruct((count, width), F32),
        compiler_params=WIDE,
        cost_estimate=pl.CostEstimate(
            flops=6 * count * width * width,
            bytes_accessed=14 * count * width + 6 * width * width,
            transcendentals=0,
        ),
        name="tokens_gradient",
    )(first_grad, packed_grad, weight)


def norm_parts(value):
    average = jnp.mean(value, axis=-1, keepdims=True)
    centred = value - average
    scale = lax.rsqrt(jnp.mean(centred * centred, axis=-1, keepdims=True) + EPSILON)
    return centred * scale, scale


def norm_back(grad, gain, normed, scale):
    inner = grad * gain
    average = jnp.mean(inner, axis=-1, keepdims=True)
    along = jnp.mean(inner * normed, axis=-1, keepdims=True)
    return scale * (inner - average - normed * along)


def row_sum(value):
    return jnp.sum(value, axis=0, keepdims=True)


def dense_kernel(load, kinds, order, context, tokens, cotangent, vectors, *refs):
    count = len(refs) - 14
    sources = refs[:count]
    layer_out, hidden, branch, first_low, inner_grad, attended, first_grad, context_grad, sums = (
        refs[count : count + 9]
    )
    output_full, inner_full, outer_full, slopes, semaphores = refs[count + 9 :]
    step = pl.program_id(0)
    chunks, width = inner_full.shape[0], context.shape[1]

    @pl.when(step == 0)
    def _():
        copy_all(load(order, sources, output_full, inner_full, outer_full), semaphores)
        sums[...] = jnp.zeros_like(sums)

    def vector(row):
        return vectors[pl.ds(row, 1), :]

    def add(row, value):
        sums[pl.ds(row, 1), :] += row_sum(value)

    output_weight = output_full[...].reshape(width, width)
    attended_out = dot_plain(context[...], output_weight) + vector(0)
    first_normed, first_scale = norm_parts(tokens[...].astype(F32) + attended_out)
    first_out = first_normed * vector(1) + vector(2)
    low = first_out.astype(BF16)
    first_low[...] = low
    second = first_out + vector(3)
    for chunk in range(chunks):
        columns = pl.ds(chunk * width, width)
        inner = dot_plain(low, inner_full[chunk].reshape(width, width)) + vector(6 + chunk)
        half = 0.5 * (1.0 + lax.erf(inner * 0.7071067811865476))
        slopes[:, columns] = half + inner * jnp.exp(-0.5 * inner * inner) * 0.3989422804014327
        hidden_low = (inner * half).astype(BF16)
        hidden[:, columns] = hidden_low
        second = second + dot_plain(hidden_low, outer_full[chunk])
    normed, scale = norm_parts(second)
    block = step * context.shape[0] // BLOCK
    valid = jnp.where(kinds[block] != 2, 1.0, 0.0).astype(F32)
    layer_out[...] = ((normed * vector(4) + vector(5)) * valid).astype(BF16)
    out_grad = cotangent[...].astype(F32) * valid
    add(4, out_grad * normed)
    add(5, out_grad)
    second_grad = norm_back(out_grad, vector(4), normed, scale)
    branch_low = second_grad.astype(BF16)
    branch[...] = branch_low
    add(3, branch_low.astype(F32))
    first_out_grad = second_grad
    for chunk in range(chunks):
        columns = pl.ds(chunk * width, width)
        hidden_grad = dot_lanes(branch_low, outer_full[chunk])
        inner_low = (hidden_grad * slopes[:, columns]).astype(BF16)
        inner_grad[:, columns] = inner_low
        add(6 + chunk, inner_low.astype(F32))
        first_out_grad = first_out_grad + dot_lanes(
            inner_low, inner_full[chunk].reshape(width, width)
        )
    add(1, first_out_grad * first_normed)
    add(2, first_out_grad)
    grad = norm_back(first_out_grad, vector(1), first_normed, first_scale)
    first_grad[...] = grad
    attended_low = grad.astype(BF16)
    attended[...] = attended_low
    add(0, attended_low.astype(F32))
    context_grad[...] = dot_lanes(attended_low, output_weight).astype(BF16)


def dense(load, copies, kinds, order, context, tokens, cotangent, vectors, sources):
    count, width = tokens.shape
    chunks = vectors.shape[0] - 6
    tile = BLOCK
    narrow = pl.BlockSpec((tile, width), lambda i, *_: (i, 0))
    wide = pl.BlockSpec((tile, chunks * width), lambda i, *_: (i, 0))
    fixed = pl.BlockSpec(vectors.shape, lambda i, *_: (0, 0))
    low = jax.ShapeDtypeStruct((count, width), BF16)
    low_wide = jax.ShapeDtypeStruct((count, chunks * width), BF16)
    return pl.pallas_call(
        functools.partial(dense_kernel, load),
        grid_spec=pltpu.PrefetchScalarGridSpec(
            num_scalar_prefetch=2,
            grid=(count // tile,),
            in_specs=[narrow, narrow, narrow, fixed] + [HBM] * len(sources),
            out_specs=[narrow, wide, narrow, narrow, wide, narrow, narrow, narrow, fixed],
            scratch_shapes=[
                pltpu.VMEM((8, width // 8, width), BF16),
                pltpu.VMEM((chunks, 8, width // 8, width), BF16),
                pltpu.VMEM((chunks, width, width), BF16),
                pltpu.VMEM((tile, chunks * width), F32),
                pltpu.SemaphoreType.DMA((copies,)),
            ],
        ),
        out_shape=(
            low,
            low_wide,
            low,
            low,
            low_wide,
            low,
            jax.ShapeDtypeStruct((count, width), F32),
            low,
            jax.ShapeDtypeStruct(vectors.shape, F32),
        ),
        compiler_params=WIDE,
        cost_estimate=pl.CostEstimate(
            flops=4 * count * width * width * (1 + 2 * chunks),
            bytes_accessed=2 * count * width * (10 + 2 * chunks),
            transcendentals=2 * count * width * chunks,
        ),
        name="dense",
    )(kinds, order, context, tokens, cotangent, vectors, *sources)


def load_slots(order, sources, output_full, inner_full, outer_full):
    pieces, outer = sources[:8], sources[8]
    depth = output_full.shape[1]
    moves = []
    for slot in range(8):
        moves.append((pieces[slot].at[pl.ds(0, depth)], output_full.at[order[slot]]))
        for chunk in range(inner_full.shape[0]):
            source = pieces[slot].at[pl.ds(depth * (1 + chunk), depth)]
            moves.append((source, inner_full.at[chunk, order[slot]]))
    return moves + [(outer, outer_full)]


def load_whole(order, sources, output_full, inner_full, outer_full):
    output, inner, outer = sources
    width = output.shape[2]
    moves = [(output, output_full), (outer, outer_full)]
    for chunk in range(inner_full.shape[0]):
        moves.append((inner.at[:, :, pl.ds(chunk * width, width)], inner_full.at[chunk]))
    return moves


def shards(
    tokens,
    block_kind,
    query_weight,
    key_weight,
    value_weight,
    query_bias,
    value_bias,
    output_weight,
    output_bias,
    first_gain,
    first_shift,
    inner_weight,
    inner_bias,
    outer_weight,
    outer_bias,
    second_gain,
    second_shift,
    cotangent,
):
    width = tokens.shape[1]
    per_device = block_kind.shape[0] // lax.axis_size("heads")
    kinds = lax.dynamic_slice_in_dim(
        block_kind, lax.axis_index("heads") * per_device, per_device
    )
    singles = (output_bias, first_gain, first_shift, outer_bias, second_gain, second_shift)
    vectors = jnp.concatenate([jnp.stack(singles), inner_bias.reshape(-1, width)]).astype(F32)
    eight_by_four = lax.axis_size("rows") == 8 and lax.axis_size("heads") == 4
    moves = SlotMoves() if eight_by_four else PlainMoves()
    packed_bias = jnp.concatenate([query_bias, jnp.zeros_like(query_bias), value_bias])
    smalls = (packed_bias.astype(F32).reshape(1, -1), vectors, kinds)
    packed_bias, vectors, kinds = moves.gather(
        (query_weight, key_weight, value_weight),
        output_weight,
        inner_weight,
        outer_weight,
        smalls,
    )
    packed, packed_weight = moves.project(tokens, packed_bias)

    units = 2 * per_device
    earlier = attend_forward((0, units // 2), kinds, packed, None)
    packed_late = moves.dense_start(packed, earlier)
    context, totals = attend_forward((units // 2, units), kinds, packed_late, earlier)
    load, copies, order, sources = moves.dense(context)
    (
        layer_out,
        hidden_low,
        branch_grad,
        first_low,
        inner_grad,
        attended_grad,
        first_grad,
        context_grad,
        sums,
    ) = dense(load, copies, kinds, order, context, tokens, cotangent, vectors, sources)

    kernel_done, outer_steps = moves.outer_terms(hidden_low, branch_grad)
    inner_grad = moves.behind(inner_grad, outer_steps, kernel_done)
    inner_terms = moves.inner_terms((first_low, inner_grad), (context, attended_grad))
    context_grad = moves.behind(context_grad, outer_steps, inner_terms[1])
    inner_steps = moves.inner_steps(inner_terms, context_grad)
    cuts = (0, units // 4, units - units // 4, units)
    grads = None
    for begin, end in zip(cuts, cuts[1:]):
        if begin == cuts[1]:
            context_grad = moves.behind(context_grad, outer_steps, grads[0])
            context_grad = moves.behind(context_grad, inner_steps, grads[0], context_grad)
        if begin == cuts[2]:
            moves.finish(outer_steps, grads[0])
            outer_weight_grad = moves.finish(outer_steps, grads[0])
            context_grad = moves.hold(context_grad, outer_weight_grad)
            context_grad = moves.behind(context_grad, inner_steps, grads[0], context_grad)
        grads = attend_backward(
            (begin, end), kinds, packed, context, context_grad, totals, grads
        )
    (packed_grad,) = grads
    packed_grad = moves.behind(packed_grad, inner_steps, packed_grad)
    packed_terms = moves.packed_terms(tokens, packed_grad, sums)

    def tokens_part(gate):
        return tokens_gradient(first_grad, after(packed_grad, *gate), packed_weight)

    tokens_grad, weight_grads, small, query_sums, value_sums, inner_both = moves.last(
        tokens_part, packed_terms, inner_steps
    )
    inner_weight_grad, output_weight_grad = moves.inner_cut(inner_both)
    return (
        layer_out,
        tokens_grad,
        *weight_grads,
        query_sums,
        value_sums,
        output_weight_grad,
        small[0],
        small[1],
        small[2],
        inner_weight_grad,
        small[6 : sums.shape[0]].reshape(-1),
        outer_weight_grad,
        small[3],
        small[4],
        small[5],
    )


def solution(mesh):
    both = P(("rows", "heads"), None)
    placed = (
        (both, P("rows"))
        + (P("rows", "heads"),) * 3
        + (P(), P(), both, P(), P(), P(), both, P(), both, P(), P(), P(), both)
    )
    given = (
        (both, both)
        + (P("rows", "heads"),) * 3
        + (P(), P(), both, P(), P(), P(), both, P(), both, P(), P(), P())
    )
    return jax.shard_map(
        shards, mesh=mesh, in_specs=placed, out_specs=given, check_vma=False
    )
```

```python
import functools

import jax
import jax.numpy as jnp
from jax import lax
from jax.experimental import pallas as pl
from jax.experimental.pallas import tpu as pltpu
from jax.sharding import PartitionSpec as P

HEAD_DIM = 64
BLOCK = 512
PARTS = 4
EPSILON = 1e-06
SCALE = 0.125
F32 = jnp.float32
BF16 = jnp.bfloat16


def by_core(first, second):
    return jnp.where(lax.axis_index("rows") & 1 == 1, second, first)


SWAPS = {"core": (1, 1), "first": (2, 4), "second": (4, 2)}


def exchange(value, stage):
    bits = SWAPS[stage]
    return lax.ppermute(value, "rows", [(i, i ^ bits[i & 1]) for i in range(8)])


def shift_line(value, step):
    return lax.ppermute(value, "heads", [(i, (i + step) % 4) for i in range(4)])


def slot_orders():
    here = lax.axis_index("rows")
    first, second = by_core(2, 4), by_core(4, 2)
    keep = jnp.stack([here, here ^ first, here ^ second, here ^ 6])
    away = jnp.stack([here, here ^ second, here ^ first, here ^ 6]) ^ 1
    return keep.astype(jnp.int32), away.astype(jnp.int32)


def after(value, *others):
    return lax.optimization_barrier((value,) + others)[0]


def behind(value, gates):
    if not gates:
        return value
    values = value if isinstance(value, tuple) else (value,)
    values = lax.optimization_barrier(values + tuple(gates))[: len(values)]
    return values if isinstance(value, tuple) else values[0]


def line_gather(piece):
    return (piece,) + tuple(shift_line(piece, step) for step in (1, 2, 3))


def line_order(pieces):
    here = lax.axis_index("heads")
    turned = [pieces[-i % 4] for i in range(4)]
    for bit in (1, 2):
        turned = [
            jnp.where(here & bit == bit, turned[i - bit], turned[i]) for i in range(4)
        ]
    return jnp.stack(turned)


def plane_gather(piece):
    return exchange(piece, "first"), exchange(piece, "second")


def plane_rest(ones):
    return exchange(after(*ones), "second")


def core_gather(mine):
    return tuple(exchange(member, "core") for member in mine)


def scatter_steps(send, keep, stack, finish):
    gates = yield send
    got = behind(exchange(send, "core"), gates)
    low = (keep[2:].astype(F32) + got[2:].astype(F32)).astype(BF16)
    gates = yield low
    got_two = behind(exchange(low, "second"), gates)
    one = (keep[1].astype(F32) + got[1].astype(F32) + got_two[1].astype(F32)).astype(BF16)
    gates = yield one
    got_one = behind(exchange(one, "first"), gates)
    sent = stack(keep, got, got_two, got_one)
    gates = yield sent[2]
    (two,) = behind((shift_line(sent[2], 2),), gates)
    gates = yield two
    one, three = behind((shift_line(sent[1], 1), shift_line(sent[3], 3)), gates)
    yield finish(sent[0], one, two, three)


def add_pieces(*pieces):
    return sum(piece.astype(F32) for piece in pieces)


def stack_rows(*parts):
    parts = [part[0] for part in parts[:3]] + [parts[3]]
    total = sum(part.astype(F32) for part in parts).astype(BF16)
    total = total.reshape(4, -1, total.shape[1])
    here = lax.axis_index("heads")
    return [
        lax.dynamic_index_in_dim(total, (here + step) % 4, keepdims=False) for step in range(4)
    ]


def columns_kernel(*refs):
    total = refs[3][...].astype(F32)
    for ref in refs[:3]:
        total = total + ref[0].astype(F32)
    here = lax.axis_index("heads")
    width = total.shape[1] // 12
    depth = total.shape[0] - 8
    rows = [total[depth:, i * 3 * width : (i + 1) * 3 * width] for i in range(4)]
    rows = jnp.concatenate(rows, axis=0).astype(BF16)
    heads = []
    for head in range(4):
        cuts = [slice((4 * i + head) * width, (4 * i + head + 1) * width) for i in range(3)]
        heads.append(jnp.concatenate([total[:depth, cut] for cut in cuts], axis=1).astype(BF16))
    for step in range(4):
        value = heads[0]
        for head in (1, 2, 3):
            value = jnp.where((here + step) % 4 == head, heads[head], value)
        refs[4 + step][:depth, :] = value
        refs[4 + step][depth:, :] = rows


def stack_columns(*parts):
    rows, columns = parts[3].shape
    own = pl.BlockSpec((1, rows, columns), lambda i: (0, 0, 0))
    out = (rows + 24, columns // 4)
    return pl.pallas_call(
        columns_kernel,
        grid=(1,),
        in_specs=[own, own, own, pl.BlockSpec((rows, columns), lambda i: (0, 0))],
        out_specs=[pl.BlockSpec(out, lambda i: (0, 0))] * 4,
        out_shape=[jax.ShapeDtypeStruct(out, BF16)] * 4,
        name="columns",
    )(*parts)


HBM = pl.BlockSpec(memory_space=pl.ANY)
WIDE = pltpu.CompilerParams(vmem_limit_bytes=58 << 20)


def copy_all(moves, semaphores):
    copies = [
        pltpu.make_async_copy(source, target, semaphores.at[i])
        for i, (source, target) in enumerate(moves)
    ]
    for copy in copies:
        copy.start()
    for copy in copies:
        copy.wait()


VMEM = pl.BlockSpec(memory_space=pltpu.VMEM)


def small_call(kernel, outs, name, *operands):
    return pl.pallas_call(
        kernel,
        in_specs=[VMEM for _ in operands],
        out_specs=[VMEM for _ in outs],
        out_shape=[jax.ShapeDtypeStruct(shape, dtype) for shape, dtype in outs],
        name=name,
    )(*operands)


def pack_kernel(*refs):
    refs[3][...] = jnp.concatenate([ref[...] for ref in refs[:3]], axis=1)


def pack(weights):
    depth, width = weights[0].shape
    return small_call(pack_kernel, [((depth, 3 * width), BF16)], "pack", *weights)[0]


def order_kernel(*refs):
    pieces, out = refs[:4], refs[4]
    here = lax.axis_index("heads")
    width = out.shape[1] // 12
    columns = []
    for head in range(4):
        value = pieces[0][...]
        for step in (1, 2, 3):
            value = jnp.where((here - head) % 4 == step, pieces[step][...], value)
        columns.append(value)
    for part in range(3):
        cut = slice(part * width, (part + 1) * width)
        out[:, part * 4 * width : (part + 1) * 4 * width] = jnp.concatenate(
            [value[:, cut] for value in columns], axis=1
        )


def order_columns(pieces):
    depth, width = pieces[0].shape
    return small_call(order_kernel, [((depth, 4 * width), BF16)], "order", *pieces)[0]


def split_kernel(*refs):
    total = sum(ref[...].astype(F32) for ref in refs[:4])
    depth, width = refs[4].shape
    for part in range(3):
        refs[4 + part][...] = total[:depth, part * width : (part + 1) * width]
    refs[7][...] = total[depth:]


def split_pieces(*pieces):
    rows, width = pieces[0].shape
    outs = [((rows - 32, width // 3), F32)] * 3 + [((32, width), F32)]
    return small_call(split_kernel, outs, "split", *pieces)


def project_kernel(order, tokens, bias, *refs):
    pieces, (packed, full, weight, semaphores) = refs[:8], refs[8:]
    step, last = pl.program_id(0), pl.num_programs(0) - 1
    out = pltpu.make_async_copy(weight, full, semaphores.at[8])

    @pl.when(step == 0)
    def _():
        copy_all([(pieces[i], weight.at[order[i]]) for i in range(8)], semaphores)
        out.start()

    whole = weight[...].reshape(-1, weight.shape[2])
    packed[...] = (dot_plain(tokens[...], whole) + bias[...]).astype(BF16)

    @pl.when(step == last)
    def _():
        out.wait()


def project(order, tokens, bias, pieces):
    count, width = tokens.shape
    depth, columns = pieces[0].shape
    tile = count // 4
    return pl.pallas_call(
        project_kernel,
        grid_spec=pltpu.PrefetchScalarGridSpec(
            num_scalar_prefetch=1,
            grid=(4,),
            in_specs=[
                pl.BlockSpec((tile, width), lambda i, *_: (i, 0)),
                pl.BlockSpec((1, columns), lambda i, *_: (0, 0)),
            ]
            + [HBM] * 8,
            out_specs=[
                pl.BlockSpec((tile, columns), lambda i, *_: (i, 0)),
                HBM,
            ],
            scratch_shapes=[
                pltpu.VMEM((8, depth, columns), BF16),
                pltpu.SemaphoreType.DMA((9,)),
            ],
        ),
        out_shape=(
            jax.ShapeDtypeStruct((count, columns), BF16),
            jax.ShapeDtypeStruct((8, depth, columns), BF16),
        ),
        compiler_params=WIDE,
        cost_estimate=pl.CostEstimate(
            flops=2 * count * width * columns,
            bytes_accessed=2 * (count * (width + columns) + 2 * width * columns),
            transcendentals=0,
        ),
        name="project",
    )(order, tokens, bias, *pieces)


def rows_terms_kernel(counts, extra, order, *refs):
    parts = len(counts)
    lefts, rights = refs[:parts], refs[parts : 2 * parts]
    send_ref, keep_ref, turned, product = refs[-4:]
    step = pl.program_id(0)
    width = product.shape[0]
    depth = width // 8
    begin = 0
    for left, right, steps in zip(lefts, rights, counts):

        @pl.when(step == begin)
        def _(left=left):
            turned[...] = left[...].T

        @pl.when((step >= begin) & (step < begin + steps))
        def _(right=right):
            product[...] = dot_plain(turned[...], right[...].reshape(right.shape[-2:]))

        begin += steps
    if extra:
        value = rights[0][...].reshape(rights[0].shape[-2:]).astype(F32)
        rows = lax.broadcasted_iota(jnp.int32, (8, width), 0)
        added = jnp.where(rows == 4, row_sum(value), refs[2 * parts][...]).astype(BF16)
    for slot in range(4):
        for out, place in ((send_ref, 4 + slot), (keep_ref, slot)):
            start = pl.multiple_of(order[place] * depth, depth)
            out[slot, :depth, :] = product[pl.ds(start, depth), :].astype(BF16)
            if extra:
                out[slot, depth:, :] = added


def rows_terms(pairs, order, extra=None):
    tokens, width = pairs[0][0].shape
    counts = [right.size // (tokens * width) for _, right in pairs]
    total = sum(counts)
    begins = [sum(counts[:i]) for i in range(len(counts))]
    depth = width // 8 + (0 if extra is None else 8)

    def right_spec(right, begin, count):
        def at(i):
            return jnp.clip(i - begin, 0, count - 1)

        if len(right.shape) == 3:
            return pl.BlockSpec((1, tokens, width), lambda i, *_: (at(i), 0, 0))
        return pl.BlockSpec((tokens, width), lambda i, *_: (0, at(i)))

    whole = pl.BlockSpec((tokens, width), lambda i, *_: (0, 0))
    slots = pl.BlockSpec((4, depth, width), lambda i, *_: (0, 0, i))
    specs = [right_spec(right, b, c) for (_, right), b, c in zip(pairs, begins, counts)]
    operands = [left for left, _ in pairs] + [right for _, right in pairs]
    if extra is not None:
        specs.append(pl.BlockSpec((8, width), lambda i, *_: (0, i)))
        operands.append(extra)
    return pl.pallas_call(
        functools.partial(rows_terms_kernel, counts, extra is not None),
        grid_spec=pltpu.PrefetchScalarGridSpec(
            num_scalar_prefetch=1,
            grid=(total,),
            in_specs=[whole for _ in pairs] + specs,
            out_specs=[slots, slots],
            scratch_shapes=[pltpu.VMEM((width, tokens), BF16), pltpu.VMEM((width, width), F32)],
        ),
        out_shape=(jax.ShapeDtypeStruct((4, depth, total * width), BF16),) * 2,
        compiler_params=pltpu.CompilerParams(vmem_limit_bytes=40 << 20),
        cost_estimate=pl.CostEstimate(
            flops=2 * tokens * width * width * total,
            bytes_accessed=2 * (tokens + width) * width * total,
            transcendentals=0,
        ),
        name="rows_terms",
    )(order, *operands)


def columns_term_kernel(order, left, right, out):
    out[0] = dot_rows(left[...], right[...]).astype(BF16)


def columns_term(left, right, order):
    tokens, width = right.shape
    depth = left.shape[1] // 8
    return pl.pallas_call(
        columns_term_kernel,
        grid_spec=pltpu.PrefetchScalarGridSpec(
            num_scalar_prefetch=1,
            grid=(4,),
            in_specs=[
                pl.BlockSpec((tokens, depth), lambda i, order: (0, order[i])),
                pl.BlockSpec((tokens, width), lambda i, order: (0, 0)),
            ],
            out_specs=pl.BlockSpec((1, depth, width), lambda i, order: (i, 0, 0)),
        ),
        out_shape=jax.ShapeDtypeStruct((4, depth, width), BF16),
        compiler_params=pltpu.CompilerParams(vmem_limit_bytes=32 << 20),
        cost_estimate=pl.CostEstimate(
            flops=2 * tokens * width * depth * 4,
            bytes_accessed=2 * (tokens * depth * 4 + tokens * width + depth * width * 4),
            transcendentals=0,
        ),
        name="columns_term",
    )(order, left, right)


class SlotMoves:
    def __init__(self):
        self.keep, self.away = slot_orders()
        self.order = jnp.concatenate([self.keep, self.away])

    def gather(self, weights, output_weight, inner_weight, outer_weight, smalls):
        depth, width = output_weight.shape
        self.columns = inner_weight.shape[1] // width
        pieces = line_gather(pack(weights))
        split = [
            inner_weight[:, i * width : (i + 1) * width] for i in range(self.columns)
        ]
        self.dense_line = line_gather(jnp.concatenate([output_weight, *split]))
        lined = order_columns(pieces)
        ones = plane_gather(lined)
        two = plane_rest(ones)
        self.dense_line = behind(self.dense_line, ones)
        mine = (lined,) + ones + (two,)
        self.packed_pieces = mine + core_gather(mine)
        outer_weight = after(outer_weight, pieces[3])
        self.outer_full = lax.all_gather(outer_weight, ("rows", "heads"), axis=0, tiled=True)
        return smalls

    def project(self, tokens, bias):
        lined = line_order(self.dense_line)
        width = lined.shape[2]
        lined = lined.reshape(4, self.columns + 1, -1, width).transpose(1, 0, 2, 3)
        lined = lined.reshape(-1, width)
        tokens = after(tokens, lined)
        packed, full = project(self.order, tokens, bias, self.packed_pieces)
        ones = behind(plane_gather(lined), (packed,))
        self.dense_mine = (lined,) + ones
        self.dense_depth = lined.shape[0] // (self.columns + 1)
        return after(packed, *ones), full.reshape(-1, full.shape[2])

    def dense_start(self, packed, earlier):
        mine = self.dense_mine
        got = core_gather(mine) + (plane_rest(mine[1:]),)
        got = got if earlier is None else behind(got, (earlier[0],))
        self.dense_got = got
        return after(packed, got[3])

    def dense(self, context):
        got = self.dense_got
        (last,) = behind(core_gather(got[3:]), (context,))
        pieces = self.dense_mine + got[3:] + got[:3] + (last,)
        outer = self.outer_full.reshape(self.columns, -1, self.outer_full.shape[1])
        return load_slots, 8 * (self.columns + 1) + 1, self.order, pieces + (outer,)

    def outer_terms(self, hidden_low, branch_grad):
        send = columns_term(hidden_low, branch_grad, self.away)
        keep = columns_term(after(hidden_low, send), branch_grad, self.keep)
        return keep, self.begin(scatter_steps(send, keep, stack_rows, add_pieces))

    def inner_terms(self, inner_pair, output_pair):
        return rows_terms((inner_pair, output_pair), self.order)

    def inner_steps(self, terms, gate):
        send, keep = terms
        return self.begin(scatter_steps(after(send, gate), keep, stack_rows, add_pieces))

    def inner_cut(self, both):
        cut = self.columns * both.shape[1] // (self.columns + 1)
        return both[:, :cut], both[:, cut:]

    def packed_terms(self, tokens, packed_grad, sums):
        width = tokens.shape[1]
        extra = jnp.concatenate([sums, jnp.zeros((24 - sums.shape[0], width), F32)])
        extra = extra.reshape(8, 3, width).reshape(8, 3 * width)
        return rows_terms(((tokens, packed_grad),), self.order, extra)

    def begin(self, steps):
        next(steps)
        return steps

    def hold(self, value, gate):
        return after(value, gate)

    def behind(self, value, steps, *gates):
        return after(value, steps.send(gates))

    def finish(self, steps, *gates):
        return steps.send(gates)

    def last(self, value, terms, earlier):
        steps = self.begin(scatter_steps(*terms, stack_columns, split_pieces))
        value = value((steps.send(()),))
        two = earlier.send((value,))
        steps.send((value, two))
        done = earlier.send(())
        steps.send((done,))
        steps.send(())
        *weights, total = steps.send(())
        rows = jnp.concatenate([total[i : i + 8] for i in (0, 8, 16, 24)], axis=1)
        rows = rows.reshape(24, -1)
        return value, weights, rows, rows[12], rows[14], done


class PlainMoves:
    def gather(self, weights, *dense):
        *dense, smalls = dense
        full = [
            lax.all_gather(lax.all_gather(w, "rows", axis=0, tiled=True), "heads", axis=1, tiled=True)
            for w in weights
        ]
        self.packed_weight = jnp.concatenate(full, axis=1)
        self.fulls = tuple(
            lax.all_gather(w, ("rows", "heads"), axis=0, tiled=True) for w in dense
        )
        return smalls

    def project(self, tokens, bias):
        packed = (dot_plain(tokens, self.packed_weight) + bias).astype(BF16)
        return packed, self.packed_weight

    def dense_start(self, packed, earlier):
        return packed

    def dense(self, context):
        output, inner, outer = self.fulls
        width = output.shape[1]
        chunks = inner.shape[1] // width
        sources = (
            output.reshape(8, -1, width),
            inner.reshape(8, -1, inner.shape[1]),
            outer.reshape(chunks, -1, width),
        )
        return load_whole, 2 + chunks, jnp.zeros((8,), jnp.int32), sources

    def scatter(self, term):
        return lax.psum_scatter(term, ("rows", "heads"), scatter_dimension=0, tiled=True)

    def outer_terms(self, hidden_low, branch_grad):
        return None, self.scatter(dot_rows(hidden_low, branch_grad))

    def inner_terms(self, inner_pair, output_pair):
        return self.scatter(dot_rows(*inner_pair)), self.scatter(dot_rows(*output_pair))

    def inner_steps(self, terms, gate):
        return terms

    def inner_cut(self, both):
        return both

    def packed_terms(self, tokens, packed_grad, sums):
        parts = [dot_rows(tokens, packed_grad[i]) for i in range(3)]
        parts = [lax.psum_scatter(p, "heads", scatter_dimension=1, tiled=True) for p in parts]
        weights = [lax.psum_scatter(p, "rows", scatter_dimension=0, tiled=True) for p in parts]
        biases = [jnp.sum(packed_grad[i], axis=0, dtype=F32) for i in (0, 2)]
        return weights, lax.psum((sums, *biases), ("rows", "heads"))

    def hold(self, value, gate):
        return value

    def behind(self, value, steps, *gates):
        return value

    def finish(self, steps, *gates):
        return steps

    def last(self, value, terms, earlier):
        weights, sums = terms
        return value(sums[:1]), weights, *sums, earlier


def head_only(value, which):
    lanes = lax.broadcasted_iota(jnp.int32, value.shape, 1)
    keep = (lanes < HEAD_DIM) if which == 0 else (lanes >= HEAD_DIM)
    return jnp.where(keep, value, jnp.zeros_like(value))


def dot_lanes(left, right):
    return lax.dot_general(left, right, (((1,), (1,)), ((), ())), preferred_element_type=F32)


def dot_rows(left, right):
    return lax.dot_general(left, right, (((0,), (0,)), ((), ())), preferred_element_type=F32)


def dot_plain(left, right):
    return lax.dot_general(left, right, (((1,), (0,)), ((), ())), preferred_element_type=F32)


def spans(parts):
    length = BLOCK // parts
    return [slice(i * length, (i + 1) * length) for i in range(parts)]


def by_part(product, left, right, parts, axis):
    return jnp.concatenate([product(left[at], right[at]) for at in spans(parts)], axis=axis)


def forward_pair(parts, query_ref, key_ref, value_ref, context_ref, total_ref, pair):
    lanes = pl.ds(pl.multiple_of(pair * 2 * HEAD_DIM, 2 * HEAD_DIM), 2 * HEAD_DIM)
    query = query_ref[:, lanes] * jnp.asarray(SCALE, BF16)
    key, value = key_ref[:, lanes], value_ref[:, lanes]
    flipped = None
    for which in range(2):
        scores = by_part(dot_lanes, key, head_only(query, which), parts, 1)
        largest = jnp.max(scores, axis=0, keepdims=True)
        powers = jnp.exp(scores - largest)
        denominator = jnp.sum(powers, axis=0, keepdims=True)
        total_ref[0, pair, which : which + 1, :] = largest + jnp.log(denominator)
        low, values = powers.astype(BF16), head_only(value, which)
        context = [dot_rows(values[at], low[:, at]) for at in spans(parts)]
        context = jnp.concatenate(context, axis=1) / denominator
        flipped = context if flipped is None else flipped + context
    context_ref[:, lanes] = flipped.T.astype(BF16)


def backward_pair(
    parts, query_ref, key_ref, value_ref, context_ref, grad_ref, total_ref, outs, pair
):
    lanes = pl.ds(pl.multiple_of(pair * 2 * HEAD_DIM, 2 * HEAD_DIM), 2 * HEAD_DIM)
    query = query_ref[:, lanes] * jnp.asarray(SCALE, BF16)
    key, value, grad = key_ref[:, lanes], value_ref[:, lanes], grad_ref[:, lanes]
    product = grad.astype(F32) * context_ref[:, lanes].astype(F32)
    flipped, key_sum, value_sum = None, None, None
    for which in range(2):
        query_one = head_only(query, which)
        grad_one = head_only(grad, which)
        ones = head_only(jnp.ones((8, 2 * HEAD_DIM), F32), which)
        row_dot = lax.dot_general(
            ones,
            product,
            (((1,), (1,)), ((), ())),
            precision=lax.Precision.HIGHEST,
            preferred_element_type=F32,
        )[:1]
        scores = by_part(dot_lanes, key, query_one, parts, 1)
        attention = jnp.exp(scores - total_ref[0, pair, which : which + 1, :])
        weight_grad = by_part(dot_lanes, value, grad_one, parts, 1)
        score_grad = (attention * (weight_grad - row_dot)).astype(BF16)
        low, keys = attention.astype(BF16), head_only(key, which)
        at_parts = spans(parts)
        value_part = [dot_plain(low[:, at], grad_one[at]) for at in at_parts]
        key_part = [dot_plain(score_grad[:, at], query_one[at]) for at in at_parts]
        query_part = [dot_rows(keys[at], score_grad[:, at]) for at in at_parts]
        value_part = jnp.concatenate(value_part, axis=0)
        key_part = jnp.concatenate(key_part, axis=0)
        query_part = jnp.concatenate(query_part, axis=1)
        flipped = query_part if flipped is None else flipped + query_part
        key_sum = key_part if key_sum is None else key_sum + key_part
        value_sum = value_part if value_sum is None else value_sum + value_part
    outs[0, :, lanes] = (flipped.T * SCALE).astype(BF16)
    outs[1, :, lanes] = key_sum.astype(BF16)
    outs[2, :, lanes] = value_sum.astype(BF16)


def own_kind(kinds, block):
    each = kinds.shape[0] // lax.axis_size("heads")
    return kinds[lax.axis_index("heads") * each + block]


def by_kind(kind, pairs, run):
    for mine, parts in ((kind != 1, 1), (kind == 1, PARTS)):

        @pl.when(mine)
        def _(parts=parts):
            if parts == 1:
                for pair in range(pairs):
                    run(parts, pair)
                return

            @pl.loop(0, pairs)
            def _(pair):
                run(parts, pair)


def forward_kernel(block, kinds, *refs):
    refs = refs[:3] + refs[-2:]
    by_kind(
        own_kind(kinds, block(pl.program_id(0))),
        refs[4].shape[1],
        lambda parts, pair: forward_pair(parts, *refs, pair),
    )


def backward_kernel(block, kinds, *refs):
    refs = refs[:6] + refs[-1:]
    by_kind(
        own_kind(kinds, block(pl.program_id(0))),
        refs[5].shape[1],
        lambda parts, pair: backward_pair(parts, *refs, pair),
    )


def attend(kernel, units, kinds, operands, earlier, outs, name):
    begin, end = units
    width = outs[0].shape[-1] // 2
    pairs = width // (2 * HEAD_DIM)

    def block(step):
        return (step + begin) // 2

    def half(step):
        return (step + begin) % 2

    narrow = (BLOCK, width)

    def spec(offset):
        return pl.BlockSpec(narrow, lambda i, *_: (block(i), half(i) + 2 * offset))

    totals = pl.BlockSpec((1, pairs, 2, BLOCK), lambda i, *_: (block(i), half(i), 0, 0))
    kinds_of = {
        2: spec(0),
        3: pl.BlockSpec((3,) + narrow, lambda i, *_: (0, block(i), half(i))),
        4: totals,
    }
    given = () if earlier is None else earlier
    first = 1 + len(operands)
    count = end - begin
    products = 4 if name == "attend_forward" else 10
    return pl.pallas_call(
        functools.partial(kernel, block),
        grid_spec=pltpu.PrefetchScalarGridSpec(
            num_scalar_prefetch=1,
            grid=(count,),
            in_specs=[totals if offset is None else spec(offset) for _, offset in operands]
            + [HBM for _ in given],
            out_specs=[kinds_of[len(out.shape)] for out in outs],
        ),
        out_shape=outs,
        input_output_aliases={first + i: i for i in range(len(given))},
        compiler_params=WIDE,
        cost_estimate=pl.CostEstimate(
            flops=products * count * BLOCK * BLOCK * width,
            bytes_accessed=products * count * BLOCK * width,
            transcendentals=count * BLOCK * BLOCK * width // HEAD_DIM,
        ),
        name=name,
    )(kinds, *[operand for operand, _ in operands], *given)


def attend_forward(units, kinds, packed, earlier):
    tokens, width = packed.shape[0], packed.shape[1] // 3
    pairs = width // (2 * HEAD_DIM)
    outs = (
        jax.ShapeDtypeStruct((tokens, width), BF16),
        jax.ShapeDtypeStruct((tokens // BLOCK, pairs, 2, BLOCK), F32),
    )
    operands = [(packed, 0), (packed, 1), (packed, 2)]
    return attend(forward_kernel, units, kinds, operands, earlier, outs, "attend_forward")


def attend_backward(units, kinds, packed, context, context_grad, totals, earlier):
    outs = (jax.ShapeDtypeStruct((3,) + context.shape, BF16),)
    operands = [(packed, 0), (packed, 1), (packed, 2), (context, 0)]
    operands += [(context_grad, 0), (totals, None)]
    return attend(backward_kernel, units, kinds, operands, earlier, outs, "attend_backward")


def tokens_kernel(first_grad, packed_grad, weight, out):
    width = out.shape[1]
    total = first_grad[...]
    for part in range(3):
        columns = weight[:, part * width : (part + 1) * width]
        total = total + dot_lanes(packed_grad[part], columns)
    out[...] = total


def tokens_gradient(first_grad, packed_grad, weight):
    count, width = first_grad.shape
    tile = count // 2
    rows = pl.BlockSpec((tile, width), lambda i: (i, 0))
    return pl.pallas_call(
        tokens_kernel,
        grid=(2,),
        in_specs=[
            rows,
            pl.BlockSpec((3, tile, width), lambda i: (0, i, 0)),
            pl.BlockSpec(weight.shape, lambda i: (0, 0)),
        ],
        out_specs=rows,
        out_shape=jax.ShapeDtypeStruct((count, width), F32),
        compiler_params=WIDE,
        cost_estimate=pl.CostEstimate(
            flops=6 * count * width * width,
            bytes_accessed=14 * count * width + 6 * width * width,
            transcendentals=0,
        ),
        name="tokens_gradient",
    )(first_grad, packed_grad, weight)


def norm_parts(value):
    average = jnp.mean(value, axis=-1, keepdims=True)
    centred = value - average
    scale = lax.rsqrt(jnp.mean(centred * centred, axis=-1, keepdims=True) + EPSILON)
    return centred * scale, scale


def norm_back(grad, gain, normed, scale):
    inner = grad * gain
    average = jnp.mean(inner, axis=-1, keepdims=True)
    along = jnp.mean(inner * normed, axis=-1, keepdims=True)
    return scale * (inner - average - normed * along)


def row_sum(value):
    return jnp.sum(value, axis=0, keepdims=True)


def dense_kernel(load, kinds, order, context, tokens, cotangent, vectors, *refs):
    count = len(refs) - 14
    sources = refs[:count]
    layer_out, hidden, branch, first_low, inner_grad, attended, first_grad, context_grad, sums = (
        refs[count : count + 9]
    )
    output_full, inner_full, outer_full, slopes, semaphores = refs[count + 9 :]
    step = pl.program_id(0)
    chunks, width = inner_full.shape[0], context.shape[1]

    @pl.when(step == 0)
    def _():
        copy_all(load(order, sources, output_full, inner_full, outer_full), semaphores)
        sums[...] = jnp.zeros_like(sums)

    def vector(row):
        return vectors[pl.ds(row, 1), :]

    def add(row, value):
        sums[pl.ds(row, 1), :] += row_sum(value)

    output_weight = output_full[...].reshape(width, width)
    attended_out = dot_plain(context[...], output_weight) + vector(0)
    first_normed, first_scale = norm_parts(tokens[...].astype(F32) + attended_out)
    first_out = first_normed * vector(1) + vector(2)
    low = first_out.astype(BF16)
    first_low[...] = low
    second = first_out + vector(3)
    for chunk in range(chunks):
        columns = pl.ds(chunk * width, width)
        inner = dot_plain(low, inner_full[chunk].reshape(width, width)) + vector(6 + chunk)
        half = 0.5 * (1.0 + lax.erf(inner * 0.7071067811865476))
        slopes[:, columns] = half + inner * jnp.exp(-0.5 * inner * inner) * 0.3989422804014327
        hidden_low = (inner * half).astype(BF16)
        hidden[:, columns] = hidden_low
        second = second + dot_plain(hidden_low, outer_full[chunk])
    normed, scale = norm_parts(second)
    block = step * context.shape[0] // BLOCK
    valid = jnp.where(kinds[block] != 2, 1.0, 0.0).astype(F32)
    layer_out[...] = ((normed * vector(4) + vector(5)) * valid).astype(BF16)
    out_grad = cotangent[...].astype(F32) * valid
    add(4, out_grad * normed)
    add(5, out_grad)
    second_grad = norm_back(out_grad, vector(4), normed, scale)
    branch_low = second_grad.astype(BF16)
    branch[...] = branch_low
    add(3, branch_low.astype(F32))
    first_out_grad = second_grad
    for chunk in range(chunks):
        columns = pl.ds(chunk * width, width)
        hidden_grad = dot_lanes(branch_low, outer_full[chunk])
        inner_low = (hidden_grad * slopes[:, columns]).astype(BF16)
        inner_grad[:, columns] = inner_low
        add(6 + chunk, inner_low.astype(F32))
        first_out_grad = first_out_grad + dot_lanes(
            inner_low, inner_full[chunk].reshape(width, width)
        )
    add(1, first_out_grad * first_normed)
    add(2, first_out_grad)
    grad = norm_back(first_out_grad, vector(1), first_normed, first_scale)
    first_grad[...] = grad
    attended_low = grad.astype(BF16)
    attended[...] = attended_low
    add(0, attended_low.astype(F32))
    context_grad[...] = dot_lanes(attended_low, output_weight).astype(BF16)


def dense(load, copies, kinds, order, context, tokens, cotangent, vectors, sources):
    count, width = tokens.shape
    chunks = vectors.shape[0] - 6
    tile = BLOCK
    narrow = pl.BlockSpec((tile, width), lambda i, *_: (i, 0))
    wide = pl.BlockSpec((tile, chunks * width), lambda i, *_: (i, 0))
    fixed = pl.BlockSpec(vectors.shape, lambda i, *_: (0, 0))
    low = jax.ShapeDtypeStruct((count, width), BF16)
    low_wide = jax.ShapeDtypeStruct((count, chunks * width), BF16)
    return pl.pallas_call(
        functools.partial(dense_kernel, load),
        grid_spec=pltpu.PrefetchScalarGridSpec(
            num_scalar_prefetch=2,
            grid=(count // tile,),
            in_specs=[narrow, narrow, narrow, fixed] + [HBM] * len(sources),
            out_specs=[narrow, wide, narrow, narrow, wide, narrow, narrow, narrow, fixed],
            scratch_shapes=[
                pltpu.VMEM((8, width // 8, width), BF16),
                pltpu.VMEM((chunks, 8, width // 8, width), BF16),
                pltpu.VMEM((chunks, width, width), BF16),
                pltpu.VMEM((tile, chunks * width), F32),
                pltpu.SemaphoreType.DMA((copies,)),
            ],
        ),
        out_shape=(
            low,
            low_wide,
            low,
            low,
            low_wide,
            low,
            jax.ShapeDtypeStruct((count, width), F32),
            low,
            jax.ShapeDtypeStruct(vectors.shape, F32),
        ),
        compiler_params=WIDE,
        cost_estimate=pl.CostEstimate(
            flops=4 * count * width * width * (1 + 2 * chunks),
            bytes_accessed=2 * count * width * (10 + 2 * chunks),
            transcendentals=2 * count * width * chunks,
        ),
        name="dense",
    )(kinds, order, context, tokens, cotangent, vectors, *sources)


def load_slots(order, sources, output_full, inner_full, outer_full):
    pieces, outer = sources[:8], sources[8]
    depth = output_full.shape[1]
    moves = []
    for slot in range(8):
        moves.append((pieces[slot].at[pl.ds(0, depth)], output_full.at[order[slot]]))
        for chunk in range(inner_full.shape[0]):
            source = pieces[slot].at[pl.ds(depth * (1 + chunk), depth)]
            moves.append((source, inner_full.at[chunk, order[slot]]))
    return moves + [(outer, outer_full)]


def load_whole(order, sources, output_full, inner_full, outer_full):
    output, inner, outer = sources
    width = output.shape[2]
    moves = [(output, output_full), (outer, outer_full)]
    for chunk in range(inner_full.shape[0]):
        moves.append((inner.at[:, :, pl.ds(chunk * width, width)], inner_full.at[chunk]))
    return moves


def shards(
    tokens,
    block_kind,
    query_weight,
    key_weight,
    value_weight,
    query_bias,
    value_bias,
    output_weight,
    output_bias,
    first_gain,
    first_shift,
    inner_weight,
    inner_bias,
    outer_weight,
    outer_bias,
    second_gain,
    second_shift,
    cotangent,
):
    width = tokens.shape[1]
    per_device = block_kind.shape[0] // lax.axis_size("heads")
    singles = (output_bias, first_gain, first_shift, outer_bias, second_gain, second_shift)
    vectors = jnp.concatenate([jnp.stack(singles), inner_bias.reshape(-1, width)]).astype(F32)
    eight_by_four = lax.axis_size("rows") == 8 and lax.axis_size("heads") == 4
    moves = SlotMoves() if eight_by_four else PlainMoves()
    packed_bias = jnp.concatenate([query_bias, jnp.zeros_like(query_bias), value_bias])
    smalls = (packed_bias.astype(F32).reshape(1, -1), vectors, block_kind)
    packed_bias, vectors, kinds = moves.gather(
        (query_weight, key_weight, value_weight),
        output_weight,
        inner_weight,
        outer_weight,
        smalls,
    )
    packed, packed_weight = moves.project(tokens, packed_bias)

    units = 2 * per_device
    earlier = attend_forward((0, units // 2), kinds, packed, None)
    packed_late = moves.dense_start(packed, earlier)
    context, totals = attend_forward((units // 2, units), kinds, packed_late, earlier)
    load, copies, order, sources = moves.dense(context)
    own_kinds = lax.dynamic_slice_in_dim(
        kinds, lax.axis_index("heads") * per_device, per_device
    )
    (
        layer_out,
        hidden_low,
        branch_grad,
        first_low,
        inner_grad,
        attended_grad,
        first_grad,
        context_grad,
        sums,
    ) = dense(load, copies, own_kinds, order, context, tokens, cotangent, vectors, sources)

    kernel_done, outer_steps = moves.outer_terms(hidden_low, branch_grad)
    inner_grad = moves.behind(inner_grad, outer_steps, kernel_done)
    inner_terms = moves.inner_terms((first_low, inner_grad), (context, attended_grad))
    context_grad = moves.behind(context_grad, outer_steps, inner_terms[1])
    inner_steps = moves.inner_steps(inner_terms, context_grad)
    cuts = (0, units // 4, units - units // 4, units)
    grads = None
    for begin, end in zip(cuts, cuts[1:]):
        if begin == cuts[1]:
            context_grad = moves.behind(context_grad, outer_steps, grads[0])
            context_grad = moves.behind(context_grad, inner_steps, grads[0], context_grad)
        if begin == cuts[2]:
            moves.finish(outer_steps, grads[0])
            outer_weight_grad = moves.finish(outer_steps, grads[0])
            context_grad = moves.hold(context_grad, outer_weight_grad)
            context_grad = moves.behind(context_grad, inner_steps, grads[0], context_grad)
        grads = attend_backward(
            (begin, end), kinds, packed, context, context_grad, totals, grads
        )
    (packed_grad,) = grads
    packed_grad = moves.behind(packed_grad, inner_steps, packed_grad)
    packed_terms = moves.packed_terms(tokens, packed_grad, sums)

    def tokens_part(gate):
        return tokens_gradient(first_grad, after(packed_grad, *gate), packed_weight)

    tokens_grad, weight_grads, small, query_sums, value_sums, inner_both = moves.last(
        tokens_part, packed_terms, inner_steps
    )
    inner_weight_grad, output_weight_grad = moves.inner_cut(inner_both)
    return (
        layer_out,
        tokens_grad,
        *weight_grads,
        query_sums,
        value_sums,
        output_weight_grad,
        small[0],
        small[1],
        small[2],
        inner_weight_grad,
        small[6 : sums.shape[0]].reshape(-1),
        outer_weight_grad,
        small[3],
        small[4],
        small[5],
    )


def solution(mesh):
    both = P(("rows", "heads"), None)
    placed = (
        (both, P("rows"))
        + (P("rows", "heads"),) * 3
        + (P(), P(), both, P(), P(), P(), both, P(), both, P(), P(), P(), both)
    )
    given = (
        (both, both)
        + (P("rows", "heads"),) * 3
        + (P(), P(), both, P(), P(), P(), both, P(), both, P(), P(), P())
    )
    return jax.shard_map(
        shards, mesh=mesh, in_specs=placed, out_specs=given, check_vma=False
    )
```
